32 devices in a mesh: rep: 2 (over x), shard: 16 (over z, y, core).
Axes of the slice: x: 2, y: 2, z: 4, core: 2. Of those that a mesh axis runs over, the one named last changes fastest.
Arguments:
- tokens: bfloat16 [4096, 1024], P(('rep', 'shard')), may hold values from -6 to 6
- cotangent: bfloat16 [4096, 1024], P(('rep', 'shard')), may hold values from -6 to 6
- segment: int32 [4096], P(('rep', 'shard')), may hold values from -1 to 127, as said below
- params: float32 [12596224], P('shard'), as said below
- first_moment: float32 [12596224], P('shard'), may hold values from -6 to 6
- second_moment: float32 [12596224], P('shard'), may hold values from 0.01 to 1
Outputs:
- output_rows: bfloat16 [4096, 1024], P(('rep', 'shard'))
- input_grad: bfloat16 [4096, 1024], P(('rep', 'shard'))
- param_grad: float32 [12596224], P('shard')
- new_params: float32 [12596224], P('shard')
- new_first: float32 [12596224], P('shard')
- new_second: float32 [12596224], P('shard')
The draws below stay inside these ranges and needn't reach their ends.
Inputs may be any that keep to these rules, and one draw needn't show every extreme that they name: `segment`: within each aligned block of 128 rows (the rows of one device) the occupied slots come first; an occupied slot holds the index within the block of the first slot of its sequence, so the first slot holds 0 and values never fall along the occupied slots; empty slots hold -1. `params`: the flat buffer in the layout of the steps.
All inputs are finite; a program needn't handle non-finite values.
Results may differ from the reference program's by a relative error of at most 0.023.
Values may be sent and summed in bfloat16 or wider, within the bound.
No kernel may reach another device: no remote copies, remote signals or barrier semaphores. Data moves between devices by JAX's collectives and lax.ppermute only.
A program may use at most 192 MiB of HBM per device.

```python
import math
import jax
import jax.numpy as jnp
from jax import lax

D = 1024
HEADS = 16
HD = 64
ROT = 16
FF = 4096
CAP = 128
STEP = 4
TOKENS = 4096
PARAMS = 12596224


def draw_segment(key, part):
    blocks = TOKENS // CAP
    key_count, key_full, key_flag = jax.random.split(key, 3)
    counts = jax.random.randint(key_count, (blocks,), CAP // 4, CAP + 1)
    full_block = jax.random.randint(key_full, (), 0, blocks)
    block_ids = jnp.arange(blocks)
    counts = jnp.where(block_ids == full_block, CAP, counts)
    slot_ids = jnp.arange(CAP)
    flags = jax.random.randint(key_flag, (blocks, CAP), 0, 24) == 0
    flags = flags | (slot_ids[None, :] == 0) | (block_ids[:, None] == full_block) & (slot_ids[None, :] == CAP - 1)
    starts = lax.cummax(jnp.where(flags, slot_ids[None, :], 0), axis=1)
    segments = jnp.where(slot_ids[None, :] < counts[:, None], starts, -1)
    return segments.reshape(-1).astype(jnp.int32)


def draw_params(key, part):
    subkeys = jax.random.split(key, 14)

    def normal_part(index, extent, spread):
        return jax.random.truncated_normal(subkeys[index], -4.0, 4.0, extent, jnp.float32) * spread

    def gain_part(index):
        return jax.random.uniform(subkeys[index], (D,), jnp.float32, 0.6, 1.4)
    w_qkv = normal_part(0, (D, 3 * D), D ** (-0.5))
    pieces = [w_qkv, normal_part(1, (3 * D,), 0.3), normal_part(2, (D, D), (D // 8) ** (-0.5)), normal_part(3, (D,), 0.3), normal_part(4, (D, FF), D ** (-0.5)), normal_part(5, (FF,), 0.3), normal_part(6, (FF, D), FF ** (-0.5)), normal_part(7, (D,), 0.3), gain_part(8), normal_part(9, (D,), 0.3), gain_part(10), normal_part(11, (D,), 0.3)]
    return jnp.concatenate([piece.reshape(-1) for piece in pieces])


def block_levels(rng, shape, cuts, low, top_value):
    factor_of, own = 1.0, jax.random.fold_in(rng, 6)
    for dim, parts in cuts:
        steps = jnp.exp(jax.random.uniform(jax.random.fold_in(own, dim), (parts,), jnp.float32, low / len(cuts), top_value / len(cuts)))
        factor_of = factor_of * jnp.repeat(steps, shape[dim] // parts).reshape([-1 if axis == dim else 1 for axis in range(len(shape))])
    return factor_of


def scatter_about(own_key, shape, scale, reach, cuts=(), held_as=jnp.bfloat16):
    level = block_levels(own_key, shape, cuts, -0.22, 0.18) if cuts else 1.0
    entries = jax.random.normal(own_key, shape, jnp.float32) * scale * level
    return jnp.minimum(jnp.maximum(entries, -reach), reach).astype(held_as)


def setup_inputs(seed: int = 0) -> dict:
    keys = jax.random.split(jax.random.key(seed), 7)
    return {
        "tokens": scatter_about(keys[0], (TOKENS, D), 1.0, 6.0, ((0, 32),)),
        "cotangent": scatter_about(keys[1], (TOKENS, D), 1.0, 6.0, ((0, 32),)),
        "segment": draw_segment(jax.random.fold_in(keys[6], 71), 0),
        "params": draw_params(jax.random.fold_in(keys[6], 71), 0),
        "first_moment": scatter_about(keys[4], (PARAMS,), 1.0, 6.0, ((0, 16),), jnp.float32),
        "second_moment": jnp.clip(jnp.exp(math.log(1.0) - 4.6051702 * jax.random.uniform(keys[5], (PARAMS,), jnp.float32) ** block_levels(keys[5], (PARAMS,), ((0, 16),), -0.2, 0.2)), 0.01, 1.0),
    }


norm_eps = 1e-05
adam_eps = 1e-08
beta_one = 0.9
beta_two = 0.999
learn_rate = 0.003
decay_rate = 0.1
root_half = 0.7071067811865476
inv_root_twopi = 0.3989422804014327

def extent_list():
    return [(D, 3 * D), (3 * D,), (D, D), (D,), (D, FF), (FF,), (FF, D), (D,), (D,), (D,), (D,), (D,)]

def unpack(flat_vec):
    pieces = []
    offset = 0
    for extent in extent_list():
        amount = math.prod(extent)
        pieces.append(flat_vec[offset:offset + amount].reshape(extent))
        offset += amount
    return pieces

def norm_forward(residual, gain, shift):
    center = residual - lax.optimization_barrier(jnp.mean(residual, axis=-1, keepdims=True))
    inverse = lax.rsqrt(lax.optimization_barrier(jnp.mean(center * center, axis=-1, keepdims=True)) + norm_eps)
    normed = center * inverse
    return (normed * gain + shift, normed, inverse)

def norm_backward(grad_norm, normed, inverse, gain):
    grad_hat = grad_norm * gain
    return inverse * (grad_hat - lax.optimization_barrier(jnp.mean(grad_hat, axis=-1, keepdims=True)) - normed * lax.optimization_barrier(jnp.mean(grad_hat * normed, axis=-1, keepdims=True)))

def rotate(values, cosine, sine_part):
    half_rot = ROT // 2
    lower_half = values[..., :half_rot]
    upper_half = values[..., half_rot:ROT]
    return jnp.concatenate([lower_half * cosine - upper_half * sine_part, upper_half * cosine + lower_half * sine_part, values[..., ROT:]], axis=-1)

def rotate_back(grads_in, cosine, sine_part):
    half_rot = ROT // 2
    lower_half = grads_in[..., :half_rot]
    upper_half = grads_in[..., half_rot:ROT]
    return jnp.concatenate([lower_half * cosine + upper_half * sine_part, upper_half * cosine - lower_half * sine_part, grads_in[..., ROT:]], axis=-1)

def gelu_exact(values):
    return 0.5 * values * (1.0 + lax.erf(values * root_half))

def gelu_slope(values):
    return 0.5 * (1.0 + lax.erf(values * root_half)) + values * jnp.exp(-0.5 * values * values) * inv_root_twopi

def angles(segments):
    row_ids = jnp.arange(segments.shape[0], dtype=jnp.int32)
    position = (row_ids - segments).astype(jnp.float32)
    frequency = 10000.0 ** (-jnp.arange(0, ROT, 2, dtype=jnp.float32) / ROT)
    phases = position[:, None] * frequency[None, :]
    return (jnp.cos(phases)[:, None, :], jnp.sin(phases)[:, None, :])

def scores_of(queries, keys_bf, segments):
    raw = jnp.einsum('ihd,jhd->hij', queries.astype(jnp.float32), keys_bf.astype(jnp.float32)) * HD ** (-0.5)
    row_ids = jnp.arange(segments.shape[0], dtype=jnp.int32)
    allowed = (segments[:, None] == segments[None, :]) & (row_ids[None, :] <= row_ids[:, None])
    return jnp.where(allowed[None], raw, -1e+30)

def layer_block(rows_in, rows_cot, segments, pieces):
    w_qkv, b_qkv, w_out, b_out, w_up, b_up, w_down, b_down, gain_one, shift_one, gain_two, shift_two = pieces
    length = rows_in.shape[0]
    residual = rows_in.astype(jnp.float32)
    normed_one, hat_one, inv_one = norm_forward(residual, gain_one.astype(jnp.float32), shift_one.astype(jnp.float32))
    normed_two, hat_two, inv_two = norm_forward(residual, gain_two.astype(jnp.float32), shift_two.astype(jnp.float32))
    input_one = normed_one.astype(jnp.bfloat16)
    input_two = normed_two.astype(jnp.bfloat16)
    mixed_rows = jnp.dot(input_one, w_qkv, preferred_element_type=jnp.float32) + b_qkv.astype(jnp.float32)
    cosine, sine_part = angles(segments)
    queries = rotate(mixed_rows[:, :D].reshape(length, HEADS, HD), cosine, sine_part).astype(jnp.bfloat16)
    keys_bf = rotate(mixed_rows[:, D:2 * D].reshape(length, HEADS, HD), cosine, sine_part).astype(jnp.bfloat16)
    values_bf = mixed_rows[:, 2 * D:].reshape(length, HEADS, HD).astype(jnp.bfloat16)
    scores = scores_of(queries, keys_bf, segments)
    row_max = lax.optimization_barrier(jnp.max(scores, axis=-1, keepdims=True))
    log_total = row_max + jnp.log(lax.optimization_barrier(jnp.sum(jnp.exp(scores - row_max), axis=-1, keepdims=True)))
    probs_bf = jnp.exp(scores - log_total).astype(jnp.bfloat16)
    heads_out = jnp.einsum('hij,jhd->ihd', probs_bf.astype(jnp.float32), values_bf.astype(jnp.float32)).reshape(length, D).astype(jnp.bfloat16)
    attention = jnp.dot(heads_out, w_out, preferred_element_type=jnp.float32) + b_out.astype(jnp.float32)
    hidden_pre = jnp.dot(input_two, w_up, preferred_element_type=jnp.float32) + b_up.astype(jnp.float32)
    active = gelu_exact(hidden_pre).astype(jnp.bfloat16)
    feed_out = jnp.dot(active, w_down, preferred_element_type=jnp.float32) + b_down.astype(jnp.float32)
    out_rows = (residual + attention + feed_out).astype(jnp.bfloat16)
    live_rows = (segments >= 0)[:, None]
    grad_bf = jnp.where(live_rows, rows_cot, jnp.zeros_like(rows_cot))
    grad_full = grad_bf.astype(jnp.float32)
    grad_w_down = jnp.dot(active.T, grad_bf, preferred_element_type=jnp.float32)
    grad_b_down = lax.optimization_barrier(jnp.sum(grad_full, axis=0))
    grad_hidden = jnp.dot(grad_bf, w_down.T, preferred_element_type=jnp.float32) * gelu_slope(hidden_pre)
    grad_hidden_bf = grad_hidden.astype(jnp.bfloat16)
    grad_b_up = lax.optimization_barrier(jnp.sum(grad_hidden, axis=0))
    grad_w_up = jnp.dot(input_two.T, grad_hidden_bf, preferred_element_type=jnp.float32)
    grad_norm_two = jnp.dot(grad_hidden_bf, w_up.T, preferred_element_type=jnp.float32)
    grad_w_out = jnp.dot(heads_out.T, grad_bf, preferred_element_type=jnp.float32)
    grad_b_out = lax.optimization_barrier(jnp.sum(grad_full, axis=0))
    grad_heads = jnp.dot(grad_bf, w_out.T, preferred_element_type=jnp.float32).astype(jnp.bfloat16).reshape(length, HEADS, HD)
    delta_rows = jnp.einsum('ihd,ihd->hi', grad_heads.astype(jnp.float32), heads_out.reshape(length, HEADS, HD).astype(jnp.float32))
    probs_exact = jnp.exp(scores_of(queries, keys_bf, segments) - log_total)
    probs_again = probs_exact.astype(jnp.bfloat16)
    grad_values = jnp.einsum('hij,ihd->jhd', probs_again.astype(jnp.float32), grad_heads.astype(jnp.float32))
    grad_probs = jnp.einsum('ihd,jhd->hij', grad_heads.astype(jnp.float32), values_bf.astype(jnp.float32))
    grad_scores = (probs_exact * (grad_probs - delta_rows[:, :, None]) * HD ** (-0.5)).astype(jnp.bfloat16)
    grad_queries = jnp.einsum('hij,jhd->ihd', grad_scores.astype(jnp.float32), keys_bf.astype(jnp.float32))
    grad_keys = jnp.einsum('hij,ihd->jhd', grad_scores.astype(jnp.float32), queries.astype(jnp.float32))
    grad_mixed = jnp.concatenate([rotate_back(grad_queries, cosine, sine_part).reshape(length, D), rotate_back(grad_keys, cosine, sine_part).reshape(length, D), grad_values.reshape(length, D)], axis=1)
    grad_b_qkv = lax.optimization_barrier(jnp.sum(grad_mixed, axis=0))
    grad_mixed_bf = grad_mixed.astype(jnp.bfloat16)
    grad_w_qkv = jnp.dot(input_one.T, grad_mixed_bf, preferred_element_type=jnp.float32)
    grad_norm_one = jnp.dot(grad_mixed_bf, w_qkv.T, preferred_element_type=jnp.float32)
    grad_rows = (grad_full + norm_backward(grad_norm_one, hat_one, inv_one, gain_one.astype(jnp.float32)) + norm_backward(grad_norm_two, hat_two, inv_two, gain_two.astype(jnp.float32))).astype(jnp.bfloat16)
    grad_list = [grad_w_qkv, grad_b_qkv, grad_w_out, grad_b_out, grad_w_up, grad_b_up, grad_w_down, grad_b_down, lax.optimization_barrier(jnp.sum(grad_norm_one * hat_one, axis=0)), lax.optimization_barrier(jnp.sum(grad_norm_one, axis=0)), lax.optimization_barrier(jnp.sum(grad_norm_two * hat_two, axis=0)), lax.optimization_barrier(jnp.sum(grad_norm_two, axis=0))]
    block_grad = jnp.concatenate([piece.reshape(-1).astype(jnp.bfloat16) for piece in grad_list])
    return (out_rows, grad_rows, block_grad)

def adam_update(weights, moment_one, moment_two, grad_total):
    first_new = beta_one * moment_one + (1.0 - beta_one) * grad_total
    second_new = beta_two * moment_two + (1.0 - beta_two) * grad_total * grad_total
    correct_one = 1.0 - beta_one ** STEP
    correct_two = 1.0 - beta_two ** STEP
    change = first_new / correct_one / (jnp.sqrt(second_new / correct_two) + adam_eps)
    return (weights - learn_rate * (change + decay_rate * weights), first_new, second_new)

def reference(tokens, cotangent, segment, params, first_moment, second_moment):
    pieces = unpack(params.astype(jnp.bfloat16))
    blocks = tokens.shape[0] // CAP

    def scan_step(grad_total, inputs):
        rows_in, rows_cot, segments = inputs
        out_rows, grad_rows, block_grad = layer_block(rows_in, rows_cot, segments, pieces)
        block_grad = lax.optimization_barrier(block_grad)
        return (grad_total + block_grad.astype(jnp.float32), (out_rows, grad_rows))
    grad_total, (outs_rows, outs_grad) = lax.scan(scan_step, jnp.zeros((PARAMS,), jnp.float32), (tokens.reshape(blocks, CAP, D), cotangent.reshape(blocks, CAP, D), segment.reshape(blocks, CAP)))
    new_weights, first_new, second_new = adam_update(params, first_moment, second_moment, grad_total)
    return (outs_rows.reshape(tokens.shape), outs_grad.reshape(tokens.shape), grad_total, new_weights, first_new, second_new)
```

```python
import math

import jax
import jax.numpy as jnp
import numpy as np
from jax import lax
from jax.sharding import PartitionSpec as P

D = 1024
HEADS = 16
HD = 64
ROT = 16
FF = 4096
STEP = 4
UNIT = HEADS

norm_eps = 1e-05
adam_eps = 1e-08
beta_one = 0.9
beta_two = 0.999
learn_rate = 0.003
decay_rate = 0.1
root_half = 0.7071067811865476
inv_root_twopi = 0.3989422804014327


QKV_END = 3 * D
OUT_END = QKV_END + D
UP_END = OUT_END + FF
DOWN_END = UP_END + FF
MAT_ROWS = DOWN_END
SECTIONS = ((0, QKV_END, 0), (QKV_END, OUT_END, 3), (OUT_END, UP_END, 4), (UP_END, DOWN_END, 8))
RUNS = (
    (QKV_END, 3, 0),
    (OUT_END + 3, 1, 3),
    (UP_END + 4, 4, 4),
    (DOWN_END + 8, 5, 8),
)
VEC_ROWS = 13
PAD = 8 * D

f32 = jnp.float32
bf16 = jnp.bfloat16


def owner_tables(owners):
    total = (MAT_ROWS + VEC_ROWS) * D
    part = total // owners
    lead = VEC_ROWS * D // owners
    rows = []
    for s in range(owners):
        start, end = s * part, (s + 1) * part
        first = next((i for i, (a, b, v) in enumerate(SECTIONS) if (b + v) * D > start), 3)
        second = min(first + 1, 3)
        run_row, run_len, vec_row = RUNS[first]
        run_a = min(max(run_row * D - start, 0), part)
        run_b = min(max((run_row + run_len) * D - start, 0), part)
        rows.append(
            (
                lead * s - SECTIONS[first][2] * D,
                lead * s - SECTIONS[second][2] * D,
                (SECTIONS[first][1] - (MAT_ROWS // owners) * s) if first < 3 else 2 * MAT_ROWS,
                run_a,
                run_b,
                run_row * D - start - vec_row * D,
            )
        )
    return np.array(rows, np.int32)


def rotate(values, cosine, sine_part):
    half_rot = ROT // 2
    lower_half = values[..., :half_rot]
    upper_half = values[..., half_rot:ROT]
    return jnp.concatenate(
        [
            lower_half * cosine - upper_half * sine_part,
            upper_half * cosine + lower_half * sine_part,
            values[..., ROT:],
        ],
        axis=-1,
    )


def gelu_parts(values):
    cdf = 0.5 * (1.0 + lax.erf(values * root_half))
    return values * cdf, cdf + values * jnp.exp(-0.5 * values * values) * inv_root_twopi


def adam_update(weights, moment_one, moment_two, grad_total):
    first_new = beta_one * moment_one + (1.0 - beta_one) * grad_total
    second_new = beta_two * moment_two + (1.0 - beta_two) * grad_total * grad_total
    correct_one = 1.0 - beta_one**STEP
    correct_two = 1.0 - beta_two**STEP
    change = first_new / correct_one / (jnp.sqrt(second_new / correct_two) + adam_eps)
    return (weights - learn_rate * (change + decay_rate * weights), first_new, second_new)


def bmm(spec, a, b):
    return jnp.einsum(spec, a, b, preferred_element_type=f32)


class Layout:
    def __init__(self, mesh):
        self.n = mesh.shape["shard"]
        self.reps = mesh.shape["rep"]
        self.ways = HEADS
        assert self.n % self.ways == 0
        self.packs = self.n // self.ways
        self.core, self.row = 2, 2
        self.line = self.ways // 4
        self.units = MAT_ROWS // UNIT // self.n
        slots = self.units + 1 + 1 + 5
        self.slots = -(-slots // self.reps) * self.reps
        self.share = self.slots // self.reps
        self.tables = owner_tables(self.n)

    def xor(self, k):
        return [(i, i ^ k) for i in range(self.n)]

    def step(self, k):
        w = self.ways
        return [(i, i - i % w + (i % w + 4 * k) % w) for i in range(self.n)]

    def rep_xor(self, k):
        return [(i, i ^ k) for i in range(self.reps)]


def gather_rows(lay, block):
    chain = [block]
    for _ in range(lay.line - 1):
        chain.append(lax.ppermute(chain[-1], "shard", lay.step(1)))
    plane = []
    for piece in chain:
        plane += [piece, lax.ppermute(piece, "shard", lay.xor(2))]
    plane = jnp.concatenate(plane, axis=0)
    return jnp.concatenate([plane, lax.ppermute(plane, "shard", lay.xor(1))], axis=0)


def scatter_rows(lay, partial_rows, length):
    half = partial_rows.shape[0] // 2
    plane = partial_rows[:half].astype(f32) + lax.ppermute(
        partial_rows[half:], "shard", lay.xor(1)
    ).astype(f32)
    plane = plane.reshape(lay.line, 2, length, -1)
    mine = []
    for d in range(lay.line):
        mine.append(plane[d, 0] + lax.ppermute(plane[d, 1].astype(bf16), "shard", lay.xor(2)))
    total = mine[-1]
    for d in range(lay.line - 2, -1, -1):
        total = mine[d] + lax.ppermute(total.astype(bf16), "shard", lay.step(-1))
    return total


def exchange(lay, parts, me):
    order = jnp.arange(lay.ways, dtype=jnp.int32) ^ me
    by_offset = jnp.take(parts, order, axis=0)
    got = [by_offset[0]]
    for k in range(1, lay.ways):
        got.append(lax.ppermute(by_offset[k], "shard", lay.xor(k)))
    return jnp.take(jnp.stack(got), order, axis=0)


def spread_matrix():
    row = lax.broadcasted_iota(jnp.int32, (D, D), 0)
    col = lax.broadcasted_iota(jnp.int32, (D, D), 1)
    return (row == (col % HD) * HEADS + col // HD).astype(bf16)


def split_params(lay, params, shard_id, rep_id):
    table = jnp.asarray(lay.tables)[shard_id]
    rows = (lay.units + 1) * UNIT
    chunk = params.astype(bf16)
    padded = jnp.pad(chunk, (PAD, rows * D + 2 * PAD - chunk.shape[0]))
    first = lax.dynamic_slice(padded, (PAD - table[0],), (rows * D,)).reshape(rows, D)
    second = lax.dynamic_slice(padded, (PAD - table[1],), (rows * D,)).reshape(rows, D)
    row_ids = lax.broadcasted_iota(jnp.int32, (rows, 1), 0)
    window = jnp.where(row_ids < table[2], first, second)
    vrow = row_ids + shard_id * (lay.units * UNIT)
    spread = spread_matrix()
    is_up = (vrow >= OUT_END) & (vrow < UP_END)
    moved = jnp.dot(window, spread, preferred_element_type=f32).astype(bf16)
    by_col = jnp.where(is_up, moved, window)
    by_col = by_col.reshape(lay.units + 1, UNIT, HEADS, HD).transpose(2, 0, 1, 3)
    by_col = by_col.reshape(HEADS, lay.units + 1, D)
    by_row = window.reshape(lay.units + 1, UNIT, D).transpose(1, 0, 2)
    unit_ids = lax.broadcasted_iota(jnp.int32, (1, lay.units + 1, 1), 1) + shard_id * lay.units
    whole_rows = ((unit_ids >= QKV_END // UNIT) & (unit_ids < OUT_END // UNIT)) | (
        unit_ids >= UP_END // UNIT
    )
    body = jnp.where(whole_rows, by_row, by_col)
    size = chunk.shape[0]
    vec = []
    for flat_row, amount, _ in RUNS:
        start = flat_row * D - shard_id * size
        begin = jnp.clip(start, -PAD, size)
        piece = lax.dynamic_slice(padded, (PAD + begin,), (amount * D,))
        vec.append(jnp.where(start == begin, piece, 0).reshape(amount, D))
    qkv_cols = vec[0].reshape(3, HEADS, HD).transpose(1, 0, 2).reshape(HEADS, 3 * HD)
    up_cols = vec[2].reshape(FF // HEADS, HEADS).T
    used = qkv_cols.shape[1] + up_cols.shape[1]
    mixed_row = jnp.concatenate([qkv_cols, up_cols, jnp.zeros((HEADS, D - used), bf16)], axis=1)
    mixed_row = mixed_row[:, None]
    full = jnp.concatenate(
        [vec[1] + vec[3][:1], vec[3][1:], jnp.zeros((lay.slots - lay.units - 7, D), bf16)], axis=0
    )
    full = jnp.broadcast_to(full[None], (HEADS,) + full.shape)
    parts = jnp.concatenate([body, mixed_row, full], axis=1)
    me = shard_id % lay.ways
    share = lax.dynamic_slice_in_dim(parts, rep_id * lay.share, lay.share, axis=1)
    got = exchange(lay, share, me)
    got = [got] + [lax.ppermute(got, "rep", lay.rep_xor(k)) for k in range(1, lay.reps)]
    got = jnp.take(jnp.stack(got), jnp.arange(lay.reps, dtype=jnp.int32) ^ rep_id, axis=0)
    got = got.transpose(1, 0, 2, 3).reshape(lay.ways, lay.slots, D)
    if lay.packs > 1:
        packs = [got] + [
            lax.ppermute(got, "shard", lay.xor(lay.ways * k)) for k in range(1, lay.packs)
        ]
        order = jnp.arange(lay.packs, dtype=jnp.int32) ^ (shard_id // lay.ways)
        got = jnp.take(jnp.stack(packs), order, axis=0).reshape(lay.n, lay.slots, D)
    carry = got[:-1, lay.units : lay.units + 1]
    carry = jnp.concatenate([jnp.zeros_like(carry[:1]), carry], axis=0)
    units = jnp.concatenate([got[:, :1] + carry, got[:, 1 : lay.units]], axis=1)
    units = units.reshape(MAT_ROWS // UNIT, D)
    w_qkv = units[: QKV_END // UNIT].reshape(D, 3 * HD)
    w_up = units[OUT_END // UNIT : UP_END // UNIT].reshape(D, FF // HEADS)
    w_down = units[UP_END // UNIT :]
    out_rows = units[QKV_END // UNIT : OUT_END // UNIT]
    w_out = exchange(lay, out_rows.reshape(HEADS, HD // HEADS, D), me)
    w_out = w_out.transpose(1, 0, 2).reshape(HD, D)
    extra = jnp.sum(got[:, lay.units + 1 : lay.units + 7].astype(f32), axis=0)
    b_qkv = extra[0, : 3 * HD]
    b_up = extra[0, 3 * HD : 3 * HD + FF // HEADS]
    return w_qkv, b_qkv, w_out, w_up, b_up, w_down, extra[1:]


def collect_grads(lay, units, mixed_row, full, shard_id, rep_id):
    me = shard_id % lay.ways
    units = units.reshape(lay.n, lay.units, D)
    after = jnp.concatenate([units[1:, :1], jnp.zeros_like(units[:1, :1])], axis=0)
    tail = jnp.concatenate(
        [mixed_row[None], full, jnp.zeros((lay.slots - lay.units - 7, D), bf16)], axis=0
    )
    tail = jnp.broadcast_to(tail[None], (lay.n,) + tail.shape)
    parts = jnp.concatenate([units, after, tail], axis=1)
    by_rep = parts.reshape(lay.n, lay.reps, lay.share, D)
    total = lax.dynamic_index_in_dim(by_rep, rep_id, axis=1, keepdims=False).astype(f32)
    for k in range(1, lay.reps):
        theirs = lax.dynamic_index_in_dim(by_rep, rep_id ^ k, axis=1, keepdims=False)
        total = total + lax.ppermute(theirs, "rep", lay.rep_xor(k)).astype(f32)
    total = total.astype(bf16)
    if lay.packs > 1:
        pack = shard_id // lay.ways
        by_pack = total.reshape(lay.packs, lay.ways, lay.share, D)
        total = lax.dynamic_index_in_dim(by_pack, pack, keepdims=False).astype(f32)
        for k in range(1, lay.packs):
            theirs = lax.dynamic_index_in_dim(by_pack, pack ^ k, keepdims=False)
            total = total + lax.ppermute(theirs, "shard", lay.xor(lay.ways * k)).astype(f32)
        total = total.astype(bf16)
    got = exchange(lay, total, me)
    got = [got] + [lax.ppermute(got, "rep", lay.rep_xor(k)) for k in range(1, lay.reps)]
    got = jnp.take(jnp.stack(got), jnp.arange(lay.reps, dtype=jnp.int32) ^ rep_id, axis=0)
    got = got.transpose(1, 0, 2, 3).reshape(lay.ways, lay.slots, D)
    body = got[:, : lay.units + 1]
    rows = (lay.units + 1) * UNIT
    by_row = body.transpose(1, 0, 2).reshape(rows, D)
    by_col = body.reshape(HEADS, lay.units + 1, UNIT, HD).transpose(1, 2, 0, 3).reshape(rows, D)
    vrow = lax.broadcasted_iota(jnp.int32, (rows, 1), 0) + shard_id * (lay.units * UNIT)
    is_up = (vrow >= OUT_END) & (vrow < UP_END)
    whole_rows = ((vrow >= QKV_END) & (vrow < OUT_END)) | (vrow >= UP_END)
    moved = jnp.dot(by_col, spread_matrix().T, preferred_element_type=f32).astype(bf16)
    window = jnp.where(whole_rows, by_row, jnp.where(is_up, moved, by_col))
    extra = got[:, lay.units + 1 : lay.units + 7].astype(f32)
    qkv_vec = extra[:, 0, : 3 * HD].reshape(HEADS, 3, HD).transpose(1, 0, 2).reshape(3 * D)
    up_vec = extra[:, 0, 3 * HD : 3 * HD + FF // HEADS].T.reshape(FF)
    norm_vec = jnp.sum(extra[:, 1:5], axis=0).reshape(4 * D)
    out_vec = extra[0, 5]
    small = jnp.concatenate([qkv_vec, out_vec, up_vec, out_vec, norm_vec])
    table = jnp.asarray(lay.tables)[shard_id]
    size = (MAT_ROWS + VEC_ROWS) * D // lay.n
    flat = jnp.pad(window.reshape(-1), (PAD, PAD))
    first = lax.dynamic_slice(flat, (PAD + table[0],), (size,))
    second = lax.dynamic_slice(flat, (PAD + table[1],), (size,))
    flat_small = jnp.pad(small, (size, size))
    vec = lax.dynamic_slice(flat_small, (size - table[5],), (size,))
    ids = lax.iota(jnp.int32, size)
    first = first.astype(f32)
    second = second.astype(f32)
    return jnp.where(ids < table[3], first, jnp.where(ids < table[4], vec, second))


def per_device(lay, tokens, cotangent, segment, params, first_moment, second_moment):
    shard_id = lax.axis_index("shard")
    rep_id = lax.axis_index("rep")
    me = shard_id % lay.ways
    length = tokens.shape[0]
    blocks = lay.ways
    total_rows = blocks * length

    w_qkv, b_qkv, w_out, w_up, b_up, w_down, full = split_params(lay, params, shard_id, rep_id)
    b_sum, gain_one, shift_one, gain_two, shift_two = (full[i] for i in range(5))
    rows_in = gather_rows(lay, tokens)
    own_grad = jnp.where((segment >= 0)[:, None], cotangent, jnp.zeros_like(cotangent))
    rows_grad = gather_rows(lay, own_grad)
    seg = gather_rows(lay, segment[None])

    residual = rows_in.astype(f32)
    center = residual - jnp.mean(residual, axis=-1, keepdims=True)
    inverse = lax.rsqrt(jnp.mean(center * center, axis=-1, keepdims=True) + norm_eps)
    hat = center * inverse
    input_one = (hat * gain_one + shift_one).astype(bf16)
    input_two = (hat * gain_two + shift_two).astype(bf16)

    mixed = bmm("ik,kj->ij", input_one, w_qkv) + b_qkv
    row_ids = jnp.arange(length, dtype=jnp.int32)
    position = (row_ids[None] - seg).astype(f32)
    frequency = 10000.0 ** (-jnp.arange(0, ROT, 2, dtype=f32) / ROT)
    phases = position[:, :, None] * frequency
    cosine, sine_part = jnp.cos(phases), jnp.sin(phases)
    mixed = mixed.reshape(blocks, length, 3 * HD)
    queries = rotate(mixed[..., :HD], cosine, sine_part).astype(bf16)
    keys = rotate(mixed[..., HD : 2 * HD], cosine, sine_part).astype(bf16)
    values = mixed[..., 2 * HD :].astype(bf16)
    scale = HD ** (-0.5)
    allowed = (seg[:, :, None] == seg[:, None, :]) & (row_ids[None, :] <= row_ids[:, None])[None]
    scores = jnp.where(allowed, bmm("bid,bjd->bij", queries, keys) * scale, -1e30)
    row_max = jnp.max(scores, axis=-1, keepdims=True)
    expd = jnp.exp(scores - row_max)
    probs = expd / jnp.sum(expd, axis=-1, keepdims=True)
    probs_bf = probs.astype(bf16)
    heads_out = bmm("bij,bjd->bid", probs_bf, values).astype(bf16)
    heads_flat = heads_out.reshape(total_rows, HD)

    hidden = bmm("ik,kj->ij", input_two, w_up) + b_up
    active, slope = gelu_parts(hidden)
    active = active.astype(bf16)
    out_part = bmm("ik,kj->ij", heads_flat, w_out) + bmm("ik,kj->ij", active, w_down)
    out_sum = scatter_rows(lay, out_part.astype(bf16), length)
    out_rows = (tokens.astype(f32) + out_sum + b_sum).astype(bf16)

    grad_hidden = bmm("ik,jk->ij", rows_grad, w_down) * slope
    grad_hidden_bf = grad_hidden.astype(bf16)
    grad_heads = bmm("ik,jk->ij", rows_grad, w_out).astype(bf16).reshape(blocks, length, HD)
    delta = jnp.sum(grad_heads.astype(f32) * heads_out.astype(f32), axis=-1, keepdims=True)
    grad_values = bmm("bij,bid->bjd", probs_bf, grad_heads)
    grad_probs = bmm("bid,bjd->bij", grad_heads, values)
    grad_scores = (probs * (grad_probs - delta) * scale).astype(bf16)
    grad_queries = bmm("bij,bjd->bid", grad_scores, keys)
    grad_keys = bmm("bij,bid->bjd", grad_scores, queries)
    grad_mixed = jnp.concatenate(
        [
            rotate(grad_queries, cosine, -sine_part),
            rotate(grad_keys, cosine, -sine_part),
            grad_values,
        ],
        axis=-1,
    ).reshape(total_rows, 3 * HD)
    grad_mixed_bf = grad_mixed.astype(bf16)
    norm_one = bmm("ij,kj->ik", grad_mixed_bf, w_qkv)
    norm_two = bmm("ij,kj->ik", grad_hidden_bf, w_up)
    g_part = norm_one * gain_one + norm_two * gain_two
    g_sum = scatter_rows(lay, g_part.astype(bf16), length)
    own_hat = hat[:length]
    grad_rows = (
        own_grad.astype(f32)
        + inverse[:length]
        * (
            g_sum
            - jnp.mean(g_sum, axis=-1, keepdims=True)
            - own_hat * jnp.mean(g_sum * own_hat, axis=-1, keepdims=True)
        )
    ).astype(bf16)

    grad_w_down = bmm("ij,ik->jk", active, rows_grad).astype(bf16)
    grad_w_out = bmm("ij,ik->jk", heads_flat, rows_grad).astype(bf16)
    grad_w_up = bmm("ik,ij->kj", input_two, grad_hidden_bf).astype(bf16)
    grad_w_qkv = bmm("ik,ij->kj", input_one, grad_mixed_bf).astype(bf16)
    back = grad_w_out.reshape(HD // HEADS, HEADS, D).transpose(1, 0, 2)
    back = exchange(lay, back, me).reshape(HD, D)
    units = jnp.concatenate(
        [
            grad_w_qkv.reshape(QKV_END // UNIT, D),
            back,
            grad_w_up.reshape(FF // UNIT, D),
            grad_w_down,
        ],
        axis=0,
    )
    used = 3 * HD + FF // HEADS
    mixed_row = jnp.concatenate(
        [jnp.sum(grad_mixed, axis=0), jnp.sum(grad_hidden, axis=0), jnp.zeros((D - used,), f32)]
    ).astype(bf16)
    vectors = jnp.stack(
        [
            jnp.sum(norm_one * hat, axis=0),
            jnp.sum(norm_one, axis=0),
            jnp.sum(norm_two * hat, axis=0),
            jnp.sum(norm_two, axis=0),
            jnp.sum(rows_grad.astype(f32), axis=0),
        ]
    ).astype(bf16)
    grad_total = collect_grads(lay, units, mixed_row, vectors, shard_id, rep_id)
    new_weights, first_new, second_new = adam_update(
        params, first_moment, second_moment, grad_total
    )
    return (out_rows, grad_rows, grad_total, new_weights, first_new, second_new)


def solution(mesh):
    lay = Layout(mesh)
    in_specs = (
        P(("rep", "shard"), None),
        P(("rep", "shard"), None),
        P(("rep", "shard")),
        P("shard"),
        P("shard"),
        P("shard"),
    )
    out_specs = (
        P(("rep", "shard"), None),
        P(("rep", "shard"), None),
        P("shard"),
        P("shard"),
        P("shard"),
        P("shard"),
    )

    def body(*args):
        return per_device(lay, *args)

    return jax.shard_map(body, mesh=mesh, in_specs=in_specs, out_specs=out_specs, check_vma=False)
```

```python
import math

import jax
import jax.numpy as jnp
import numpy as np
from jax import lax
from jax.sharding import PartitionSpec as P

D = 1024
HEADS = 16
HD = 64
ROT = 16
FF = 4096
STEP = 4
UNIT = HEADS

norm_eps = 1e-05
adam_eps = 1e-08
beta_one = 0.9
beta_two = 0.999
learn_rate = 0.003
decay_rate = 0.1
root_half = 0.7071067811865476
inv_root_twopi = 0.3989422804014327


QKV_END = 3 * D
OUT_END = QKV_END + D
UP_END = OUT_END + FF
DOWN_END = UP_END + FF
MAT_ROWS = DOWN_END
SECTIONS = ((0, QKV_END, 0), (QKV_END, OUT_END, 3), (OUT_END, UP_END, 4), (UP_END, DOWN_END, 8))
RUNS = (
    (QKV_END, 3, 0),
    (OUT_END + 3, 1, 3),
    (UP_END + 4, 4, 4),
    (DOWN_END + 8, 5, 8),
)
VEC_ROWS = 13
PAD = 8 * D

f32 = jnp.float32
bf16 = jnp.bfloat16


def owner_tables(owners):
    total = (MAT_ROWS + VEC_ROWS) * D
    part = total // owners
    lead = VEC_ROWS * D // owners
    rows = []
    for s in range(owners):
        start, end = s * part, (s + 1) * part
        first = next((i for i, (a, b, v) in enumerate(SECTIONS) if (b + v) * D > start), 3)
        second = min(first + 1, 3)
        run_row, run_len, vec_row = RUNS[first]
        run_a = min(max(run_row * D - start, 0), part)
        run_b = min(max((run_row + run_len) * D - start, 0), part)
        rows.append(
            (
                lead * s - SECTIONS[first][2] * D,
                lead * s - SECTIONS[second][2] * D,
                (SECTIONS[first][1] - (MAT_ROWS // owners) * s) if first < 3 else 2 * MAT_ROWS,
                run_a,
                run_b,
                run_row * D - start - vec_row * D,
            )
        )
    return np.array(rows, np.int32)


def rotate(values, cosine, sine_part):
    half_rot = ROT // 2
    lower_half = values[..., :half_rot]
    upper_half = values[..., half_rot:ROT]
    return jnp.concatenate(
        [
            lower_half * cosine - upper_half * sine_part,
            upper_half * cosine + lower_half * sine_part,
            values[..., ROT:],
        ],
        axis=-1,
    )


def gelu_parts(values):
    cdf = 0.5 * (1.0 + lax.erf(values * root_half))
    return values * cdf, cdf + values * jnp.exp(-0.5 * values * values) * inv_root_twopi


def adam_update(weights, moment_one, moment_two, grad_total):
    first_new = beta_one * moment_one + (1.0 - beta_one) * grad_total
    second_new = beta_two * moment_two + (1.0 - beta_two) * grad_total * grad_total
    correct_one = 1.0 - beta_one**STEP
    correct_two = 1.0 - beta_two**STEP
    change = first_new / correct_one / (jnp.sqrt(second_new / correct_two) + adam_eps)
    return (weights - learn_rate * (change + decay_rate * weights), first_new, second_new)


def bmm(spec, a, b):
    return jnp.einsum(spec, a, b, preferred_element_type=f32)


class Layout:
    def __init__(self, mesh):
        self.n = mesh.shape["shard"]
        self.reps = mesh.shape["rep"]
        self.ways = HEADS
        assert self.n % self.ways == 0
        self.packs = self.n // self.ways
        self.core, self.row = 2, 2
        self.line = self.ways // 4
        self.units = MAT_ROWS // UNIT // self.n
        slots = self.units + 1 + 1 + 5
        self.slots = -(-slots // self.reps) * self.reps
        self.share = self.slots // self.reps
        self.tables = owner_tables(self.n)

    def xor(self, k):
        return [(i, i ^ k) for i in range(self.n)]

    def step(self, k):
        w = self.ways
        return [(i, i - i % w + (i % w + 4 * k) % w) for i in range(self.n)]

    def rep_xor(self, k):
        return [(i, i ^ k) for i in range(self.reps)]


def gather_rows(lay, block):
    chain = [block]
    for _ in range(lay.line - 1):
        chain.append(lax.ppermute(chain[-1], "shard", lay.step(1)))
    plane = []
    for piece in chain:
        plane += [piece, lax.ppermute(piece, "shard", lay.xor(2))]
    plane = jnp.concatenate(plane, axis=0)
    return jnp.concatenate([plane, lax.ppermute(plane, "shard", lay.xor(1))], axis=0)


def scatter_rows(lay, partial_rows, length):
    half = partial_rows.shape[0] // 2
    plane = partial_rows[:half].astype(f32) + lax.ppermute(
        partial_rows[half:], "shard", lay.xor(1)
    ).astype(f32)
    plane = plane.reshape(lay.line, 2, length, -1)
    mine = []
    for d in range(lay.line):
        mine.append(plane[d, 0] + lax.ppermute(plane[d, 1].astype(bf16), "shard", lay.xor(2)))
    total = mine[-1]
    for d in range(lay.line - 2, -1, -1):
        total = mine[d] + lax.ppermute(total.astype(bf16), "shard", lay.step(-1))
    return total


def exchange(lay, parts):
    groups = [list(range(p * lay.ways, (p + 1) * lay.ways)) for p in range(lay.packs)]
    return lax.all_to_all(
        parts, "shard", 0, 0, axis_index_groups=groups if lay.packs > 1 else None, tiled=True
    )


def spread_matrix():
    row = lax.broadcasted_iota(jnp.int32, (D, D), 0)
    col = lax.broadcasted_iota(jnp.int32, (D, D), 1)
    return (row == (col % HD) * HEADS + col // HD).astype(bf16)


def split_params(lay, params, segment, shard_id, rep_id):
    table = jnp.asarray(lay.tables)[shard_id]
    rows = (lay.units + 1) * UNIT
    chunk = params.astype(bf16)
    padded = jnp.pad(chunk, (PAD, rows * D + 2 * PAD - chunk.shape[0]))
    first = lax.dynamic_slice(padded, (PAD - table[0],), (rows * D,)).reshape(rows, D)
    second = lax.dynamic_slice(padded, (PAD - table[1],), (rows * D,)).reshape(rows, D)
    row_ids = lax.broadcasted_iota(jnp.int32, (rows, 1), 0)
    window = jnp.where(row_ids < table[2], first, second)
    vrow = row_ids + shard_id * (lay.units * UNIT)
    spread = spread_matrix()
    is_up = (vrow >= OUT_END) & (vrow < UP_END)
    moved = jnp.dot(window, spread, preferred_element_type=f32).astype(bf16)
    by_col = jnp.where(is_up, moved, window)
    by_col = by_col.reshape(lay.units + 1, UNIT, HEADS, HD).transpose(2, 0, 1, 3)
    by_col = by_col.reshape(HEADS, lay.units + 1, D)
    by_row = window.reshape(lay.units + 1, UNIT, D).transpose(1, 0, 2)
    unit_ids = lax.broadcasted_iota(jnp.int32, (1, lay.units + 1, 1), 1) + shard_id * lay.units
    whole_rows = ((unit_ids >= QKV_END // UNIT) & (unit_ids < OUT_END // UNIT)) | (
        unit_ids >= UP_END // UNIT
    )
    body = jnp.where(whole_rows, by_row, by_col)
    size = chunk.shape[0]
    vec = []
    for flat_row, amount, _ in RUNS:
        start = flat_row * D - shard_id * size
        begin = jnp.clip(start, -PAD, size)
        piece = lax.dynamic_slice(padded, (PAD + begin,), (amount * D,))
        vec.append(jnp.where(start == begin, piece, 0).reshape(amount, D))
    qkv_cols = vec[0].reshape(3, HEADS, HD).transpose(1, 0, 2).reshape(HEADS, 3 * HD)
    up_cols = vec[2].reshape(FF // HEADS, HEADS).T
    used = qkv_cols.shape[1] + up_cols.shape[1]
    mixed_row = jnp.concatenate([qkv_cols, up_cols, jnp.zeros((HEADS, D - used), bf16)], axis=1)
    mixed_row = mixed_row[:, None]
    full = jnp.concatenate(
        [vec[1] + vec[3][:1], vec[3][1:], jnp.zeros((lay.slots - lay.units - 7, D), bf16)], axis=0
    )
    full = jnp.broadcast_to(full[None], (HEADS,) + full.shape)
    parts = jnp.concatenate([body, mixed_row, full], axis=1)
    share = lax.dynamic_slice_in_dim(parts, rep_id * lay.share, lay.share, axis=1)
    seg_row = jnp.pad(segment.astype(bf16), (0, D - segment.shape[0]))
    seg_row = jnp.broadcast_to(seg_row[None, None], (HEADS, 1, D))
    got = exchange(lay, jnp.concatenate([share, seg_row], axis=1))
    seg_all = got[:, lay.share, : segment.shape[0]].astype(jnp.int32)
    got = got[:, : lay.share]
    got = [got] + [lax.ppermute(got, "rep", lay.rep_xor(k)) for k in range(1, lay.reps)]
    got = jnp.take(jnp.stack(got), jnp.arange(lay.reps, dtype=jnp.int32) ^ rep_id, axis=0)
    got = got.transpose(1, 0, 2, 3).reshape(lay.ways, lay.slots, D)
    if lay.packs > 1:
        packs = [got] + [
            lax.ppermute(got, "shard", lay.xor(lay.ways * k)) for k in range(1, lay.packs)
        ]
        order = jnp.arange(lay.packs, dtype=jnp.int32) ^ (shard_id // lay.ways)
        got = jnp.take(jnp.stack(packs), order, axis=0).reshape(lay.n, lay.slots, D)
    carry = got[:-1, lay.units : lay.units + 1]
    carry = jnp.concatenate([jnp.zeros_like(carry[:1]), carry], axis=0)
    units = jnp.concatenate([got[:, :1] + carry, got[:, 1 : lay.units]], axis=1)
    units = units.reshape(MAT_ROWS // UNIT, D)
    w_qkv = units[: QKV_END // UNIT].reshape(D, 3 * HD)
    w_up = units[OUT_END // UNIT : UP_END // UNIT].reshape(D, FF // HEADS)
    w_down = units[UP_END // UNIT :]
    out_rows = units[QKV_END // UNIT : OUT_END // UNIT]
    w_out = exchange(lay, out_rows.reshape(HEADS, HD // HEADS, D))
    w_out = w_out.transpose(1, 0, 2).reshape(HD, D)
    extra = jnp.sum(got[:, lay.units + 1 : lay.units + 7].astype(f32), axis=0)
    b_qkv = extra[0, : 3 * HD]
    b_up = extra[0, 3 * HD : 3 * HD + FF // HEADS]
    return w_qkv, b_qkv, w_out, w_up, b_up, w_down, extra[1:], seg_all


def collect_grads(lay, units, mixed_row, full, shard_id, rep_id):
    units = units.reshape(lay.n, lay.units, D)
    after = jnp.concatenate([units[1:, :1], jnp.zeros_like(units[:1, :1])], axis=0)
    tail = jnp.concatenate(
        [mixed_row[None], full, jnp.zeros((lay.slots - lay.units - 7, D), bf16)], axis=0
    )
    tail = jnp.broadcast_to(tail[None], (lay.n,) + tail.shape)
    parts = jnp.concatenate([units, after, tail], axis=1)
    by_rep = parts.reshape(lay.n, lay.reps, lay.share, D)
    total = lax.dynamic_index_in_dim(by_rep, rep_id, axis=1, keepdims=False).astype(f32)
    for k in range(1, lay.reps):
        theirs = lax.dynamic_index_in_dim(by_rep, rep_id ^ k, axis=1, keepdims=False)
        total = total + lax.ppermute(theirs, "rep", lay.rep_xor(k)).astype(f32)
    total = total.astype(bf16)
    if lay.packs > 1:
        pack = shard_id // lay.ways
        by_pack = total.reshape(lay.packs, lay.ways, lay.share, D)
        total = lax.dynamic_index_in_dim(by_pack, pack, keepdims=False).astype(f32)
        for k in range(1, lay.packs):
            theirs = lax.dynamic_index_in_dim(by_pack, pack ^ k, keepdims=False)
            total = total + lax.ppermute(theirs, "shard", lay.xor(lay.ways * k)).astype(f32)
        total = total.astype(bf16)
    got = exchange(lay, total)
    got = [got] + [lax.ppermute(got, "rep", lay.rep_xor(k)) for k in range(1, lay.reps)]
    got = jnp.take(jnp.stack(got), jnp.arange(lay.reps, dtype=jnp.int32) ^ rep_id, axis=0)
    got = got.transpose(1, 0, 2, 3).reshape(lay.ways, lay.slots, D)
    body = got[:, : lay.units + 1]
    rows = (lay.units + 1) * UNIT
    by_row = body.transpose(1, 0, 2).reshape(rows, D)
    by_col = body.reshape(HEADS, lay.units + 1, UNIT, HD).transpose(1, 2, 0, 3).reshape(rows, D)
    vrow = lax.broadcasted_iota(jnp.int32, (rows, 1), 0) + shard_id * (lay.units * UNIT)
    is_up = (vrow >= OUT_END) & (vrow < UP_END)
    whole_rows = ((vrow >= QKV_END) & (vrow < OUT_END)) | (vrow >= UP_END)
    moved = jnp.dot(by_col, spread_matrix().T, preferred_element_type=f32).astype(bf16)
    window = jnp.where(whole_rows, by_row, jnp.where(is_up, moved, by_col))
    extra = got[:, lay.units + 1 : lay.units + 7].astype(f32)
    qkv_vec = extra[:, 0, : 3 * HD].reshape(HEADS, 3, HD).transpose(1, 0, 2).reshape(3 * D)
    up_vec = extra[:, 0, 3 * HD : 3 * HD + FF // HEADS].T.reshape(FF)
    norm_vec = jnp.sum(extra[:, 1:5], axis=0).reshape(4 * D)
    out_vec = extra[0, 5]
    small = jnp.concatenate([qkv_vec, out_vec, up_vec, out_vec, norm_vec])
    table = jnp.asarray(lay.tables)[shard_id]
    size = (MAT_ROWS + VEC_ROWS) * D // lay.n
    flat = jnp.pad(window.reshape(-1), (PAD, PAD))
    first = lax.dynamic_slice(flat, (PAD + table[0],), (size,))
    second = lax.dynamic_slice(flat, (PAD + table[1],), (size,))
    flat_small = jnp.pad(small, (size, size))
    vec = lax.dynamic_slice(flat_small, (size - table[5],), (size,))
    ids = lax.iota(jnp.int32, size)
    first = first.astype(f32)
    second = second.astype(f32)
    return jnp.where(ids < table[3], first, jnp.where(ids < table[4], vec, second))


def per_device(lay, tokens, cotangent, segment, params, first_moment, second_moment):
    shard_id = lax.axis_index("shard")
    rep_id = lax.axis_index("rep")
    me = shard_id % lay.ways
    length = tokens.shape[0]
    blocks = lay.ways
    total_rows = blocks * length

    rows_in = gather_rows(lay, tokens)
    w_qkv, b_qkv, w_out, w_up, b_up, w_down, full, seg_all = split_params(
        lay, params, segment, shard_id, rep_id
    )
    b_sum, gain_one, shift_one, gain_two, shift_two = (full[i] for i in range(5))
    own_grad = jnp.where((segment >= 0)[:, None], cotangent, jnp.zeros_like(cotangent))
    rows_grad = gather_rows(lay, own_grad)
    spot = jnp.arange(blocks, dtype=jnp.int32)
    d_core, d_line, d_row = spot // (2 * lay.line), spot // 2 % lay.line, spot % 2
    source = (
        (me // 4 - d_line) % lay.line * 4 + ((me // 2 % 2) ^ d_row) * 2 + ((me % 2) ^ d_core)
    )
    seg = jnp.take(seg_all, source, axis=0)

    residual = rows_in.astype(f32)
    center = residual - jnp.mean(residual, axis=-1, keepdims=True)
    inverse = lax.rsqrt(jnp.mean(center * center, axis=-1, keepdims=True) + norm_eps)
    hat = center * inverse
    input_one = (hat * gain_one + shift_one).astype(bf16)
    input_two = (hat * gain_two + shift_two).astype(bf16)

    mixed = bmm("ik,kj->ij", input_one, w_qkv) + b_qkv
    row_ids = jnp.arange(length, dtype=jnp.int32)
    position = (row_ids[None] - seg).astype(f32)
    frequency = 10000.0 ** (-jnp.arange(0, ROT, 2, dtype=f32) / ROT)
    phases = position[:, :, None] * frequency
    cosine, sine_part = jnp.cos(phases), jnp.sin(phases)
    mixed = mixed.reshape(blocks, length, 3 * HD)
    queries = rotate(mixed[..., :HD], cosine, sine_part).astype(bf16)
    keys = rotate(mixed[..., HD : 2 * HD], cosine, sine_part).astype(bf16)
    values = mixed[..., 2 * HD :].astype(bf16)
    scale = HD ** (-0.5)
    allowed = (seg[:, :, None] == seg[:, None, :]) & (row_ids[None, :] <= row_ids[:, None])[None]
    scores = jnp.where(allowed, bmm("bid,bjd->bij", queries, keys) * scale, -1e30)
    row_max = jnp.max(scores, axis=-1, keepdims=True)
    expd = jnp.exp(scores - row_max)
    probs = expd / jnp.sum(expd, axis=-1, keepdims=True)
    probs_bf = probs.astype(bf16)
    heads_out = bmm("bij,bjd->bid", probs_bf, values).astype(bf16)
    heads_flat = heads_out.reshape(total_rows, HD)

    hidden = bmm("ik,kj->ij", input_two, w_up) + b_up
    active, slope = gelu_parts(hidden)
    active = active.astype(bf16)
    out_part = bmm("ik,kj->ij", heads_flat, w_out) + bmm("ik,kj->ij", active, w_down)
    out_sum = scatter_rows(lay, out_part.astype(bf16), length)

    grad_hidden = bmm("ik,jk->ij", rows_grad, w_down) * slope
    grad_hidden_bf = grad_hidden.astype(bf16)
    grad_heads = bmm("ik,jk->ij", rows_grad, w_out).astype(bf16).reshape(blocks, length, HD)
    delta = jnp.sum(grad_heads.astype(f32) * heads_out.astype(f32), axis=-1, keepdims=True)
    grad_values = bmm("bij,bid->bjd", probs_bf, grad_heads)
    grad_probs = bmm("bid,bjd->bij", grad_heads, values)
    grad_scores = (probs * (grad_probs - delta) * scale).astype(bf16)
    grad_queries = bmm("bij,bjd->bid", grad_scores, keys)
    grad_keys = bmm("bij,bid->bjd", grad_scores, queries)
    grad_mixed = jnp.concatenate(
        [
            rotate(grad_queries, cosine, -sine_part),
            rotate(grad_keys, cosine, -sine_part),
            grad_values,
        ],
        axis=-1,
    ).reshape(total_rows, 3 * HD)
    grad_mixed_bf = grad_mixed.astype(bf16)
    norm_one = bmm("ij,kj->ik", grad_mixed_bf, w_qkv)
    norm_two = bmm("ij,kj->ik", grad_hidden_bf, w_up)
    g_part = norm_one * gain_one + norm_two * gain_two
    g_sum = scatter_rows(lay, g_part.astype(bf16), length)
    own_hat = hat[:length]
    grad_rows = (
        own_grad.astype(f32)
        + inverse[:length]
        * (
            g_sum
            - jnp.mean(g_sum, axis=-1, keepdims=True)
            - own_hat * jnp.mean(g_sum * own_hat, axis=-1, keepdims=True)
        )
    ).astype(bf16)

    grad_w_down = bmm("ij,ik->jk", active, rows_grad).astype(bf16)
    grad_w_out = bmm("ij,ik->jk", heads_flat, rows_grad).astype(bf16)
    grad_w_up = bmm("ik,ij->kj", input_two, grad_hidden_bf).astype(bf16)
    grad_w_qkv = bmm("ik,ij->kj", input_one, grad_mixed_bf).astype(bf16)
    back = grad_w_out.reshape(HD // HEADS, HEADS, D).transpose(1, 0, 2)
    back = exchange(lay, back).reshape(HD, D)
    units = jnp.concatenate(
        [
            grad_w_qkv.reshape(QKV_END // UNIT, D),
            back,
            grad_w_up.reshape(FF // UNIT, D),
            grad_w_down,
        ],
        axis=0,
    )
    used = 3 * HD + FF // HEADS
    mixed_row = jnp.concatenate(
        [jnp.sum(grad_mixed, axis=0), jnp.sum(grad_hidden, axis=0), jnp.zeros((D - used,), f32)]
    ).astype(bf16)
    vectors = jnp.stack(
        [
            jnp.sum(norm_one * hat, axis=0),
            jnp.sum(norm_one, axis=0),
            jnp.sum(norm_two * hat, axis=0),
            jnp.sum(norm_two, axis=0),
            jnp.sum(rows_grad.astype(f32), axis=0),
        ]
    ).astype(bf16)
    units, out_sum = lax.optimization_barrier((units, out_sum))
    out_rows = (tokens.astype(f32) + out_sum + b_sum).astype(bf16)
    grad_total = collect_grads(lay, units, mixed_row, vectors, shard_id, rep_id)
    new_weights, first_new, second_new = adam_update(
        params, first_moment, second_moment, grad_total
    )
    return (out_rows, grad_rows, grad_total, new_weights, first_new, second_new)


def solution(mesh):
    lay = Layout(mesh)
    in_specs = (
        P(("rep", "shard"), None),
        P(("rep", "shard"), None),
        P(("rep", "shard")),
        P("shard"),
        P("shard"),
        P("shard"),
    )
    out_specs = (
        P(("rep", "shard"), None),
        P(("rep", "shard"), None),
        P("shard"),
        P("shard"),
        P("shard"),
        P("shard"),
    )

    def body(*args):
        return per_device(lay, *args)

    return jax.shard_map(body, mesh=mesh, in_specs=in_specs, out_specs=out_specs, check_vma=False)
```

```python
import math

import jax
import jax.numpy as jnp
import numpy as np
from jax import lax
from jax.experimental import pallas as pl
from jax.experimental.pallas import tpu as pltpu
from jax.sharding import PartitionSpec as P

D = 1024
HEADS = 16
HD = 64
ROT = 16
FF = 4096
STEP = 4
UNIT = HEADS

norm_eps = 1e-05
adam_eps = 1e-08
beta_one = 0.9
beta_two = 0.999
learn_rate = 0.003
decay_rate = 0.1
root_half = 0.7071067811865476
inv_root_twopi = 0.3989422804014327


QKV_END = 3 * D
OUT_END = QKV_END + D
UP_END = OUT_END + FF
DOWN_END = UP_END + FF
MAT_ROWS = DOWN_END
SECTIONS = ((0, QKV_END, 0), (QKV_END, OUT_END, 3), (OUT_END, UP_END, 4), (UP_END, DOWN_END, 8))
RUNS = (
    (QKV_END, 3, 0),
    (OUT_END + 3, 1, 3),
    (UP_END + 4, 4, 4),
    (DOWN_END + 8, 5, 8),
)
VEC_ROWS = 13
PAD = 8 * D

f32 = jnp.float32
bf16 = jnp.bfloat16


def owner_tables(owners):
    total = (MAT_ROWS + VEC_ROWS) * D
    part = total // owners
    lead = VEC_ROWS * D // owners
    rows = []
    for s in range(owners):
        start, end = s * part, (s + 1) * part
        first = next((i for i, (a, b, v) in enumerate(SECTIONS) if (b + v) * D > start), 3)
        second = min(first + 1, 3)
        run_row, run_len, vec_row = RUNS[first]
        run_a = min(max(run_row * D - start, 0), part)
        run_b = min(max((run_row + run_len) * D - start, 0), part)
        rows.append(
            (
                lead * s - SECTIONS[first][2] * D,
                lead * s - SECTIONS[second][2] * D,
                (SECTIONS[first][1] - (MAT_ROWS // owners) * s) if first < 3 else 2 * MAT_ROWS,
                run_a,
                run_b,
                run_row * D - start - vec_row * D,
            )
        )
    return np.array(rows, np.int32)


def rotate(values, cosine, sine_part):
    half_rot = ROT // 2
    lower_half = values[..., :half_rot]
    upper_half = values[..., half_rot:ROT]
    return jnp.concatenate(
        [
            lower_half * cosine - upper_half * sine_part,
            upper_half * cosine + lower_half * sine_part,
            values[..., ROT:],
        ],
        axis=-1,
    )


def gelu_parts(values):
    cdf = 0.5 * (1.0 + lax.erf(values * root_half))
    return values * cdf, cdf + values * jnp.exp(-0.5 * values * values) * inv_root_twopi


def adam_update(weights, moment_one, moment_two, grad_total):
    first_new = beta_one * moment_one + (1.0 - beta_one) * grad_total
    second_new = beta_two * moment_two + (1.0 - beta_two) * grad_total * grad_total
    correct_one = 1.0 - beta_one**STEP
    correct_two = 1.0 - beta_two**STEP
    change = first_new / correct_one / (jnp.sqrt(second_new / correct_two) + adam_eps)
    return (weights - learn_rate * (change + decay_rate * weights), first_new, second_new)


def bmm(spec, a, b):
    return jnp.einsum(spec, a, b, preferred_element_type=f32)


class Layout:
    def __init__(self, mesh):
        self.n = mesh.shape["shard"]
        self.reps = mesh.shape["rep"]
        self.ways = HEADS
        assert self.n % self.ways == 0
        self.packs = self.n // self.ways
        self.core, self.row = 2, 2
        self.line = self.ways // 4
        self.units = MAT_ROWS // UNIT // self.n
        slots = self.units + 1 + 1 + 5
        self.slots = -(-slots // self.reps) * self.reps
        self.share = self.slots // self.reps
        self.tables = owner_tables(self.n)

    def xor(self, k):
        return [(i, i ^ k) for i in range(self.n)]

    def step(self, k):
        w = self.ways
        return [(i, i - i % w + (i % w + 4 * k) % w) for i in range(self.n)]

    def rep_xor(self, k):
        return [(i, i ^ k) for i in range(self.reps)]


def gather_rows(lay, block):
    chain = [block]
    for _ in range(lay.line - 1):
        chain.append(lax.ppermute(chain[-1], "shard", lay.step(1)))
    plane = []
    for piece in chain:
        plane += [piece, lax.ppermute(piece, "shard", lay.xor(2))]
    plane = jnp.concatenate(plane, axis=0)
    return jnp.concatenate([plane, lax.ppermute(plane, "shard", lay.xor(1))], axis=0)


def scatter_rows(lay, partial_rows, length):
    half = partial_rows.shape[0] // 2
    plane = partial_rows[:half].astype(f32) + lax.ppermute(
        partial_rows[half:], "shard", lay.xor(1)
    ).astype(f32)
    plane = plane.reshape(lay.line, 2, length, -1)
    mine = []
    for d in range(lay.line):
        mine.append(plane[d, 0] + lax.ppermute(plane[d, 1].astype(bf16), "shard", lay.xor(2)))
    total = mine[-1]
    for d in range(lay.line - 2, -1, -1):
        total = mine[d] + lax.ppermute(total.astype(bf16), "shard", lay.step(-1))
    return total


def exchange(lay, parts):
    groups = [list(range(p * lay.ways, (p + 1) * lay.ways)) for p in range(lay.packs)]
    return lax.all_to_all(
        parts, "shard", 0, 0, axis_index_groups=groups if lay.packs > 1 else None, tiled=True
    )


LANES = 128
SUB = D // LANES
TILE = 256
VMEM_LIMIT = 56 * 1024 * 1024


def spread_matrix():
    row = lax.broadcasted_iota(jnp.int32, (D, D), 0)
    col = lax.broadcasted_iota(jnp.int32, (D, D), 1)
    return jnp.where(row == (col % HD) * HEADS + col // HD, 1.0, 0.0).astype(bf16)


def unit_masks(first_unit, amount):
    unit = lax.broadcasted_iota(jnp.int32, (amount, LANES), 0) // SUB + first_unit
    is_up = (unit >= OUT_END // UNIT) & (unit < UP_END // UNIT)
    by_row = ((unit >= QKV_END // UNIT) & (unit < OUT_END // UNIT)) | (unit >= UP_END // UNIT)
    return is_up, by_row


def pack_kernel(info_ref, first_ref, second_ref, out_ref, x_ref):
    rows = first_ref.shape[0]
    amount = rows // UNIT
    ids = lax.broadcasted_iota(jnp.int32, (rows, LANES), 0)
    x_ref[...] = jnp.where(
        ids < info_ref[0], first_ref[...].astype(f32), second_ref[...].astype(f32)
    )
    is_up, by_row = unit_masks(info_ref[1], amount)
    low = lax.broadcasted_iota(jnp.int32, (amount, LANES), 1) < HD
    spread = spread_matrix()
    halves = []
    for p in range(2):
        cols = [x_ref[pl.ds(SUB * p + a, amount, stride=UNIT), :] for a in range(SUB)]
        moved = jnp.dot(
            jnp.concatenate(cols, axis=1).astype(bf16), spread, preferred_element_type=f32
        )
        halves.append(
            [
                jnp.where(is_up, moved[:, a * LANES : (a + 1) * LANES], cols[a])
                for a in range(SUB)
            ]
        )
    whole = x_ref[...].reshape(amount // SUB, UNIT, SUB, LANES)
    for t in range(HEADS):
        zero, one = halves[0][t // 2], halves[1][t // 2]
        if t % 2 == 0:
            piece = jnp.where(low, zero, pltpu.roll(one, HD, 1))
        else:
            piece = jnp.where(low, pltpu.roll(zero, HD, 1), one)
        direct = whole[:, t].reshape(amount, LANES)
        out_ref[t] = jnp.where(by_row, direct, piece).astype(bf16)


def pack(first, second, bound, first_unit):
    rows = first.shape[0]
    return pl.pallas_call(
        pack_kernel,
        out_shape=jax.ShapeDtypeStruct((HEADS, rows // UNIT, LANES), bf16),
        in_specs=[
            pl.BlockSpec(memory_space=pltpu.SMEM),
            pl.BlockSpec(memory_space=pltpu.VMEM),
            pl.BlockSpec(memory_space=pltpu.VMEM),
        ],
        out_specs=pl.BlockSpec(memory_space=pltpu.VMEM),
        scratch_shapes=[pltpu.VMEM((rows, LANES), f32)],
        compiler_params=pltpu.CompilerParams(vmem_limit_bytes=VMEM_LIMIT),
        name="pack",
    )(jnp.stack([bound, first_unit]).astype(jnp.int32), first, second)


MARGIN = 64


def unpack_kernel(info_ref, got_ref, out_ref, x_ref):
    amount = got_ref.shape[1]
    rows = amount * UNIT
    is_up, by_row = unit_masks(info_ref[0], amount)
    low = lax.broadcasted_iota(jnp.int32, (amount, LANES), 1) < HD
    spread = spread_matrix()
    x_ref[pl.ds(0, MARGIN), :] = jnp.zeros((MARGIN, LANES), f32)
    x_ref[pl.ds(MARGIN + rows, MARGIN), :] = jnp.zeros((MARGIN, LANES), f32)
    for p in range(2):
        cols = []
        for a in range(SUB):
            even, odd = got_ref[2 * a].astype(f32), got_ref[2 * a + 1].astype(f32)
            if p == 0:
                cols.append(jnp.where(low, even, pltpu.roll(odd, HD, 1)))
            else:
                cols.append(jnp.where(low, pltpu.roll(even, HD, 1), odd))
        moved = lax.dot_general(
            jnp.concatenate(cols, axis=1).astype(bf16),
            spread,
            (((1,), (1,)), ((), ())),
            preferred_element_type=f32,
        )
        for a in range(SUB):
            x_ref[pl.ds(MARGIN + SUB * p + a, amount, stride=UNIT), :] = jnp.where(
                is_up, moved[:, a * LANES : (a + 1) * LANES], cols[a]
            )
    whole = x_ref[pl.ds(MARGIN, rows), :].reshape(amount // SUB, UNIT, SUB, LANES)
    keep = by_row.reshape(amount // SUB, SUB, LANES)
    mixed = [
        jnp.where(keep, got_ref[t].astype(f32).reshape(amount // SUB, SUB, LANES), whole[:, t])
        for t in range(HEADS)
    ]
    x_ref[pl.ds(MARGIN, rows), :] = jnp.stack(mixed, axis=1).reshape(rows, LANES)
    size = out_ref.shape[0]
    low = lax.broadcasted_iota(jnp.int32, (size, LANES), 1) < HD

    def cut(start):
        base = start // 2
        here = x_ref[pl.ds(base, size), :]
        after = x_ref[pl.ds(base + 1, size), :]
        split = jnp.where(low, pltpu.roll(here, HD, 1), pltpu.roll(after, HD, 1))
        return jnp.where(start % 2 == 1, split, here)

    place = 2 * lax.broadcasted_iota(jnp.int32, (size, LANES), 0) + jnp.where(low, 0, 1)
    first = cut(info_ref[1])
    out_ref[...] = first
    out_ref[...] = jnp.where(place < info_ref[3], out_ref[...], cut(info_ref[2]))


def unpack(got, first_unit, start_one, start_two, bound, size):
    amount = got.shape[1]
    out_rows = -(-size // (SUB * LANES)) * SUB
    info = jnp.stack([first_unit, start_one // HD, start_two // HD, bound // HD])
    return pl.pallas_call(
        unpack_kernel,
        out_shape=jax.ShapeDtypeStruct((out_rows, LANES), f32),
        in_specs=[
            pl.BlockSpec(memory_space=pltpu.SMEM),
            pl.BlockSpec(memory_space=pltpu.VMEM),
        ],
        out_specs=pl.BlockSpec(memory_space=pltpu.VMEM),
        scratch_shapes=[pltpu.VMEM((amount * UNIT + 2 * MARGIN, LANES), f32)],
        compiler_params=pltpu.CompilerParams(vmem_limit_bytes=VMEM_LIMIT),
        name="unpack",
    )(info.astype(jnp.int32), got)


def nt(a, b):
    return lax.dot_general(a, b, (((1,), (1,)), ((), ())), preferred_element_type=f32)


def tn(a, b):
    return lax.dot_general(a, b, (((0,), (0,)), ((), ())), preferred_element_type=f32)


def nn(a, b):
    return lax.dot_general(a, b, (((1,), (0,)), ((), ())), preferred_element_type=f32)


def layer_kernel(
    x_ref,
    go_ref,
    cos_ref,
    sin_ref,
    mask_ref,
    w_qkv_ref,
    w_up_ref,
    w_down_ref,
    w_out_ref,
    bias_ref,
    vec_ref,
    out_ref,
    g_ref,
    gqkv_ref,
    gup_ref,
    gdown_ref,
    gout_ref,
    gbias_ref,
    gvec_ref,
    aqkv,
    aup,
    adown,
    aout,
):
    step = pl.program_id(0)

    @pl.when(step == 0)
    def _():
        for ref in (aqkv, aup, adown, aout, gbias_ref, gvec_ref):
            ref[...] = jnp.zeros(ref.shape, ref.dtype)

    length = mask_ref.shape[1]
    lane = lax.broadcasted_iota(jnp.int32, (TILE, 2 * LANES), 1) % HD
    low_rot = lane < ROT // 2
    low = lax.broadcasted_iota(jnp.int32, (length, LANES), 1) < HD
    gain_one, shift_one = vec_ref[1:2, :], vec_ref[2:3, :]
    gain_two, shift_two = vec_ref[3:4, :], vec_ref[4:5, :]

    def swap(v):
        ahead = pltpu.roll(v, 2 * LANES - ROT // 2, 1)
        return jnp.where(low_rot, ahead, pltpu.roll(v, ROT // 2, 1))

    x = x_ref[...].astype(f32)
    center = x - jnp.mean(x, axis=1, keepdims=True)
    inverse = lax.rsqrt(jnp.mean(center * center, axis=1, keepdims=True) + norm_eps)
    hat = center * inverse
    in_one = (hat * gain_one + shift_one).astype(bf16)
    in_two = (hat * gain_two + shift_two).astype(bf16)
    go = go_ref[...]

    hidden = nn(in_two, w_up_ref[...]) + bias_ref[1:2, :]
    cdf = 0.5 * (1.0 + lax.erf(hidden * root_half))
    active = (hidden * cdf).astype(bf16)
    slope = cdf + hidden * jnp.exp(-0.5 * hidden * hidden) * inv_root_twopi
    ghid = nt(go, w_down_ref[...]) * slope
    ghid_bf = ghid.astype(bf16)

    mixed = nn(in_one, w_qkv_ref[...]) + bias_ref[0:1, :]
    cosine, sine = cos_ref[...], sin_ref[...]
    rot = mixed * cosine + swap(mixed) * sine
    gheads = nt(go, w_out_ref[...]).astype(bf16)
    scale = HD ** (-0.5)
    heads, gmix = [], []
    for b in range(TILE // length):
        part = slice(b * length, (b + 1) * length)
        qk = rot[part, :LANES]
        vv = rot[part, LANES:].astype(bf16)
        turned = pltpu.roll(qk, HD, 1)
        q_low = jnp.where(low, qk, 0.0).astype(bf16)
        k_low = jnp.where(low, turned, 0.0).astype(bf16)
        q_high = jnp.where(low, 0.0, turned).astype(bf16)
        gh = gheads[part]
        scores = nt(q_low, k_low) * scale + mask_ref[part, :]
        expd = jnp.exp(scores - jnp.max(scores, axis=1, keepdims=True))
        probs = expd / jnp.sum(expd, axis=1, keepdims=True)
        probs_bf = probs.astype(bf16)
        head = nn(probs_bf, vv).astype(bf16)
        heads.append(head)
        delta = jnp.sum(gh.astype(f32) * head.astype(f32), axis=1, keepdims=True)
        gs = (probs * (nt(gh, vv) - delta) * scale).astype(bf16)
        gqk = nn(gs, k_low) + tn(gs, q_high)
        gv = tn(probs_bf, gh)
        gmix.append(jnp.concatenate([gqk, gv], axis=1))
    head = jnp.concatenate(heads, axis=0)
    gmix = jnp.concatenate(gmix, axis=0)
    gmix = gmix * cosine - swap(gmix) * sine
    gmix_bf = gmix.astype(bf16)

    out_ref[...] = (nn(head, w_out_ref[...]) + nn(active, w_down_ref[...])).astype(bf16)
    norm_one = nt(gmix_bf, w_qkv_ref[...])
    norm_two = nt(ghid_bf, w_up_ref[...])
    g_ref[...] = (norm_one * gain_one + norm_two * gain_two).astype(bf16)
    gvec_ref[0:1, :] += jnp.sum(norm_one * hat, axis=0, keepdims=True)
    gvec_ref[1:2, :] += jnp.sum(norm_one, axis=0, keepdims=True)
    gvec_ref[2:3, :] += jnp.sum(norm_two * hat, axis=0, keepdims=True)
    gvec_ref[3:4, :] += jnp.sum(norm_two, axis=0, keepdims=True)
    gvec_ref[4:5, :] += jnp.sum(go.astype(f32), axis=0, keepdims=True)
    gbias_ref[0:1, :] += jnp.sum(gmix, axis=0, keepdims=True)
    gbias_ref[1:2, :] += jnp.sum(ghid, axis=0, keepdims=True)
    aqkv[...] += tn(in_one, gmix_bf)
    aup[...] += tn(in_two, ghid_bf)
    adown[...] += tn(active, go)
    aout[...] += tn(head, go)

    @pl.when(step == pl.num_programs(0) - 1)
    def _():
        gqkv_ref[...] = aqkv[...].astype(bf16)
        gup_ref[...] = aup[...].astype(bf16)
        gdown_ref[...] = adown[...].astype(bf16)
        gout_ref[...] = aout[...].astype(bf16)


def layer(x, go, cosine, sine, mask, w_qkv, w_up, w_down, w_out, bias, vec):
    rows = x.shape[0]
    wide = 2 * LANES
    cols = FF // HEADS

    def tile(width):
        return pl.BlockSpec((TILE, width), lambda i: (i, 0))

    def whole(a, b):
        return pl.BlockSpec((a, b), lambda i: (0, 0))

    return pl.pallas_call(
        layer_kernel,
        grid=(rows // TILE,),
        in_specs=[
            tile(D),
            tile(D),
            tile(wide),
            tile(wide),
            tile(mask.shape[1]),
            whole(D, wide),
            whole(D, cols),
            whole(cols, D),
            whole(LANES, D),
            whole(8, wide),
            whole(8, D),
        ],
        out_specs=[
            tile(D),
            tile(D),
            whole(D, wide),
            whole(D, cols),
            whole(cols, D),
            whole(LANES, D),
            whole(8, wide),
            whole(8, D),
        ],
        out_shape=[
            jax.ShapeDtypeStruct((rows, D), bf16),
            jax.ShapeDtypeStruct((rows, D), bf16),
            jax.ShapeDtypeStruct((D, wide), bf16),
            jax.ShapeDtypeStruct((D, cols), bf16),
            jax.ShapeDtypeStruct((cols, D), bf16),
            jax.ShapeDtypeStruct((LANES, D), bf16),
            jax.ShapeDtypeStruct((8, wide), f32),
            jax.ShapeDtypeStruct((8, D), f32),
        ],
        scratch_shapes=[
            pltpu.VMEM((D, wide), f32),
            pltpu.VMEM((D, cols), f32),
            pltpu.VMEM((cols, D), f32),
            pltpu.VMEM((LANES, D), f32),
        ],
        compiler_params=pltpu.CompilerParams(vmem_limit_bytes=VMEM_LIMIT),
        name="layer",
    )(x, go, cosine, sine, mask, w_qkv, w_up, w_down, w_out, bias, vec)


def split_params(lay, params, segment, shard_id, rep_id):
    table = jnp.asarray(lay.tables)[shard_id]
    rows = (lay.units + 1) * UNIT
    chunk = params.astype(bf16)
    padded = jnp.pad(chunk, (PAD, rows * D + 2 * PAD - chunk.shape[0]))
    first = lax.dynamic_slice(padded, (PAD - table[0],), (rows * D,)).reshape(rows * SUB, LANES)
    second = lax.dynamic_slice(padded, (PAD - table[1],), (rows * D,)).reshape(rows * SUB, LANES)
    body = pack(first, second, table[2] * SUB, shard_id * lay.units)
    size = chunk.shape[0]
    vec = []
    for flat_row, amount, _ in RUNS:
        start = flat_row * D - shard_id * size
        begin = jnp.clip(start, -PAD, size)
        piece = lax.dynamic_slice(padded, (PAD + begin,), (amount * D,))
        vec.append(jnp.where(start == begin, piece, 0).reshape(amount, D))
    qkv_cols = vec[0].reshape(3, HEADS, HD).transpose(1, 0, 2).reshape(HEADS, 3 * HD)
    up_cols = vec[2].reshape(FF // HEADS, HEADS).T
    used = qkv_cols.shape[1] + up_cols.shape[1]
    mixed_row = jnp.concatenate([qkv_cols, up_cols, jnp.zeros((HEADS, D - used), bf16)], axis=1)
    mixed_row = mixed_row[:, None]
    full = jnp.concatenate(
        [vec[1] + vec[3][:1], vec[3][1:], jnp.zeros((lay.slots - lay.units - 7, D), bf16)], axis=0
    )
    full = jnp.broadcast_to(full[None], (HEADS,) + full.shape)
    tail = jnp.concatenate([mixed_row, full], axis=1).reshape(HEADS, -1, LANES)
    parts = jnp.concatenate([body, tail], axis=1)
    wide = lay.share * SUB
    share = lax.dynamic_slice_in_dim(parts, rep_id * wide, wide, axis=1)
    seg_row = jnp.pad(segment.astype(bf16), (0, D - segment.shape[0]))
    seg_row = jnp.broadcast_to(seg_row.reshape(1, SUB, LANES), (HEADS, SUB, LANES))
    got = exchange(lay, jnp.concatenate([share, seg_row], axis=1))
    seg_all = got[:, wide].astype(jnp.int32)
    got = got[:, :wide]
    got = [got] + [lax.ppermute(got, "rep", lay.rep_xor(k)) for k in range(1, lay.reps)]
    got = jnp.take(jnp.stack(got), jnp.arange(lay.reps, dtype=jnp.int32) ^ rep_id, axis=0)
    got = got.transpose(1, 0, 2, 3).reshape(lay.ways, lay.slots, SUB, LANES)
    if lay.packs > 1:
        packs = [got] + [
            lax.ppermute(got, "shard", lay.xor(lay.ways * k)) for k in range(1, lay.packs)
        ]
        order = jnp.arange(lay.packs, dtype=jnp.int32) ^ (shard_id // lay.ways)
        got = jnp.take(jnp.stack(packs), order, axis=0).reshape(lay.n, lay.slots, SUB, LANES)
    carry = got[:-1, lay.units : lay.units + 1]
    carry = jnp.concatenate([jnp.zeros_like(carry[:1]), carry], axis=0)
    units = jnp.concatenate([got[:, :1] + carry, got[:, 1 : lay.units]], axis=1)
    units = units.reshape(MAT_ROWS // UNIT, SUB, LANES)
    w_qkv = units[: QKV_END // UNIT].reshape(D, 3 * HD)
    w_up = units[OUT_END // UNIT : UP_END // UNIT].reshape(D, FF // HEADS)
    w_down = units[UP_END // UNIT :].reshape(FF // HEADS, D)
    out_rows = units[QKV_END // UNIT : OUT_END // UNIT]
    w_out = exchange(lay, out_rows.reshape(HEADS, HD // HEADS, D))
    w_out = w_out.transpose(1, 0, 2).reshape(HD, D)
    extra = jnp.sum(got[:, lay.units + 1 : lay.units + 7].astype(f32), axis=0).reshape(6, D)
    b_qkv = extra[0, : 3 * HD]
    b_up = extra[0, 3 * HD : 3 * HD + FF // HEADS]
    return w_qkv, b_qkv, w_out, w_up, b_up, w_down, extra[1:], seg_all


def collect_grads(lay, units, mixed_row, full, shard_id, rep_id):
    units = units.reshape(lay.n, lay.units, D)
    after = jnp.concatenate([units[1:, :1], jnp.zeros_like(units[:1, :1])], axis=0)
    tail = jnp.concatenate(
        [mixed_row[None], full, jnp.zeros((lay.slots - lay.units - 7, D), bf16)], axis=0
    )
    tail = jnp.broadcast_to(tail[None], (lay.n,) + tail.shape)
    parts = jnp.concatenate([units, after, tail], axis=1)
    by_rep = parts.reshape(lay.n, lay.reps, lay.share, D)
    total = lax.dynamic_index_in_dim(by_rep, rep_id, axis=1, keepdims=False).astype(f32)
    for k in range(1, lay.reps):
        theirs = lax.dynamic_index_in_dim(by_rep, rep_id ^ k, axis=1, keepdims=False)
        total = total + lax.ppermute(theirs, "rep", lay.rep_xor(k)).astype(f32)
    total = total.astype(bf16)
    if lay.packs > 1:
        pack = shard_id // lay.ways
        by_pack = total.reshape(lay.packs, lay.ways, lay.share, D)
        total = lax.dynamic_index_in_dim(by_pack, pack, keepdims=False).astype(f32)
        for k in range(1, lay.packs):
            theirs = lax.dynamic_index_in_dim(by_pack, pack ^ k, keepdims=False)
            total = total + lax.ppermute(theirs, "shard", lay.xor(lay.ways * k)).astype(f32)
        total = total.astype(bf16)
    got = exchange(lay, total)
    got = [got] + [lax.ppermute(got, "rep", lay.rep_xor(k)) for k in range(1, lay.reps)]
    got = jnp.take(jnp.stack(got), jnp.arange(lay.reps, dtype=jnp.int32) ^ rep_id, axis=0)
    got = got.transpose(1, 0, 2, 3).reshape(lay.ways, lay.slots, D)
    body = got[:, : lay.units + 1].reshape(lay.ways, -1, LANES)
    extra = got[:, lay.units + 1 : lay.units + 7].astype(f32)
    qkv_vec = extra[:, 0, : 3 * HD].reshape(HEADS, 3, HD).transpose(1, 0, 2).reshape(3 * D)
    up_vec = extra[:, 0, 3 * HD : 3 * HD + FF // HEADS].T.reshape(FF)
    norm_vec = jnp.sum(extra[:, 1:5], axis=0).reshape(4 * D)
    out_vec = extra[0, 5]
    small = jnp.concatenate([qkv_vec, out_vec, up_vec, out_vec, norm_vec])
    table = jnp.asarray(lay.tables)[shard_id]
    size = (MAT_ROWS + VEC_ROWS) * D // lay.n
    flat = unpack(
        body, shard_id * lay.units, PAD + table[0], PAD + table[1], table[3], size
    )
    flat = flat.reshape(-1)[:size]
    run = 5 * D
    start = jnp.clip(table[3], 0, size - run)
    ids = start + lax.iota(jnp.int32, run)
    from_small = jnp.clip(start - table[5], -run, VEC_ROWS * D) + run
    vec = lax.dynamic_slice(jnp.pad(small, (run, run)), (from_small,), (run,))
    old = lax.dynamic_slice(flat, (start,), (run,))
    new = jnp.where((ids >= table[3]) & (ids < table[4]), vec, old)
    return lax.dynamic_update_slice(flat, new, (start,))


def per_device(lay, tokens, cotangent, segment, params, first_moment, second_moment):
    shard_id = lax.axis_index("shard")
    rep_id = lax.axis_index("rep")
    me = shard_id % lay.ways
    length = tokens.shape[0]
    blocks = lay.ways
    total_rows = blocks * length

    rows_in = gather_rows(lay, tokens)
    w_qkv, b_qkv, w_out, w_up, b_up, w_down, full, seg_all = split_params(
        lay, params, segment, shard_id, rep_id
    )
    b_sum, gain_one, shift_one, gain_two, shift_two = (full[i] for i in range(5))
    own_grad = jnp.where((segment >= 0)[:, None], cotangent, jnp.zeros_like(cotangent))
    rows_grad = gather_rows(lay, own_grad)
    spot = jnp.arange(blocks, dtype=jnp.int32)
    d_core, d_line, d_row = spot // (2 * lay.line), spot // 2 % lay.line, spot % 2
    source = (
        (me // 4 - d_line) % lay.line * 4 + ((me // 2 % 2) ^ d_row) * 2 + ((me % 2) ^ d_core)
    )
    seg = jnp.take(seg_all, source, axis=0)

    row_ids = jnp.arange(length, dtype=jnp.int32)
    position = (row_ids[None] - seg).astype(f32)
    frequency = 10000.0 ** (-jnp.arange(0, ROT, 2, dtype=f32) / ROT)
    phases = position[:, :, None] * frequency
    cosine, sine = jnp.cos(phases), jnp.sin(phases)
    still = jnp.ones((blocks, length, HD - ROT), f32)
    cos_head = jnp.concatenate([cosine, cosine, still], axis=-1)
    sin_head = jnp.concatenate([-sine, sine, 0.0 * still], axis=-1)
    ones = jnp.ones((blocks, length, 2 * HD), f32)
    cosine = jnp.concatenate([cos_head, cos_head, ones], axis=-1).reshape(total_rows, 4 * HD)
    sine = jnp.concatenate([sin_head, sin_head, 0.0 * ones], axis=-1).reshape(total_rows, 4 * HD)
    allowed = (seg[:, :, None] == seg[:, None, :]) & (row_ids[None, :] <= row_ids[:, None])[None]
    mask = jnp.where(allowed, 0.0, -1e30).astype(f32).reshape(total_rows, length)
    bias = jnp.pad(jnp.stack([jnp.pad(b_qkv, (0, HD)), b_up]), ((0, 6), (0, 0)))
    out_part, g_part, grad_qkv, grad_w_up, grad_w_down, grad_w_out, bias_sums, vec_sums = layer(
        rows_in,
        rows_grad,
        cosine,
        sine,
        mask,
        jnp.pad(w_qkv, ((0, 0), (0, HD))),
        w_up,
        w_down,
        jnp.pad(w_out, ((0, LANES - HD), (0, 0))),
        bias,
        jnp.pad(full, ((0, 8 - full.shape[0]), (0, 0))),
    )
    out_sum = scatter_rows(lay, out_part, length)
    g_sum = scatter_rows(lay, g_part, length)
    own = tokens.astype(f32)
    own_center = own - jnp.mean(own, axis=-1, keepdims=True)
    own_inverse = lax.rsqrt(jnp.mean(own_center * own_center, axis=-1, keepdims=True) + norm_eps)
    own_hat = own_center * own_inverse
    grad_rows = (
        own_grad.astype(f32)
        + own_inverse
        * (
            g_sum
            - jnp.mean(g_sum, axis=-1, keepdims=True)
            - own_hat * jnp.mean(g_sum * own_hat, axis=-1, keepdims=True)
        )
    ).astype(bf16)

    grad_w_qkv = grad_qkv[:, : 3 * HD]
    back = grad_w_out[:HD].reshape(HD // HEADS, HEADS, D).transpose(1, 0, 2)
    back = exchange(lay, back).reshape(HD, D)
    units = jnp.concatenate(
        [
            grad_w_qkv.reshape(QKV_END // UNIT, D),
            back,
            grad_w_up.reshape(FF // UNIT, D),
            grad_w_down,
        ],
        axis=0,
    )
    used = 3 * HD + FF // HEADS
    mixed_row = jnp.concatenate(
        [bias_sums[0, : 3 * HD], bias_sums[1], jnp.zeros((D - used,), f32)]
    ).astype(bf16)
    vectors = vec_sums[:5].astype(bf16)
    units, out_sum = lax.optimization_barrier((units, out_sum))
    out_rows = (tokens.astype(f32) + out_sum + b_sum).astype(bf16)
    grad_total = collect_grads(lay, units, mixed_row, vectors, shard_id, rep_id)
    new_weights, first_new, second_new = adam_update(
        params, first_moment, second_moment, grad_total
    )
    return (out_rows, grad_rows, grad_total, new_weights, first_new, second_new)


def solution(mesh):
    lay = Layout(mesh)
    in_specs = (
        P(("rep", "shard"), None),
        P(("rep", "shard"), None),
        P(("rep", "shard")),
        P("shard"),
        P("shard"),
        P("shard"),
    )
    out_specs = (
        P(("rep", "shard"), None),
        P(("rep", "shard"), None),
        P("shard"),
        P("shard"),
        P("shard"),
        P("shard"),
    )

    def body(*args):
        return per_device(lay, *args)

    return jax.shard_map(body, mesh=mesh, in_specs=in_specs, out_specs=out_specs, check_vma=False)
```

```python
import math

import jax
import jax.numpy as jnp
import numpy as np
from jax import lax
from jax.experimental import pallas as pl
from jax.experimental.pallas import tpu as pltpu
from jax.sharding import PartitionSpec as P

D = 1024
HEADS = 16
HD = 64
ROT = 16
FF = 4096
STEP = 4
UNIT = HEADS

norm_eps = 1e-05
adam_eps = 1e-08
beta_one = 0.9
beta_two = 0.999
learn_rate = 0.003
decay_rate = 0.1
root_half = 0.7071067811865476
inv_root_twopi = 0.3989422804014327


QKV_END = 3 * D
OUT_END = QKV_END + D
UP_END = OUT_END + FF
DOWN_END = UP_END + FF
MAT_ROWS = DOWN_END
SECTIONS = ((0, QKV_END, 0), (QKV_END, OUT_END, 3), (OUT_END, UP_END, 4), (UP_END, DOWN_END, 8))
RUNS = (
    (QKV_END, 3, 0),
    (OUT_END + 3, 1, 3),
    (UP_END + 4, 4, 4),
    (DOWN_END + 8, 5, 8),
)
VEC_ROWS = 13
PAD = 8 * D

f32 = jnp.float32
bf16 = jnp.bfloat16


def owner_tables(owners):
    total = (MAT_ROWS + VEC_ROWS) * D
    part = total // owners
    lead = VEC_ROWS * D // owners
    rows = []
    for s in range(owners):
        start, end = s * part, (s + 1) * part
        first = next((i for i, (a, b, v) in enumerate(SECTIONS) if (b + v) * D > start), 3)
        second = min(first + 1, 3)
        run_row, run_len, vec_row = RUNS[first]
        run_a = min(max(run_row * D - start, 0), part)
        run_b = min(max((run_row + run_len) * D - start, 0), part)
        rows.append(
            (
                lead * s - SECTIONS[first][2] * D,
                lead * s - SECTIONS[second][2] * D,
                (SECTIONS[first][1] - (MAT_ROWS // owners) * s) if first < 3 else 2 * MAT_ROWS,
                run_a,
                run_b,
                run_row * D - start - vec_row * D,
            )
        )
    return np.array(rows, np.int32)


def rotate(values, cosine, sine_part):
    half_rot = ROT // 2
    lower_half = values[..., :half_rot]
    upper_half = values[..., half_rot:ROT]
    return jnp.concatenate(
        [
            lower_half * cosine - upper_half * sine_part,
            upper_half * cosine + lower_half * sine_part,
            values[..., ROT:],
        ],
        axis=-1,
    )


def gelu_parts(values):
    cdf = 0.5 * (1.0 + lax.erf(values * root_half))
    return values * cdf, cdf + values * jnp.exp(-0.5 * values * values) * inv_root_twopi


def adam_update(weights, moment_one, moment_two, grad_total):
    first_new = beta_one * moment_one + (1.0 - beta_one) * grad_total
    second_new = beta_two * moment_two + (1.0 - beta_two) * grad_total * grad_total
    correct_one = 1.0 - beta_one**STEP
    correct_two = 1.0 - beta_two**STEP
    change = first_new / correct_one / (jnp.sqrt(second_new / correct_two) + adam_eps)
    return (weights - learn_rate * (change + decay_rate * weights), first_new, second_new)


def bmm(spec, a, b):
    return jnp.einsum(spec, a, b, preferred_element_type=f32)


class Layout:
    def __init__(self, mesh):
        self.n = mesh.shape["shard"]
        self.reps = mesh.shape["rep"]
        self.ways = HEADS
        assert self.n % self.ways == 0
        self.packs = self.n // self.ways
        self.core, self.row = 2, 2
        self.line = self.ways // 4
        self.units = MAT_ROWS // UNIT // self.n
        slots = self.units + 1 + 1 + 5
        self.slots = -(-slots // self.reps) * self.reps
        self.share = self.slots // self.reps
        self.tables = owner_tables(self.n)

    def xor(self, k):
        return [(i, i ^ k) for i in range(self.n)]

    def step(self, k):
        w = self.ways
        return [(i, i - i % w + (i % w + 4 * k) % w) for i in range(self.n)]

    def rep_xor(self, k):
        return [(i, i ^ k) for i in range(self.reps)]


def gather_rows(lay, block):
    chain = [block]
    for _ in range(lay.line - 1):
        chain.append(lax.ppermute(chain[-1], "shard", lay.step(1)))
    plane = []
    for piece in chain:
        plane += [piece, lax.ppermute(piece, "shard", lay.xor(2))]
    plane = jnp.concatenate(plane, axis=0)
    return jnp.concatenate([plane, lax.ppermute(plane, "shard", lay.xor(1))], axis=0)


def scatter_rows(lay, partial_rows, length):
    half = partial_rows.shape[0] // 2
    plane = partial_rows[:half].astype(f32) + lax.ppermute(
        partial_rows[half:], "shard", lay.xor(1)
    ).astype(f32)
    plane = plane.reshape(lay.line, 2, length, -1)
    mine = []
    for d in range(lay.line):
        mine.append(plane[d, 0] + lax.ppermute(plane[d, 1].astype(bf16), "shard", lay.xor(2)))
    total = mine[-1]
    for d in range(lay.line - 2, -1, -1):
        total = mine[d] + lax.ppermute(total.astype(bf16), "shard", lay.step(-1))
    return total


def exchange(lay, parts):
    groups = [list(range(p * lay.ways, (p + 1) * lay.ways)) for p in range(lay.packs)]
    return lax.all_to_all(
        parts, "shard", 0, 0, axis_index_groups=groups if lay.packs > 1 else None, tiled=True
    )


LANES = 128
SUB = D // LANES
TILE = 256
VMEM_LIMIT = 56 * 1024 * 1024


def spread_matrix():
    row = lax.broadcasted_iota(jnp.int32, (D, D), 0)
    col = lax.broadcasted_iota(jnp.int32, (D, D), 1)
    return jnp.where(row == (col % HD) * HEADS + col // HD, 1.0, 0.0).astype(bf16)


def unit_masks(first_unit, amount):
    unit = lax.broadcasted_iota(jnp.int32, (amount, LANES), 0) // SUB + first_unit
    is_up = (unit >= OUT_END // UNIT) & (unit < UP_END // UNIT)
    by_row = ((unit >= QKV_END // UNIT) & (unit < OUT_END // UNIT)) | (unit >= UP_END // UNIT)
    return is_up, by_row


def pack_kernel(info_ref, first_ref, second_ref, out_ref, x_ref):
    rows = first_ref.shape[0]
    amount = rows // UNIT
    ids = lax.broadcasted_iota(jnp.int32, (rows, LANES), 0)
    x_ref[...] = jnp.where(
        ids < info_ref[0], first_ref[...].astype(f32), second_ref[...].astype(f32)
    )
    is_up, by_row = unit_masks(info_ref[1], amount)
    low = lax.broadcasted_iota(jnp.int32, (amount, LANES), 1) < HD
    spread = spread_matrix()
    halves = []
    for p in range(2):
        cols = [x_ref[pl.ds(SUB * p + a, amount, stride=UNIT), :] for a in range(SUB)]
        moved = jnp.dot(
            jnp.concatenate(cols, axis=1).astype(bf16), spread, preferred_element_type=f32
        )
        halves.append(
            [
                jnp.where(is_up, moved[:, a * LANES : (a + 1) * LANES], cols[a])
                for a in range(SUB)
            ]
        )
    whole = x_ref[...].reshape(amount // SUB, UNIT, SUB, LANES)
    for t in range(HEADS):
        zero, one = halves[0][t // 2], halves[1][t // 2]
        if t % 2 == 0:
            piece = jnp.where(low, zero, pltpu.roll(one, HD, 1))
        else:
            piece = jnp.where(low, pltpu.roll(zero, HD, 1), one)
        direct = whole[:, t].reshape(amount, LANES)
        out_ref[t] = jnp.where(by_row, direct, piece).astype(bf16)


def pack(first, second, bound, first_unit):
    rows = first.shape[0]
    return pl.pallas_call(
        pack_kernel,
        out_shape=jax.ShapeDtypeStruct((HEADS, rows // UNIT, LANES), bf16),
        in_specs=[
            pl.BlockSpec(memory_space=pltpu.SMEM),
            pl.BlockSpec(memory_space=pltpu.VMEM),
            pl.BlockSpec(memory_space=pltpu.VMEM),
        ],
        out_specs=pl.BlockSpec(memory_space=pltpu.VMEM),
        scratch_shapes=[pltpu.VMEM((rows, LANES), f32)],
        compiler_params=pltpu.CompilerParams(vmem_limit_bytes=VMEM_LIMIT),
        name="pack",
    )(jnp.stack([bound, first_unit]).astype(jnp.int32), first, second)


MARGIN = 64


def unpack_kernel(info_ref, got_ref, out_ref, x_ref):
    amount = got_ref.shape[1]
    rows = amount * UNIT
    is_up, by_row = unit_masks(info_ref[0], amount)
    low = lax.broadcasted_iota(jnp.int32, (amount, LANES), 1) < HD
    spread = spread_matrix()
    x_ref[pl.ds(0, MARGIN), :] = jnp.zeros((MARGIN, LANES), f32)
    x_ref[pl.ds(MARGIN + rows, MARGIN), :] = jnp.zeros((MARGIN, LANES), f32)
    for p in range(2):
        cols = []
        for a in range(SUB):
            even, odd = got_ref[2 * a].astype(f32), got_ref[2 * a + 1].astype(f32)
            if p == 0:
                cols.append(jnp.where(low, even, pltpu.roll(odd, HD, 1)))
            else:
                cols.append(jnp.where(low, pltpu.roll(even, HD, 1), odd))
        moved = lax.dot_general(
            jnp.concatenate(cols, axis=1).astype(bf16),
            spread,
            (((1,), (1,)), ((), ())),
            preferred_element_type=f32,
        )
        for a in range(SUB):
            x_ref[pl.ds(MARGIN + SUB * p + a, amount, stride=UNIT), :] = jnp.where(
                is_up, moved[:, a * LANES : (a + 1) * LANES], cols[a]
            )
    whole = x_ref[pl.ds(MARGIN, rows), :].reshape(amount // SUB, UNIT, SUB, LANES)
    keep = by_row.reshape(amount // SUB, SUB, LANES)
    mixed = [
        jnp.where(keep, got_ref[t].astype(f32).reshape(amount // SUB, SUB, LANES), whole[:, t])
        for t in range(HEADS)
    ]
    x_ref[pl.ds(MARGIN, rows), :] = jnp.stack(mixed, axis=1).reshape(rows, LANES)
    size = out_ref.shape[0]
    low = lax.broadcasted_iota(jnp.int32, (size, LANES), 1) < HD

    def cut(start):
        base = start // 2
        here = x_ref[pl.ds(base, size), :]
        after = x_ref[pl.ds(base + 1, size), :]
        split = jnp.where(low, pltpu.roll(here, HD, 1), pltpu.roll(after, HD, 1))
        return jnp.where(start % 2 == 1, split, here)

    place = 2 * lax.broadcasted_iota(jnp.int32, (size, LANES), 0) + jnp.where(low, 0, 1)
    first = cut(info_ref[1])
    out_ref[...] = first
    out_ref[...] = jnp.where(place < info_ref[3], out_ref[...], cut(info_ref[2]))


def unpack(got, first_unit, start_one, start_two, bound, size):
    amount = got.shape[1]
    out_rows = -(-size // (SUB * LANES)) * SUB
    info = jnp.stack([first_unit, start_one // HD, start_two // HD, bound // HD])
    return pl.pallas_call(
        unpack_kernel,
        out_shape=jax.ShapeDtypeStruct((out_rows, LANES), f32),
        in_specs=[
            pl.BlockSpec(memory_space=pltpu.SMEM),
            pl.BlockSpec(memory_space=pltpu.VMEM),
        ],
        out_specs=pl.BlockSpec(memory_space=pltpu.VMEM),
        scratch_shapes=[pltpu.VMEM((amount * UNIT + 2 * MARGIN, LANES), f32)],
        compiler_params=pltpu.CompilerParams(vmem_limit_bytes=VMEM_LIMIT),
        name="unpack",
    )(info.astype(jnp.int32), got)


def nt(a, b):
    return lax.dot_general(a, b, (((1,), (1,)), ((), ())), preferred_element_type=f32)


def tn(a, b):
    return lax.dot_general(a, b, (((0,), (0,)), ((), ())), preferred_element_type=f32)


def nn(a, b):
    return lax.dot_general(a, b, (((1,), (0,)), ((), ())), preferred_element_type=f32)


def layer_kernel(
    both_ref,
    cos_ref,
    sin_ref,
    mask_ref,
    w_qkv_ref,
    w_up_ref,
    w_down_ref,
    w_out_ref,
    bias_ref,
    vec_ref,
    sums_ref,
    gqkv_ref,
    gup_ref,
    gdown_ref,
    gout_ref,
    gbias_ref,
    gvec_ref,
    aqkv,
    aup,
    adown,
    aout,
):
    step = pl.program_id(0)

    @pl.when(step == 0)
    def _():
        for ref in (aqkv, aup, adown, aout, gbias_ref, gvec_ref):
            ref[...] = jnp.zeros(ref.shape, ref.dtype)

    length = mask_ref.shape[1]
    lane = lax.broadcasted_iota(jnp.int32, (TILE, 2 * LANES), 1) % HD
    low_rot = lane < ROT // 2
    low = lax.broadcasted_iota(jnp.int32, (length, LANES), 1) < HD
    gain_one, shift_one = vec_ref[1:2, :], vec_ref[2:3, :]
    gain_two, shift_two = vec_ref[3:4, :], vec_ref[4:5, :]

    def swap(v):
        ahead = pltpu.roll(v, 2 * LANES - ROT // 2, 1)
        return jnp.where(low_rot, ahead, pltpu.roll(v, ROT // 2, 1))

    x = both_ref[:, :D].astype(f32)
    center = x - jnp.mean(x, axis=1, keepdims=True)
    inverse = lax.rsqrt(jnp.mean(center * center, axis=1, keepdims=True) + norm_eps)
    hat = center * inverse
    in_one = (hat * gain_one + shift_one).astype(bf16)
    in_two = (hat * gain_two + shift_two).astype(bf16)
    go = both_ref[:, D:]

    hidden = nn(in_two, w_up_ref[...]) + bias_ref[1:2, :]
    cdf = 0.5 * (1.0 + lax.erf(hidden * root_half))
    active = (hidden * cdf).astype(bf16)
    slope = cdf + hidden * jnp.exp(-0.5 * hidden * hidden) * inv_root_twopi
    ghid = nt(go, w_down_ref[...]) * slope
    ghid_bf = ghid.astype(bf16)

    mixed = nn(in_one, w_qkv_ref[...]) + bias_ref[0:1, :]
    cosine, sine = cos_ref[...], sin_ref[...]
    rot = mixed * cosine + swap(mixed) * sine
    gheads = nt(go, w_out_ref[...]).astype(bf16)
    scale = HD ** (-0.5)
    heads, gmix = [], []
    for b in range(TILE // length):
        part = slice(b * length, (b + 1) * length)
        qk = rot[part, :LANES]
        vv = rot[part, LANES:].astype(bf16)
        turned = pltpu.roll(qk, HD, 1)
        q_low = jnp.where(low, qk, 0.0).astype(bf16)
        k_low = jnp.where(low, turned, 0.0).astype(bf16)
        q_high = jnp.where(low, 0.0, turned).astype(bf16)
        gh = gheads[part]
        scores = nt(q_low, k_low) * scale + mask_ref[part, :]
        expd = jnp.exp(scores - jnp.max(scores, axis=1, keepdims=True))
        probs = expd / jnp.sum(expd, axis=1, keepdims=True)
        probs_bf = probs.astype(bf16)
        head = nn(probs_bf, vv).astype(bf16)
        heads.append(head)
        delta = jnp.sum(gh.astype(f32) * head.astype(f32), axis=1, keepdims=True)
        gs = (probs * (nt(gh, vv) - delta) * scale).astype(bf16)
        gqk = nn(gs, k_low) + tn(gs, q_high)
        gv = tn(probs_bf, gh)
        gmix.append(jnp.concatenate([gqk, gv], axis=1))
    head = jnp.concatenate(heads, axis=0)
    gmix = jnp.concatenate(gmix, axis=0)
    gmix = gmix * cosine - swap(gmix) * sine
    gmix_bf = gmix.astype(bf16)

    sums_ref[:, :D] = (nn(head, w_out_ref[...]) + nn(active, w_down_ref[...])).astype(bf16)
    norm_one = nt(gmix_bf, w_qkv_ref[...])
    norm_two = nt(ghid_bf, w_up_ref[...])
    sums_ref[:, D:] = (norm_one * gain_one + norm_two * gain_two).astype(bf16)
    gvec_ref[0:1, :] += jnp.sum(norm_one * hat, axis=0, keepdims=True)
    gvec_ref[1:2, :] += jnp.sum(norm_one, axis=0, keepdims=True)
    gvec_ref[2:3, :] += jnp.sum(norm_two * hat, axis=0, keepdims=True)
    gvec_ref[3:4, :] += jnp.sum(norm_two, axis=0, keepdims=True)
    gvec_ref[4:5, :] += jnp.sum(go.astype(f32), axis=0, keepdims=True)
    gbias_ref[0:1, :] += jnp.sum(gmix, axis=0, keepdims=True)
    gbias_ref[1:2, :] += jnp.sum(ghid, axis=0, keepdims=True)
    aqkv[...] += tn(in_one, gmix_bf)
    aup[...] += tn(in_two, ghid_bf)
    adown[...] += tn(active, go)
    aout[...] += tn(head, go)

    @pl.when(step == pl.num_programs(0) - 1)
    def _():
        gqkv_ref[...] = aqkv[...].astype(bf16)
        gup_ref[...] = aup[...].astype(bf16)
        gdown_ref[...] = adown[...].astype(bf16)
        gout_ref[...] = aout[...].astype(bf16)


def layer(both, cosine, sine, mask, w_qkv, w_up, w_down, w_out, bias, vec):
    rows = both.shape[0]
    wide = 2 * LANES
    cols = FF // HEADS

    def tile(width):
        return pl.BlockSpec((TILE, width), lambda i: (i, 0))

    def whole(a, b):
        return pl.BlockSpec((a, b), lambda i: (0, 0))

    return pl.pallas_call(
        layer_kernel,
        grid=(rows // TILE,),
        in_specs=[
            tile(2 * D),
            tile(wide),
            tile(wide),
            tile(mask.shape[1]),
            whole(D, wide),
            whole(D, cols),
            whole(cols, D),
            whole(LANES, D),
            whole(8, wide),
            whole(8, D),
        ],
        out_specs=[
            tile(2 * D),
            whole(D, wide),
            whole(D, cols),
            whole(cols, D),
            whole(LANES, D),
            whole(8, wide),
            whole(8, D),
        ],
        out_shape=[
            jax.ShapeDtypeStruct((rows, 2 * D), bf16),
            jax.ShapeDtypeStruct((D, wide), bf16),
            jax.ShapeDtypeStruct((D, cols), bf16),
            jax.ShapeDtypeStruct((cols, D), bf16),
            jax.ShapeDtypeStruct((LANES, D), bf16),
            jax.ShapeDtypeStruct((8, wide), f32),
            jax.ShapeDtypeStruct((8, D), f32),
        ],
        scratch_shapes=[
            pltpu.VMEM((D, wide), f32),
            pltpu.VMEM((D, cols), f32),
            pltpu.VMEM((cols, D), f32),
            pltpu.VMEM((LANES, D), f32),
        ],
        compiler_params=pltpu.CompilerParams(vmem_limit_bytes=VMEM_LIMIT),
        name="layer",
    )(both, cosine, sine, mask, w_qkv, w_up, w_down, w_out, bias, vec)


def split_params(lay, params, segment, shard_id, rep_id):
    table = jnp.asarray(lay.tables)[shard_id]
    rows = (lay.units + 1) * UNIT
    chunk = params.astype(bf16)
    padded = jnp.pad(chunk, (PAD, rows * D + 2 * PAD - chunk.shape[0]))
    first = lax.dynamic_slice(padded, (PAD - table[0],), (rows * D,)).reshape(rows * SUB, LANES)
    second = lax.dynamic_slice(padded, (PAD - table[1],), (rows * D,)).reshape(rows * SUB, LANES)
    body = pack(first, second, table[2] * SUB, shard_id * lay.units)
    size = chunk.shape[0]
    vec = []
    for flat_row, amount, _ in RUNS:
        start = flat_row * D - shard_id * size
        begin = jnp.clip(start, -PAD, size)
        piece = lax.dynamic_slice(padded, (PAD + begin,), (amount * D,))
        vec.append(jnp.where(start == begin, piece, 0).reshape(amount, D))
    qkv_cols = vec[0].reshape(3, HEADS, HD).transpose(1, 0, 2).reshape(HEADS, 3 * HD)
    up_cols = vec[2].reshape(FF // HEADS, HEADS).T
    used = qkv_cols.shape[1] + up_cols.shape[1]
    mixed_row = jnp.concatenate([qkv_cols, up_cols, jnp.zeros((HEADS, D - used), bf16)], axis=1)
    mixed_row = mixed_row[:, None]
    full = jnp.concatenate(
        [vec[1] + vec[3][:1], vec[3][1:], jnp.zeros((lay.slots - lay.units - 7, D), bf16)], axis=0
    )
    full = jnp.broadcast_to(full[None], (HEADS,) + full.shape)
    tail = jnp.concatenate([mixed_row, full], axis=1).reshape(HEADS, -1, LANES)
    parts = jnp.concatenate([body, tail], axis=1)
    wide = lay.share * SUB
    share = lax.dynamic_slice_in_dim(parts, rep_id * wide, wide, axis=1)
    seg_row = jnp.pad(segment.astype(bf16), (0, D - segment.shape[0]))
    seg_row = jnp.broadcast_to(seg_row.reshape(1, SUB, LANES), (HEADS, SUB, LANES))
    got = exchange(lay, jnp.concatenate([share, seg_row], axis=1))
    seg_all = got[:, wide].astype(jnp.int32)
    got = got[:, :wide]
    got = [got] + [lax.ppermute(got, "rep", lay.rep_xor(k)) for k in range(1, lay.reps)]
    got = jnp.take(jnp.stack(got), jnp.arange(lay.reps, dtype=jnp.int32) ^ rep_id, axis=0)
    got = got.transpose(1, 0, 2, 3).reshape(lay.ways, lay.slots, SUB, LANES)
    if lay.packs > 1:
        packs = [got] + [
            lax.ppermute(got, "shard", lay.xor(lay.ways * k)) for k in range(1, lay.packs)
        ]
        order = jnp.arange(lay.packs, dtype=jnp.int32) ^ (shard_id // lay.ways)
        got = jnp.take(jnp.stack(packs), order, axis=0).reshape(lay.n, lay.slots, SUB, LANES)
    carry = got[:-1, lay.units : lay.units + 1]
    carry = jnp.concatenate([jnp.zeros_like(carry[:1]), carry], axis=0)
    units = jnp.concatenate([got[:, :1] + carry, got[:, 1 : lay.units]], axis=1)
    units = units.reshape(MAT_ROWS // UNIT, SUB, LANES)
    w_qkv = units[: QKV_END // UNIT].reshape(D, 3 * HD)
    w_up = units[OUT_END // UNIT : UP_END // UNIT].reshape(D, FF // HEADS)
    w_down = units[UP_END // UNIT :].reshape(FF // HEADS, D)
    out_rows = units[QKV_END // UNIT : OUT_END // UNIT]
    w_out = exchange(lay, out_rows.reshape(HEADS, HD // HEADS, D))
    w_out = w_out.transpose(1, 0, 2).reshape(HD, D)
    extra = jnp.sum(got[:, lay.units + 1 : lay.units + 7].astype(f32), axis=0).reshape(6, D)
    b_qkv = extra[0, : 3 * HD]
    b_up = extra[0, 3 * HD : 3 * HD + FF // HEADS]
    return w_qkv, b_qkv, w_out, w_up, b_up, w_down, extra[1:], seg_all


def collect_grads(lay, units, mixed_row, full, shard_id, rep_id):
    units = units.reshape(lay.n, lay.units, D)
    after = jnp.concatenate([units[1:, :1], jnp.zeros_like(units[:1, :1])], axis=0)
    tail = jnp.concatenate(
        [mixed_row[None], full, jnp.zeros((lay.slots - lay.units - 7, D), bf16)], axis=0
    )
    tail = jnp.broadcast_to(tail[None], (lay.n,) + tail.shape)
    parts = jnp.concatenate([units, after, tail], axis=1)
    by_rep = parts.reshape(lay.n, lay.reps, lay.share, D)
    total = lax.dynamic_index_in_dim(by_rep, rep_id, axis=1, keepdims=False).astype(f32)
    for k in range(1, lay.reps):
        theirs = lax.dynamic_index_in_dim(by_rep, rep_id ^ k, axis=1, keepdims=False)
        total = total + lax.ppermute(theirs, "rep", lay.rep_xor(k)).astype(f32)
    total = total.astype(bf16)
    if lay.packs > 1:
        pack = shard_id // lay.ways
        by_pack = total.reshape(lay.packs, lay.ways, lay.share, D)
        total = lax.dynamic_index_in_dim(by_pack, pack, keepdims=False).astype(f32)
        for k in range(1, lay.packs):
            theirs = lax.dynamic_index_in_dim(by_pack, pack ^ k, keepdims=False)
            total = total + lax.ppermute(theirs, "shard", lay.xor(lay.ways * k)).astype(f32)
        total = total.astype(bf16)
    got = exchange(lay, total)
    got = [got] + [lax.ppermute(got, "rep", lay.rep_xor(k)) for k in range(1, lay.reps)]
    got = jnp.take(jnp.stack(got), jnp.arange(lay.reps, dtype=jnp.int32) ^ rep_id, axis=0)
    got = got.transpose(1, 0, 2, 3).reshape(lay.ways, lay.slots, D)
    body = got[:, : lay.units + 1].reshape(lay.ways, -1, LANES)
    extra = got[:, lay.units + 1 : lay.units + 7].astype(f32)
    qkv_vec = extra[:, 0, : 3 * HD].reshape(HEADS, 3, HD).transpose(1, 0, 2).reshape(3 * D)
    up_vec = extra[:, 0, 3 * HD : 3 * HD + FF // HEADS].T.reshape(FF)
    norm_vec = jnp.sum(extra[:, 1:5], axis=0).reshape(4 * D)
    out_vec = extra[0, 5]
    small = jnp.concatenate([qkv_vec, out_vec, up_vec, out_vec, norm_vec])
    table = jnp.asarray(lay.tables)[shard_id]
    size = (MAT_ROWS + VEC_ROWS) * D // lay.n
    flat = unpack(
        body, shard_id * lay.units, PAD + table[0], PAD + table[1], table[3], size
    )
    flat = flat.reshape(-1)[:size]
    run = 5 * D
    start = jnp.clip(table[3], 0, size - run)
    ids = start + lax.iota(jnp.int32, run)
    from_small = jnp.clip(start - table[5], -run, VEC_ROWS * D) + run
    vec = lax.dynamic_slice(jnp.pad(small, (run, run)), (from_small,), (run,))
    old = lax.dynamic_slice(flat, (start,), (run,))
    new = jnp.where((ids >= table[3]) & (ids < table[4]), vec, old)
    return lax.dynamic_update_slice(flat, new, (start,))


def per_device(lay, tokens, cotangent, segment, params, first_moment, second_moment):
    shard_id = lax.axis_index("shard")
    rep_id = lax.axis_index("rep")
    me = shard_id % lay.ways
    length = tokens.shape[0]
    blocks = lay.ways
    total_rows = blocks * length

    own_grad = jnp.where((segment >= 0)[:, None], cotangent, jnp.zeros_like(cotangent))
    rows_both = gather_rows(lay, jnp.concatenate([tokens, own_grad], axis=1))
    w_qkv, b_qkv, w_out, w_up, b_up, w_down, full, seg_all = split_params(
        lay, params, segment, shard_id, rep_id
    )
    b_sum, gain_one, shift_one, gain_two, shift_two = (full[i] for i in range(5))
    spot = jnp.arange(blocks, dtype=jnp.int32)
    d_core, d_line, d_row = spot // (2 * lay.line), spot // 2 % lay.line, spot % 2
    source = (
        (me // 4 - d_line) % lay.line * 4 + ((me // 2 % 2) ^ d_row) * 2 + ((me % 2) ^ d_core)
    )
    seg = jnp.take(seg_all, source, axis=0)

    row_ids = jnp.arange(length, dtype=jnp.int32)
    position = (row_ids[None] - seg).astype(f32)
    frequency = 10000.0 ** (-jnp.arange(0, ROT, 2, dtype=f32) / ROT)
    phases = position[:, :, None] * frequency
    cosine, sine = jnp.cos(phases), jnp.sin(phases)
    still = jnp.ones((blocks, length, HD - ROT), f32)
    cos_head = jnp.concatenate([cosine, cosine, still], axis=-1)
    sin_head = jnp.concatenate([-sine, sine, 0.0 * still], axis=-1)
    ones = jnp.ones((blocks, length, 2 * HD), f32)
    cosine = jnp.concatenate([cos_head, cos_head, ones], axis=-1).reshape(total_rows, 4 * HD)
    sine = jnp.concatenate([sin_head, sin_head, 0.0 * ones], axis=-1).reshape(total_rows, 4 * HD)
    allowed = (seg[:, :, None] == seg[:, None, :]) & (row_ids[None, :] <= row_ids[:, None])[None]
    mask = jnp.where(allowed, 0.0, -1e30).astype(f32).reshape(total_rows, length)
    bias = jnp.pad(jnp.stack([jnp.pad(b_qkv, (0, HD)), b_up]), ((0, 6), (0, 0)))
    sums, grad_qkv, grad_w_up, grad_w_down, grad_w_out, bias_sums, vec_sums = layer(
        rows_both,
        cosine,
        sine,
        mask,
        jnp.pad(w_qkv, ((0, 0), (0, HD))),
        w_up,
        w_down,
        jnp.pad(w_out, ((0, LANES - HD), (0, 0))),
        bias,
        jnp.pad(full, ((0, 8 - full.shape[0]), (0, 0))),
    )
    sums = scatter_rows(lay, sums, length)
    out_sum, g_sum = sums[:, :D], sums[:, D:]
    own = tokens.astype(f32)
    own_center = own - jnp.mean(own, axis=-1, keepdims=True)
    own_inverse = lax.rsqrt(jnp.mean(own_center * own_center, axis=-1, keepdims=True) + norm_eps)
    own_hat = own_center * own_inverse
    grad_rows = (
        own_grad.astype(f32)
        + own_inverse
        * (
            g_sum
            - jnp.mean(g_sum, axis=-1, keepdims=True)
            - own_hat * jnp.mean(g_sum * own_hat, axis=-1, keepdims=True)
        )
    ).astype(bf16)

    grad_w_qkv = grad_qkv[:, : 3 * HD]
    back = grad_w_out[:HD].reshape(HD // HEADS, HEADS, D).transpose(1, 0, 2)
    back = exchange(lay, back).reshape(HD, D)
    units = jnp.concatenate(
        [
            grad_w_qkv.reshape(QKV_END // UNIT, D),
            back,
            grad_w_up.reshape(FF // UNIT, D),
            grad_w_down,
        ],
        axis=0,
    )
    used = 3 * HD + FF // HEADS
    mixed_row = jnp.concatenate(
        [bias_sums[0, : 3 * HD], bias_sums[1], jnp.zeros((D - used,), f32)]
    ).astype(bf16)
    vectors = vec_sums[:5].astype(bf16)
    out_rows = (tokens.astype(f32) + out_sum + b_sum).astype(bf16)
    grad_total = collect_grads(lay, units, mixed_row, vectors, shard_id, rep_id)
    new_weights, first_new, second_new = adam_update(
        params, first_moment, second_moment, grad_total
    )
    return (out_rows, grad_rows, grad_total, new_weights, first_new, second_new)


def solution(mesh):
    lay = Layout(mesh)
    in_specs = (
        P(("rep", "shard"), None),
        P(("rep", "shard"), None),
        P(("rep", "shard")),
        P("shard"),
        P("shard"),
        P("shard"),
    )
    out_specs = (
        P(("rep", "shard"), None),
        P(("rep", "shard"), None),
        P("shard"),
        P("shard"),
        P("shard"),
        P("shard"),
    )

    def body(*args):
        return per_device(lay, *args)

    return jax.shard_map(body, mesh=mesh, in_specs=in_specs, out_specs=out_specs, check_vma=False)
```

```python
import jax
import jax.numpy as jnp
import numpy as np
from jax import lax
from jax.experimental import pallas as pl
from jax.experimental.pallas import tpu as pltpu
from jax.sharding import PartitionSpec as P


D = 1024
HEADS = 16
HD = 64
ROT = 16
FF = 4096
STEP = 4
UNIT = HEADS

norm_eps = 1e-05
adam_eps = 1e-08
beta_one = 0.9
beta_two = 0.999
learn_rate = 0.003
decay_rate = 0.1
root_half = 0.7071067811865476
inv_root_twopi = 0.3989422804014327


QKV_END = 3 * D
OUT_END = QKV_END + D
UP_END = OUT_END + FF
DOWN_END = UP_END + FF
MAT_ROWS = DOWN_END
SECTIONS = ((0, QKV_END, 0), (QKV_END, OUT_END, 3), (OUT_END, UP_END, 4), (UP_END, DOWN_END, 8))
RUNS = (
    (QKV_END, 3, 0),
    (OUT_END + 3, 1, 3),
    (UP_END + 4, 4, 4),
    (DOWN_END + 8, 5, 8),
)
VEC_ROWS = 13
PAD = 8 * D

f32 = jnp.float32
bf16 = jnp.bfloat16


def owner_tables(owners):
    total = (MAT_ROWS + VEC_ROWS) * D
    part = total // owners
    lead = VEC_ROWS * D // owners
    rows = []
    for s in range(owners):
        start = s * part
        first = next((i for i, (a, b, v) in enumerate(SECTIONS) if (b + v) * D > start), 3)
        second = min(first + 1, 3)
        run_row, run_len, vec_row = RUNS[first]
        run_a = min(max(run_row * D - start, 0), part)
        run_b = min(max((run_row + run_len) * D - start, 0), part)
        rows.append(
            (
                lead * s - SECTIONS[first][2] * D,
                lead * s - SECTIONS[second][2] * D,
                (SECTIONS[first][1] - (MAT_ROWS // owners) * s) if first < 3 else 2 * MAT_ROWS,
                run_a,
                run_b,
                run_row * D - start - vec_row * D,
            )
        )
    return np.array(rows, np.int32)


def adam_update(weights, moment_one, moment_two, grad_total):
    first_new = beta_one * moment_one + (1.0 - beta_one) * grad_total
    second_new = beta_two * moment_two + (1.0 - beta_two) * grad_total * grad_total
    correct_one = 1.0 - beta_one**STEP
    correct_two = 1.0 - beta_two**STEP
    change = first_new / correct_one / (jnp.sqrt(second_new / correct_two) + adam_eps)
    return (weights - learn_rate * (change + decay_rate * weights), first_new, second_new)


class Layout:
    def __init__(self, mesh):
        self.n = mesh.shape["shard"]
        self.reps = mesh.shape["rep"]
        self.ways = HEADS
        assert self.n % self.ways == 0
        self.packs = self.n // self.ways
        self.core, self.row = 2, 2
        self.line = self.ways // 4
        self.units = MAT_ROWS // UNIT // self.n
        slots = self.units + 1 + 1 + 5
        self.slots = -(-slots // self.reps) * self.reps
        self.share = self.slots // self.reps
        self.tables = owner_tables(self.n)

    def xor(self, k):
        return [(i, i ^ k) for i in range(self.n)]

    def step(self, k):
        w = self.ways
        return [(i, i - i % w + (i % w + 4 * k) % w) for i in range(self.n)]

    def rep_xor(self, k):
        return [(i, i ^ k) for i in range(self.reps)]


def gather_rows(lay, block, first_step):
    along, across = first_step
    chain = [block, along]
    for _ in range(lay.line - 2):
        chain.append(lax.ppermute(chain[-1], "shard", lay.step(1)))
    plane = [block, across]
    for piece in chain[1:]:
        plane += [piece, lax.ppermute(piece, "shard", lay.xor(2))]
    near, far = (
        jnp.concatenate(plane[i : i + lay.line], axis=0) for i in range(0, 2 * lay.line, lay.line)
    )
    return near, far, *(lax.ppermute(half, "shard", lay.xor(1)) for half in (near, far))


def scatter_planes(lay, quarters, length):
    near, far, other_near, other_far = quarters
    kept, sent = {}, {}
    for base, own, other in ((lay.line // 2, far, other_far), (0, near, other_near)):
        came = lax.ppermute(other, "shard", lay.xor(1))
        for d in range(lay.line // 2 - 1, -1, -1):
            at = slice(2 * d * length, (2 * d + 1) * length)
            to = slice((2 * d + 1) * length, (2 * d + 2) * length)
            kept[base + d] = own[at].astype(f32) + came[at].astype(f32)
            sent[base + d] = lax.ppermute(
                (own[to].astype(f32) + came[to].astype(f32)).astype(bf16), "shard", lay.xor(2)
            )
    return kept, sent


def scatter_step(lay, total, kept, sent, d):
    mine = kept[d] + sent[d].astype(f32)
    if total is None:
        return mine
    return mine + lax.ppermute(total.astype(bf16), "shard", lay.step(-1)).astype(f32)


def exchange(lay, parts):
    groups = [list(range(p * lay.ways, (p + 1) * lay.ways)) for p in range(lay.packs)]
    return lax.all_to_all(
        parts, "shard", 0, 0, axis_index_groups=groups if lay.packs > 1 else None, tiled=True
    )


LANES = 128
SUB = D // LANES
TILE = 256
VMEM_LIMIT = 56 * 1024 * 1024


def spread_matrix():
    row = lax.broadcasted_iota(jnp.int32, (D, D), 0)
    col = lax.broadcasted_iota(jnp.int32, (D, D), 1)
    return jnp.where(row == (col % HD) * HEADS + col // HD, 1.0, 0.0).astype(bf16)


def unit_masks(first_unit, amount):
    unit = lax.broadcasted_iota(jnp.int32, (amount, LANES), 0) // SUB + first_unit
    is_up = (unit >= OUT_END // UNIT) & (unit < UP_END // UNIT)
    by_row = ((unit >= QKV_END // UNIT) & (unit < OUT_END // UNIT)) | (unit >= UP_END // UNIT)
    return is_up, by_row


def pack_kernel(info_ref, first_ref, second_ref, out_ref, x_ref):
    rows = first_ref.shape[0]
    amount = rows // UNIT
    ids = lax.broadcasted_iota(jnp.int32, (rows, LANES), 0)
    x_ref[...] = jnp.where(
        ids < info_ref[0], first_ref[...].astype(f32), second_ref[...].astype(f32)
    )
    is_up, by_row = unit_masks(info_ref[1], amount)
    low = lax.broadcasted_iota(jnp.int32, (amount, LANES), 1) < HD
    spread = spread_matrix()
    halves = []
    for p in range(2):
        cols = [x_ref[pl.ds(SUB * p + a, amount, stride=UNIT), :] for a in range(SUB)]
        moved = jnp.dot(
            jnp.concatenate(cols, axis=1).astype(bf16), spread, preferred_element_type=f32
        )
        halves.append(
            [
                jnp.where(is_up, moved[:, a * LANES : (a + 1) * LANES], cols[a])
                for a in range(SUB)
            ]
        )
    whole = x_ref[...].reshape(amount // SUB, UNIT, SUB, LANES)
    for t in range(HEADS):
        zero, one = halves[0][t // 2], halves[1][t // 2]
        if t % 2 == 0:
            piece = jnp.where(low, zero, pltpu.roll(one, HD, 1))
        else:
            piece = jnp.where(low, pltpu.roll(zero, HD, 1), one)
        direct = whole[:, t].reshape(amount, LANES)
        out_ref[t] = jnp.where(by_row, direct, piece).astype(bf16)


def pack(first, second, bound, first_unit):
    rows = first.shape[0]
    return pl.pallas_call(
        pack_kernel,
        out_shape=jax.ShapeDtypeStruct((HEADS, rows // UNIT, LANES), bf16),
        in_specs=[
            pl.BlockSpec(memory_space=pltpu.SMEM),
            pl.BlockSpec(memory_space=pltpu.VMEM),
            pl.BlockSpec(memory_space=pltpu.VMEM),
        ],
        out_specs=pl.BlockSpec(memory_space=pltpu.VMEM),
        scratch_shapes=[pltpu.VMEM((rows, LANES), f32)],
        compiler_params=pltpu.CompilerParams(vmem_limit_bytes=VMEM_LIMIT),
        cost_estimate=pl.CostEstimate(
            flops=2 * rows * LANES * D, bytes_accessed=6 * rows * LANES, transcendentals=0
        ),
        name="pack",
    )(jnp.stack([bound, first_unit]).astype(jnp.int32), first, second)


MARGIN = 64


def unpack_kernel(info_ref, got_ref, out_ref, x_ref):
    amount = got_ref.shape[1]
    rows = amount * UNIT
    is_up, by_row = unit_masks(info_ref[0], amount)
    low = lax.broadcasted_iota(jnp.int32, (amount, LANES), 1) < HD
    spread = spread_matrix()
    x_ref[pl.ds(0, MARGIN), :] = jnp.zeros((MARGIN, LANES), f32)
    x_ref[pl.ds(MARGIN + rows, MARGIN), :] = jnp.zeros((MARGIN, LANES), f32)
    for p in range(2):
        cols = []
        for a in range(SUB):
            even, odd = got_ref[2 * a].astype(f32), got_ref[2 * a + 1].astype(f32)
            if p == 0:
                cols.append(jnp.where(low, even, pltpu.roll(odd, HD, 1)))
            else:
                cols.append(jnp.where(low, pltpu.roll(even, HD, 1), odd))
        moved = lax.dot_general(
            jnp.concatenate(cols, axis=1).astype(bf16),
            spread,
            (((1,), (1,)), ((), ())),
            preferred_element_type=f32,
        )
        for a in range(SUB):
            x_ref[pl.ds(MARGIN + SUB * p + a, amount, stride=UNIT), :] = jnp.where(
                is_up, moved[:, a * LANES : (a + 1) * LANES], cols[a]
            )
    whole = x_ref[pl.ds(MARGIN, rows), :].reshape(amount // SUB, UNIT, SUB, LANES)
    keep = by_row.reshape(amount // SUB, SUB, LANES)
    mixed = [
        jnp.where(keep, got_ref[t].astype(f32).reshape(amount // SUB, SUB, LANES), whole[:, t])
        for t in range(HEADS)
    ]
    x_ref[pl.ds(MARGIN, rows), :] = jnp.stack(mixed, axis=1).reshape(rows, LANES)
    size = out_ref.shape[0]
    low = lax.broadcasted_iota(jnp.int32, (size, LANES), 1) < HD

    def cut(start):
        base = start // 2
        here = x_ref[pl.ds(base, size), :]
        after = x_ref[pl.ds(base + 1, size), :]
        split = jnp.where(low, pltpu.roll(here, HD, 1), pltpu.roll(after, HD, 1))
        return jnp.where(start % 2 == 1, split, here)

    place = 2 * lax.broadcasted_iota(jnp.int32, (size, LANES), 0) + jnp.where(low, 0, 1)
    first = cut(info_ref[1])
    out_ref[...] = first
    out_ref[...] = jnp.where(place < info_ref[3], out_ref[...], cut(info_ref[2]))


def unpack(got, first_unit, start_one, start_two, bound, size):
    amount = got.shape[1]
    out_rows = -(-size // (SUB * LANES)) * SUB
    info = jnp.stack([first_unit, start_one // HD, start_two // HD, bound // HD])
    return pl.pallas_call(
        unpack_kernel,
        out_shape=jax.ShapeDtypeStruct((out_rows, LANES), f32),
        in_specs=[
            pl.BlockSpec(memory_space=pltpu.SMEM),
            pl.BlockSpec(memory_space=pltpu.VMEM),
        ],
        out_specs=pl.BlockSpec(memory_space=pltpu.VMEM),
        scratch_shapes=[pltpu.VMEM((amount * UNIT + 2 * MARGIN, LANES), f32)],
        compiler_params=pltpu.CompilerParams(vmem_limit_bytes=VMEM_LIMIT),
        cost_estimate=pl.CostEstimate(
            flops=2 * amount * UNIT * LANES * D, bytes_accessed=6 * amount * UNIT * LANES, transcendentals=0
        ),
        name="unpack",
    )(info.astype(jnp.int32), got)


def nt(a, b):
    return lax.dot_general(a, b, (((1,), (1,)), ((), ())), preferred_element_type=f32)


def tn(a, b):
    return lax.dot_general(a, b, (((0,), (0,)), ((), ())), preferred_element_type=f32)


def nn(a, b):
    return lax.dot_general(a, b, (((1,), (0,)), ((), ())), preferred_element_type=f32)


QUARTERS = 4


def pick_tile(refs):
    quarter = pl.program_id(0) // (pl.num_programs(0) // QUARTERS)
    value = refs[0][...]
    for q in range(1, QUARTERS):
        value = jnp.where(quarter == q, refs[q][...], value)
    return value


def start_tile(refs):
    both = pick_tile(refs)
    x = both[:, :D].astype(f32)
    center = x - jnp.mean(x, axis=1, keepdims=True)
    inverse = lax.rsqrt(jnp.mean(center * center, axis=1, keepdims=True) + norm_eps)
    return center * inverse, both[:, D:]


def store_tile(refs, col, value):
    quarter = pl.program_id(0) // (pl.num_programs(0) // QUARTERS)
    for q in range(QUARTERS):

        @pl.when(quarter == q)
        def _():
            refs[q][:, col : col + D] = value


def feed_kernel(*refs):
    rows_refs, sums_refs = refs[:4], refs[8:12]
    w_up_ref, w_down_ref, bias_ref, vec_ref = refs[4:8]
    gup_ref, gdown_ref, gbias_ref, gvec_ref, aup, adown = refs[12:]
    step = pl.program_id(0)

    @pl.when(step == 0)
    def _():
        for ref in (aup, adown, gbias_ref, gvec_ref):
            ref[...] = jnp.zeros(ref.shape, ref.dtype)

    hat, go = start_tile(rows_refs)
    gain, shift = vec_ref[3:4, :], vec_ref[4:5, :]
    rows_in = (hat * gain + shift).astype(bf16)
    hidden = nn(rows_in, w_up_ref[...]) + bias_ref[1:2, :]
    cdf = 0.5 * (1.0 + lax.erf(hidden * root_half))
    active = (hidden * cdf).astype(bf16)
    slope = cdf + hidden * jnp.exp(-0.5 * hidden * hidden) * inv_root_twopi
    ghid = nt(go, w_down_ref[...]) * slope
    ghid_bf = ghid.astype(bf16)
    store_tile(sums_refs, 0, nn(active, w_down_ref[...]).astype(bf16))
    norm = nt(ghid_bf, w_up_ref[...])
    store_tile(sums_refs, D, (norm * gain).astype(bf16))
    gvec_ref[0:1, :] += jnp.sum(norm * hat, axis=0, keepdims=True)
    gvec_ref[1:2, :] += jnp.sum(norm, axis=0, keepdims=True)
    gvec_ref[2:3, :] += jnp.sum(go.astype(f32), axis=0, keepdims=True)
    gbias_ref[0:1, :] += jnp.sum(ghid, axis=0, keepdims=True)
    aup[...] += tn(rows_in, ghid_bf)
    adown[...] += tn(active, go)

    @pl.when(step == pl.num_programs(0) - 1)
    def _():
        gup_ref[...] = aup[...].astype(bf16)
        gdown_ref[...] = adown[...].astype(bf16)


def heads_kernel(*refs):
    rows_refs, part_refs, sums_refs = refs[:4], refs[4:8], refs[14:18]
    seg_ref, table_ref, w_qkv_ref, w_out_ref, bias_ref, vec_ref = refs[8:14]
    gqkv_ref, gout_ref, gbias_ref, gvec_ref, aqkv, aout = refs[18:]
    step = pl.program_id(0)

    @pl.when(step == 0)
    def _():
        for ref in (aqkv, aout, gbias_ref, gvec_ref):
            ref[...] = jnp.zeros(ref.shape, ref.dtype)

    length = seg_ref.shape[1]
    wide = 2 * LANES
    hat, go = start_tile(rows_refs)
    gain, shift = vec_ref[1:2, :], vec_ref[2:3, :]
    rows_in = (hat * gain + shift).astype(bf16)
    low_rot = lax.broadcasted_iota(jnp.int32, (TILE, wide), 1) % HD < ROT // 2
    low = lax.broadcasted_iota(jnp.int32, (length, LANES), 1) < HD
    row_id = lax.broadcasted_iota(jnp.int32, (length, length), 0)
    col_id = lax.broadcasted_iota(jnp.int32, (length, length), 1)
    spot = lax.broadcasted_iota(jnp.int32, (length, wide), 1).astype(f32)
    rows_f = lax.broadcasted_iota(jnp.int32, (length, 1), 0).astype(f32)

    masks, picks = [], []
    for b in range(TILE // length):
        seg_row = seg_ref[pl.ds(step * (TILE // length) + b, 1), :]
        seg_col = jnp.sum(jnp.where(row_id == col_id, seg_row, 0.0), axis=1, keepdims=True)
        masks.append(jnp.where((seg_col == seg_row) & (col_id <= row_id), 0.0, -1e30))
        picks.append(jnp.where(spot == rows_f - seg_col, 1.0, 0.0).astype(bf16))
    pick = jnp.concatenate(picks, axis=0)
    cosine = nn(pick, table_ref[0]) + nn(pick, table_ref[1])
    sine = nn(pick, table_ref[2]) + nn(pick, table_ref[3])

    def swap(v):
        ahead = pltpu.roll(v, wide - ROT // 2, 1)
        return jnp.where(low_rot, ahead, pltpu.roll(v, ROT // 2, 1))

    mixed = nn(rows_in, w_qkv_ref[...]) + bias_ref[0:1, :]
    rot = mixed * cosine + swap(mixed) * sine
    gheads = nt(go, w_out_ref[...]).astype(bf16)
    scale = HD ** (-0.5)
    heads, gmix = [], []
    for b in range(TILE // length):
        part = slice(b * length, (b + 1) * length)
        qk = rot[part, :LANES]
        vv = rot[part, LANES:].astype(bf16)
        turned = pltpu.roll(qk, HD, 1)
        q_low = jnp.where(low, qk, 0.0).astype(bf16)
        k_low = jnp.where(low, turned, 0.0).astype(bf16)
        q_high = jnp.where(low, 0.0, turned).astype(bf16)
        gh = gheads[part]
        scores = nt(q_low, k_low) * scale + masks[b]
        expd = jnp.exp(scores - jnp.max(scores, axis=1, keepdims=True))
        probs = expd / jnp.sum(expd, axis=1, keepdims=True)
        probs_bf = probs.astype(bf16)
        head = nn(probs_bf, vv).astype(bf16)
        heads.append(head)
        delta = jnp.sum(gh.astype(f32) * head.astype(f32), axis=1, keepdims=True)
        gs = (probs * (nt(gh, vv) - delta) * scale).astype(bf16)
        gqk = nn(gs, k_low) + tn(gs, q_high)
        gv = tn(probs_bf, gh)
        gmix.append(jnp.concatenate([gqk, gv], axis=1))
    head = jnp.concatenate(heads, axis=0)
    gmix = jnp.concatenate(gmix, axis=0)
    gmix = gmix * cosine - swap(gmix) * sine
    gmix_bf = gmix.astype(bf16)

    part = pick_tile(part_refs).astype(f32)
    store_tile(sums_refs, 0, (nn(head, w_out_ref[...]) + part[:, :D]).astype(bf16))
    norm = nt(gmix_bf, w_qkv_ref[...])
    store_tile(sums_refs, D, (norm * gain + part[:, D:]).astype(bf16))
    gvec_ref[0:1, :] += jnp.sum(norm * hat, axis=0, keepdims=True)
    gvec_ref[1:2, :] += jnp.sum(norm, axis=0, keepdims=True)
    gbias_ref[0:1, :] += jnp.sum(gmix, axis=0, keepdims=True)
    aqkv[...] += tn(rows_in, gmix_bf)
    aout[...] += tn(head, go)

    @pl.when(step == pl.num_programs(0) - 1)
    def _():
        gqkv_ref[...] = aqkv[...].astype(bf16)
        gout_ref[...] = aout[...].astype(bf16)


def quarter_tiles(width, count):
    def spec(q):
        return pl.BlockSpec((TILE, width), lambda i: (jnp.clip(i - q * count, 0, count - 1), 0))

    return [spec(q) for q in range(QUARTERS)]


def whole(*shape):
    return pl.BlockSpec(shape, lambda i: (0,) * len(shape))


def feed(rows, w_up, w_down, bias, vec):
    count = rows[0].shape[0] // TILE
    cols = FF // HEADS
    sums = jax.ShapeDtypeStruct(rows[0].shape, bf16)
    return pl.pallas_call(
        feed_kernel,
        grid=(QUARTERS * count,),
        in_specs=[
            *quarter_tiles(2 * D, count),
            whole(D, cols),
            whole(cols, D),
            whole(8, cols),
            whole(8, D),
        ],
        out_specs=[
            *quarter_tiles(2 * D, count),
            whole(D, cols),
            whole(cols, D),
            whole(8, cols),
            whole(8, D),
        ],
        out_shape=[
            *[sums] * QUARTERS,
            jax.ShapeDtypeStruct((D, cols), bf16),
            jax.ShapeDtypeStruct((cols, D), bf16),
            jax.ShapeDtypeStruct((8, cols), f32),
            jax.ShapeDtypeStruct((8, D), f32),
        ],
        scratch_shapes=[pltpu.VMEM((D, cols), f32), pltpu.VMEM((cols, D), f32)],
        compiler_params=pltpu.CompilerParams(vmem_limit_bytes=VMEM_LIMIT),
        cost_estimate=pl.CostEstimate(
            flops=12 * QUARTERS * rows[0].shape[0] * D * FF // HEADS, bytes_accessed=4 * QUARTERS * rows[0].size, transcendentals=0
        ),
        name="feed",
    )(*rows, w_up, w_down, bias, vec)


def attend(rows, parts, seg, table, w_qkv, w_out, bias, vec):
    count = rows[0].shape[0] // TILE
    wide = 2 * LANES
    sums = jax.ShapeDtypeStruct(rows[0].shape, bf16)
    return pl.pallas_call(
        heads_kernel,
        grid=(QUARTERS * count,),
        in_specs=[
            *quarter_tiles(2 * D, count),
            *quarter_tiles(2 * D, count),
            whole(*seg.shape),
            whole(*table.shape),
            whole(D, wide),
            whole(LANES, D),
            whole(8, wide),
            whole(8, D),
        ],
        out_specs=[
            *quarter_tiles(2 * D, count),
            whole(D, wide),
            whole(LANES, D),
            whole(8, wide),
            whole(8, D),
        ],
        out_shape=[
            *[sums] * QUARTERS,
            jax.ShapeDtypeStruct((D, wide), bf16),
            jax.ShapeDtypeStruct((LANES, D), bf16),
            jax.ShapeDtypeStruct((8, wide), f32),
            jax.ShapeDtypeStruct((8, D), f32),
        ],
        scratch_shapes=[pltpu.VMEM((D, wide), f32), pltpu.VMEM((LANES, D), f32)],
        compiler_params=pltpu.CompilerParams(vmem_limit_bytes=VMEM_LIMIT),
        cost_estimate=pl.CostEstimate(
            flops=12 * QUARTERS * rows[0].shape[0] * D * 4 * HD, bytes_accessed=6 * QUARTERS * rows[0].size, transcendentals=0
        ),
        name="attend",
    )(*rows, *parts, seg, table, w_qkv, w_out, bias, vec)


def turn_table():
    wide = 2 * LANES
    lane = jnp.arange(wide)
    inner = lane % HD
    turns = (inner < ROT) & (lane < 2 * HD)
    frequency = 10000.0 ** (-2.0 * (lane % (ROT // 2)).astype(f32) / ROT)
    phase = jnp.arange(wide, dtype=f32)[:, None] * frequency[None]
    cosine = jnp.where(turns, jnp.cos(phase), 1.0)
    sine = jnp.where(turns, jnp.where(inner < ROT // 2, -1.0, 1.0) * jnp.sin(phase), 0.0)
    out = []
    for values in (cosine, sine):
        top = lax.reduce_precision(values, 8, 7)
        out += [top.astype(bf16), (values - top).astype(bf16)]
    return jnp.stack(out)


def split_params(lay, params, segment, shard_id, first_step):
    table = jnp.asarray(lay.tables)[shard_id]
    rows = (lay.units + 1) * UNIT
    chunk = params.astype(bf16)
    padded = jnp.pad(chunk, (PAD, rows * D + 2 * PAD - chunk.shape[0]))
    first = lax.dynamic_slice(padded, (PAD - table[0],), (rows * D,)).reshape(rows * SUB, LANES)
    second = lax.dynamic_slice(padded, (PAD - table[1],), (rows * D,)).reshape(rows * SUB, LANES)
    body = pack(first, second, table[2] * SUB, shard_id * lay.units)
    size = chunk.shape[0]
    vec = []
    for flat_row, amount, _ in RUNS:
        start = flat_row * D - shard_id * size
        begin = jnp.clip(start, -PAD, size)
        piece = lax.dynamic_slice(padded, (PAD + begin,), (amount * D,))
        vec.append(jnp.where(start == begin, piece, 0).reshape(amount, D))
    qkv_cols = vec[0].reshape(3, HEADS, HD).transpose(1, 0, 2).reshape(HEADS, 3 * HD)
    up_cols = vec[2].reshape(FF // HEADS, HEADS).T
    used = qkv_cols.shape[1] + up_cols.shape[1]
    mixed_row = jnp.concatenate([qkv_cols, up_cols, jnp.zeros((HEADS, D - used), bf16)], axis=1)
    mixed_row = mixed_row[:, None]
    full = jnp.concatenate(
        [vec[1] + vec[3][:1], vec[3][1:], jnp.zeros((lay.slots - lay.units - 7, D), bf16)], axis=0
    )
    full = jnp.broadcast_to(full[None], (HEADS,) + full.shape)
    tail = jnp.concatenate([mixed_row, full], axis=1).reshape(HEADS, -1, LANES)
    seg_row = jnp.pad(segment.astype(bf16), (0, D - segment.shape[0]))
    seg_row = jnp.broadcast_to(seg_row.reshape(1, SUB, LANES), (HEADS, SUB, LANES))
    parts, rows = lax.optimization_barrier(
        (jnp.concatenate([body, tail, seg_row], axis=1), first_step)
    )
    got = exchange(lay, parts)
    got = got.reshape(lay.ways, lay.slots + 1, SUB, LANES)
    seg_all = got[:, lay.slots, 0].astype(f32)
    if lay.packs > 1:
        packs = [got] + [
            lax.ppermute(got, "shard", lay.xor(lay.ways * k)) for k in range(1, lay.packs)
        ]
        order = jnp.arange(lay.packs, dtype=jnp.int32) ^ (shard_id // lay.ways)
        got = jnp.take(jnp.stack(packs), order, axis=0)
        got = got.reshape(lay.n, lay.slots + 1, SUB, LANES)
    carry = got[:-1, lay.units : lay.units + 1]
    carry = jnp.concatenate([jnp.zeros_like(carry[:1]), carry], axis=0)
    units = jnp.concatenate([got[:, :1] + carry, got[:, 1 : lay.units]], axis=1)
    units = units.reshape(MAT_ROWS // UNIT, SUB, LANES)
    w_qkv = units[: QKV_END // UNIT].reshape(D, 3 * HD)
    w_up = units[OUT_END // UNIT : UP_END // UNIT].reshape(D, FF // HEADS)
    w_down = units[UP_END // UNIT :].reshape(FF // HEADS, D)
    out_rows = units[QKV_END // UNIT : OUT_END // UNIT]
    w_out = exchange(lay, out_rows.reshape(HEADS, HD // HEADS, D))
    w_out = w_out.transpose(1, 0, 2).reshape(HD, D)
    extra = jnp.sum(got[:, lay.units + 1 : lay.units + 7].astype(f32), axis=0).reshape(6, D)
    b_qkv = extra[0, : 3 * HD]
    b_up = extra[0, 3 * HD : 3 * HD + FF // HEADS]
    return w_qkv, b_qkv, w_out, w_up, b_up, w_down, extra[1:], seg_all, rows


def share_sum(lay, parts, rep_id):
    by_rep = parts.reshape(parts.shape[0], lay.reps, lay.share, D)
    total = lax.dynamic_index_in_dim(by_rep, rep_id, axis=1, keepdims=False).astype(f32)
    for k in range(1, lay.reps):
        theirs = lax.dynamic_index_in_dim(by_rep, rep_id ^ k, axis=1, keepdims=False)
        total = total + lax.ppermute(theirs, "rep", lay.rep_xor(k)).astype(f32)
    return total.astype(bf16)


def windows(lay, units, first, last):
    body = units[: (last - first) * lay.units].reshape(last - first, lay.units, D)
    after = units[lay.units :: lay.units][: last - first, None]
    short = last - first - after.shape[0]
    after = jnp.pad(after, ((0, short), (0, 0), (0, 0)))
    room = jnp.zeros((last - first, lay.slots - lay.units - 1, D), bf16)
    return jnp.concatenate([body, after, room], axis=1)


def own_share(lay, late, early, mixed_row, full, shard_id, rep_id):
    total = jnp.concatenate([late, early], axis=0)
    tail = jnp.concatenate([mixed_row[None], full], axis=0)
    for k in [2**i for i in range((lay.reps - 1).bit_length())]:
        tail = tail + lax.ppermute(tail.astype(bf16), "rep", lay.rep_xor(k)).astype(f32)
    tail = jnp.pad(tail, ((lay.units + 1, lay.slots - lay.units - 7), (0, 0))).astype(bf16)
    tail = lax.dynamic_slice_in_dim(tail, rep_id * lay.share, lay.share, axis=0)
    total = total + tail[None]
    if lay.packs > 1:
        pack_id = shard_id // lay.ways
        by_pack = total.reshape(lay.packs, lay.ways, lay.share, D)
        total = lax.dynamic_index_in_dim(by_pack, pack_id, keepdims=False).astype(f32)
        for k in range(1, lay.packs):
            theirs = lax.dynamic_index_in_dim(by_pack, pack_id ^ k, keepdims=False)
            total = total + lax.ppermute(theirs, "shard", lay.xor(lay.ways * k)).astype(f32)
        total = total.astype(bf16)
    return total


def all_shares(lay, got, rep_id):
    got = [got] + [lax.ppermute(got, "rep", lay.rep_xor(k)) for k in range(1, lay.reps)]
    if lay.reps == 2:
        got = [jnp.where(rep_id == r, got[0], got[1]) for r in range(2)]
        return jnp.concatenate(got, axis=1)
    got = jnp.take(jnp.stack(got), jnp.arange(lay.reps, dtype=jnp.int32) ^ rep_id, axis=0)
    return got.transpose(1, 0, 2, 3).reshape(lay.ways, lay.slots, D)


def owner_part(lay, got, shard_id):
    body = got[:, : lay.units + 1].reshape(lay.ways, -1, LANES)
    extra = got[:, lay.units + 1 : lay.units + 7].astype(f32)
    qkv_vec = extra[:, 0, : 3 * HD].reshape(HEADS, 3, HD).transpose(1, 0, 2).reshape(3 * D)
    up_vec = extra[:, 0, 3 * HD : 3 * HD + FF // HEADS].T.reshape(FF)
    norm_vec = jnp.sum(extra[:, 1:5], axis=0).reshape(4 * D)
    out_vec = extra[0, 5]
    small = jnp.concatenate([qkv_vec, out_vec, up_vec, out_vec, norm_vec])
    table = jnp.asarray(lay.tables)[shard_id]
    size = (MAT_ROWS + VEC_ROWS) * D // lay.n
    flat = unpack(
        body, shard_id * lay.units, PAD + table[0], PAD + table[1], table[3], size
    )
    flat = flat.reshape(-1)[:size]
    run = 5 * D
    start = jnp.clip(table[3], 0, size - run)
    ids = start + lax.iota(jnp.int32, run)
    from_small = jnp.clip(start - table[5], -run, VEC_ROWS * D) + run
    vec = lax.dynamic_slice(jnp.pad(small, (run, run)), (from_small,), (run,))
    old = lax.dynamic_slice(flat, (start,), (run,))
    new = jnp.where((ids >= table[3]) & (ids < table[4]), vec, old)
    return lax.dynamic_update_slice(flat, new, (start,))


def per_device(lay, tokens, cotangent, segment, params, first_moment, second_moment):
    shard_id = lax.axis_index("shard")
    rep_id = lax.axis_index("rep")
    me = shard_id % lay.ways
    length = tokens.shape[0]
    blocks = lay.ways

    own_grad = jnp.where((segment >= 0)[:, None], cotangent, jnp.zeros_like(cotangent))
    block = jnp.concatenate([tokens, own_grad], axis=1)
    first_step = (
        lax.ppermute(block, "shard", lay.step(1)),
        lax.ppermute(block, "shard", lay.xor(2)),
    )
    w_qkv, b_qkv, w_out, w_up, b_up, w_down, full, seg_all, first_step = split_params(
        lay, params, segment, shard_id, first_step
    )
    rows = gather_rows(lay, block, first_step)
    b_sum, _, _, _, _ = (full[i] for i in range(5))
    spot = jnp.arange(blocks, dtype=jnp.int32)
    d_core, d_line, d_row = spot // (2 * lay.line), spot // 2 % lay.line, spot % 2
    source = (
        (me // 4 - d_line) % lay.line * 4 + ((me // 2 % 2) ^ d_row) * 2 + ((me % 2) ^ d_core)
    )
    seg = jnp.take(seg_all, source, axis=0)

    bias = jnp.pad(jnp.stack([jnp.pad(b_qkv, (0, HD)), b_up]), ((0, 6), (0, 0)))
    vec = jnp.pad(full, ((0, 8 - full.shape[0]), (0, 0)))
    *parts, grad_w_up, grad_w_down, up_sums, feed_sums = feed(rows, w_up, w_down, bias, vec)
    cut = -(-OUT_END // UNIT // lay.units)
    units_feed = jnp.concatenate([grad_w_up.reshape(FF // UNIT, D), grad_w_down], axis=0)
    early = windows(lay, units_feed[cut * lay.units - OUT_END // UNIT :], cut, lay.n)
    early = share_sum(lay, early, rep_id)
    *sums, grad_qkv, grad_w_out, qkv_sums, heads_sums = attend(
        rows,
        parts,
        seg,
        turn_table(),
        jnp.pad(w_qkv, ((0, 0), (0, HD))),
        jnp.pad(w_out, ((0, LANES - HD), (0, 0))),
        bias,
        vec,
    )
    own = tokens.astype(f32)
    own_center = own - jnp.mean(own, axis=-1, keepdims=True)
    own_inverse = lax.rsqrt(jnp.mean(own_center * own_center, axis=-1, keepdims=True) + norm_eps)
    own_hat = own_center * own_inverse
    grad_w_qkv = grad_qkv[:, : 3 * HD]
    back = grad_w_out[:HD].reshape(HD // HEADS, HEADS, D).transpose(1, 0, 2)
    back = exchange(lay, back).reshape(HD, D)
    units = jnp.concatenate(
        [grad_w_qkv.reshape(QKV_END // UNIT, D), back, units_feed[: (cut + 1) * lay.units]], axis=0
    )
    late = windows(lay, units[: cut * lay.units + 1], 0, cut)
    late = share_sum(lay, late, rep_id)
    used = 3 * HD + FF // HEADS
    mixed_row = jnp.concatenate([qkv_sums[0, : 3 * HD], up_sums[0], jnp.zeros((D - used,), f32)])
    vectors = jnp.concatenate([heads_sums[:2], feed_sums[:3]], axis=0)
    share = own_share(lay, late, early, mixed_row, vectors, shard_id, rep_id)

    kept, sent = scatter_planes(lay, sums, length)
    top = lay.line - 1
    share, sent[top] = lax.optimization_barrier((share, sent[top]))
    got = exchange(lay, share)
    total = scatter_step(lay, None, kept, sent, top)
    total = scatter_step(lay, total, kept, sent, top - 1)
    got, total = lax.optimization_barrier((got, total))
    got = all_shares(lay, got, rep_id)
    for d in range(top - 2, 0, -1):
        total = scatter_step(lay, total, kept, sent, d)
    got, total = lax.optimization_barrier((got, total))
    grad_total = owner_part(lay, got, shard_id)
    sums = scatter_step(lay, total, kept, sent, 0)
    out_sum, g_sum = sums[:, :D], sums[:, D:]
    out_rows = (tokens.astype(f32) + out_sum + b_sum).astype(bf16)
    grad_rows = (
        own_grad.astype(f32)
        + own_inverse
        * (
            g_sum
            - jnp.mean(g_sum, axis=-1, keepdims=True)
            - own_hat * jnp.mean(g_sum * own_hat, axis=-1, keepdims=True)
        )
    ).astype(bf16)

    new_weights, first_new, second_new = adam_update(
        params, first_moment, second_moment, grad_total
    )
    return (out_rows, grad_rows, grad_total, new_weights, first_new, second_new)


def solution(mesh):
    lay = Layout(mesh)
    in_specs = (
        P(("rep", "shard"), None),
        P(("rep", "shard"), None),
        P(("rep", "shard")),
        P("shard"),
        P("shard"),
        P("shard"),
    )
    out_specs = (
        P(("rep", "shard"), None),
        P(("rep", "shard"), None),
        P("shard"),
        P("shard"),
        P("shard"),
        P("shard"),
    )

    def body(*args):
        return per_device(lay, *args)

    return jax.shard_map(body, mesh=mesh, in_specs=in_specs, out_specs=out_specs, check_vma=False)
```

```python
import math

import jax
import jax.numpy as jnp
import numpy as np
from jax import lax
from jax.experimental import pallas as pl
from jax.experimental.pallas import tpu as pltpu
from jax.sharding import PartitionSpec as P

D = 1024
HEADS = 16
HD = 64
ROT = 16
FF = 4096
STEP = 4
UNIT = HEADS

norm_eps = 1e-05
adam_eps = 1e-08
beta_one = 0.9
beta_two = 0.999
learn_rate = 0.003
decay_rate = 0.1
root_half = 0.7071067811865476
inv_root_twopi = 0.3989422804014327


QKV_END = 3 * D
OUT_END = QKV_END + D
UP_END = OUT_END + FF
DOWN_END = UP_END + FF
MAT_ROWS = DOWN_END
SECTIONS = ((0, QKV_END, 0), (QKV_END, OUT_END, 3), (OUT_END, UP_END, 4), (UP_END, DOWN_END, 8))
RUNS = (
    (QKV_END, 3, 0),
    (OUT_END + 3, 1, 3),
    (UP_END + 4, 4, 4),
    (DOWN_END + 8, 5, 8),
)
VEC_ROWS = 13
PAD = 8 * D

f32 = jnp.float32
bf16 = jnp.bfloat16


def owner_tables(owners):
    total = (MAT_ROWS + VEC_ROWS) * D
    part = total // owners
    lead = VEC_ROWS * D // owners
    rows = []
    for s in range(owners):
        start, end = s * part, (s + 1) * part
        first = next((i for i, (a, b, v) in enumerate(SECTIONS) if (b + v) * D > start), 3)
        second = min(first + 1, 3)
        run_row, run_len, vec_row = RUNS[first]
        run_a = min(max(run_row * D - start, 0), part)
        run_b = min(max((run_row + run_len) * D - start, 0), part)
        rows.append(
            (
                lead * s - SECTIONS[first][2] * D,
                lead * s - SECTIONS[second][2] * D,
                (SECTIONS[first][1] - (MAT_ROWS // owners) * s) if first < 3 else 2 * MAT_ROWS,
                run_a,
                run_b,
                run_row * D - start - vec_row * D,
            )
        )
    return np.array(rows, np.int32)


def rotate(values, cosine, sine_part):
    half_rot = ROT // 2
    lower_half = values[..., :half_rot]
    upper_half = values[..., half_rot:ROT]
    return jnp.concatenate(
        [
            lower_half * cosine - upper_half * sine_part,
            upper_half * cosine + lower_half * sine_part,
            values[..., ROT:],
        ],
        axis=-1,
    )


def gelu_parts(values):
    cdf = 0.5 * (1.0 + lax.erf(values * root_half))
    return values * cdf, cdf + values * jnp.exp(-0.5 * values * values) * inv_root_twopi


def adam_update(weights, moment_one, moment_two, grad_total):
    first_new = beta_one * moment_one + (1.0 - beta_one) * grad_total
    second_new = beta_two * moment_two + (1.0 - beta_two) * grad_total * grad_total
    correct_one = 1.0 - beta_one**STEP
    correct_two = 1.0 - beta_two**STEP
    change = first_new / correct_one / (jnp.sqrt(second_new / correct_two) + adam_eps)
    return (weights - learn_rate * (change + decay_rate * weights), first_new, second_new)


def bmm(spec, a, b):
    return jnp.einsum(spec, a, b, preferred_element_type=f32)


class Layout:
    def __init__(self, mesh):
        self.n = mesh.shape["shard"]
        self.reps = mesh.shape["rep"]
        self.ways = HEADS
        assert self.n % self.ways == 0
        self.packs = self.n // self.ways
        self.core, self.row = 2, 2
        self.line = self.ways // 4
        self.units = MAT_ROWS // UNIT // self.n
        slots = self.units + 1 + 1 + 5
        self.slots = -(-slots // self.reps) * self.reps
        self.share = self.slots // self.reps
        self.tables = owner_tables(self.n)

    def xor(self, k):
        return [(i, i ^ k) for i in range(self.n)]

    def step(self, k):
        w = self.ways
        return [(i, i - i % w + (i % w + 4 * k) % w) for i in range(self.n)]

    def rep_xor(self, k):
        return [(i, i ^ k) for i in range(self.reps)]


def gather_start(lay, block):
    along = lax.ppermute(block, "shard", lay.step(1))
    return along, lax.ppermute(block, "shard", lay.xor(2))


def gather_line(lay, block, start):
    chain, across = [block, start[0]], [start[1]]
    while len(chain) < lay.line:
        chain.append(lax.ppermute(chain[-1], "shard", lay.step(1)))
        across.append(lax.ppermute(chain[len(across)], "shard", lay.xor(2)))
    return chain, across


def gather_end(lay, chain, across):
    across = across + [lax.ppermute(chain[-1], "shard", lay.xor(2))]
    plane = [piece for pair in zip(chain, across) for piece in pair]
    near, far = (
        jnp.concatenate(plane[i : i + lay.line], axis=0) for i in range(0, 2 * lay.line, lay.line)
    )
    return near, far, *(lax.ppermute(half, "shard", lay.xor(1)) for half in (near, far))


def scatter_planes(lay, quarters, length):
    near, far, other_near, other_far = quarters
    kept, sent = {}, {}
    for base, own, other in ((lay.line // 2, far, other_far), (0, near, other_near)):
        came = lax.ppermute(other, "shard", lay.xor(1))
        for d in range(lay.line // 2 - 1, -1, -1):
            at = slice(2 * d * length, (2 * d + 1) * length)
            to = slice((2 * d + 1) * length, (2 * d + 2) * length)
            kept[base + d] = own[at].astype(f32) + came[at].astype(f32)
            sent[base + d] = lax.ppermute(
                (own[to].astype(f32) + came[to].astype(f32)).astype(bf16), "shard", lay.xor(2)
            )
    return kept, sent


def scatter_step(lay, total, kept, sent, d):
    mine = kept[d] + sent[d].astype(f32)
    if total is None:
        return mine
    return mine + lax.ppermute(total.astype(bf16), "shard", lay.step(-1)).astype(f32)


def exchange(lay, parts):
    groups = [list(range(p * lay.ways, (p + 1) * lay.ways)) for p in range(lay.packs)]
    return lax.all_to_all(
        parts, "shard", 0, 0, axis_index_groups=groups if lay.packs > 1 else None, tiled=True
    )


LANES = 128
SUB = D // LANES
TILE = 256
VMEM_LIMIT = 56 * 1024 * 1024


def spread_matrix():
    row = lax.broadcasted_iota(jnp.int32, (D, D), 0)
    col = lax.broadcasted_iota(jnp.int32, (D, D), 1)
    return jnp.where(row == (col % HD) * HEADS + col // HD, 1.0, 0.0).astype(bf16)


def unit_masks(first_unit, amount):
    unit = lax.broadcasted_iota(jnp.int32, (amount, LANES), 0) // SUB + first_unit
    is_up = (unit >= OUT_END // UNIT) & (unit < UP_END // UNIT)
    by_row = ((unit >= QKV_END // UNIT) & (unit < OUT_END // UNIT)) | (unit >= UP_END // UNIT)
    return is_up, by_row


def pack_kernel(info_ref, first_ref, second_ref, out_ref, x_ref):
    rows = first_ref.shape[0]
    amount = rows // UNIT
    ids = lax.broadcasted_iota(jnp.int32, (rows, LANES), 0)
    x_ref[...] = jnp.where(
        ids < info_ref[0], first_ref[...].astype(f32), second_ref[...].astype(f32)
    )
    is_up, by_row = unit_masks(info_ref[1], amount)
    low = lax.broadcasted_iota(jnp.int32, (amount, LANES), 1) < HD
    spread = spread_matrix()
    halves = []
    for p in range(2):
        cols = [x_ref[pl.ds(SUB * p + a, amount, stride=UNIT), :] for a in range(SUB)]
        moved = jnp.dot(
            jnp.concatenate(cols, axis=1).astype(bf16), spread, preferred_element_type=f32
        )
        halves.append(
            [
                jnp.where(is_up, moved[:, a * LANES : (a + 1) * LANES], cols[a])
                for a in range(SUB)
            ]
        )
    whole = x_ref[...].reshape(amount // SUB, UNIT, SUB, LANES)
    for t in range(HEADS):
        zero, one = halves[0][t // 2], halves[1][t // 2]
        if t % 2 == 0:
            piece = jnp.where(low, zero, pltpu.roll(one, HD, 1))
        else:
            piece = jnp.where(low, pltpu.roll(zero, HD, 1), one)
        direct = whole[:, t].reshape(amount, LANES)
        out_ref[t] = jnp.where(by_row, direct, piece).astype(bf16)


def pack(first, second, bound, first_unit):
    rows = first.shape[0]
    return pl.pallas_call(
        pack_kernel,
        out_shape=jax.ShapeDtypeStruct((HEADS, rows // UNIT, LANES), bf16),
        in_specs=[
            pl.BlockSpec(memory_space=pltpu.SMEM),
            pl.BlockSpec(memory_space=pltpu.VMEM),
            pl.BlockSpec(memory_space=pltpu.VMEM),
        ],
        out_specs=pl.BlockSpec(memory_space=pltpu.VMEM),
        scratch_shapes=[pltpu.VMEM((rows, LANES), f32)],
        compiler_params=pltpu.CompilerParams(vmem_limit_bytes=VMEM_LIMIT),
        cost_estimate=pl.CostEstimate(
            flops=2 * rows * LANES * D, bytes_accessed=6 * rows * LANES, transcendentals=0
        ),
        name="pack",
    )(jnp.stack([bound, first_unit]).astype(jnp.int32), first, second)


MARGIN = 64


def unpack_kernel(info_ref, got_ref, out_ref, x_ref):
    amount = got_ref.shape[1]
    rows = amount * UNIT
    is_up, by_row = unit_masks(info_ref[0], amount)
    low = lax.broadcasted_iota(jnp.int32, (amount, LANES), 1) < HD
    spread = spread_matrix()
    x_ref[pl.ds(0, MARGIN), :] = jnp.zeros((MARGIN, LANES), f32)
    x_ref[pl.ds(MARGIN + rows, MARGIN), :] = jnp.zeros((MARGIN, LANES), f32)
    for p in range(2):
        cols = []
        for a in range(SUB):
            even, odd = got_ref[2 * a].astype(f32), got_ref[2 * a + 1].astype(f32)
            if p == 0:
                cols.append(jnp.where(low, even, pltpu.roll(odd, HD, 1)))
            else:
                cols.append(jnp.where(low, pltpu.roll(even, HD, 1), odd))
        moved = lax.dot_general(
            jnp.concatenate(cols, axis=1).astype(bf16),
            spread,
            (((1,), (1,)), ((), ())),
            preferred_element_type=f32,
        )
        for a in range(SUB):
            x_ref[pl.ds(MARGIN + SUB * p + a, amount, stride=UNIT), :] = jnp.where(
                is_up, moved[:, a * LANES : (a + 1) * LANES], cols[a]
            )
    whole = x_ref[pl.ds(MARGIN, rows), :].reshape(amount // SUB, UNIT, SUB, LANES)
    keep = by_row.reshape(amount // SUB, SUB, LANES)
    mixed = [
        jnp.where(keep, got_ref[t].astype(f32).reshape(amount // SUB, SUB, LANES), whole[:, t])
        for t in range(HEADS)
    ]
    x_ref[pl.ds(MARGIN, rows), :] = jnp.stack(mixed, axis=1).reshape(rows, LANES)
    size = out_ref.shape[0]
    low = lax.broadcasted_iota(jnp.int32, (size, LANES), 1) < HD

    def cut(start):
        base = start // 2
        here = x_ref[pl.ds(base, size), :]
        after = x_ref[pl.ds(base + 1, size), :]
        split = jnp.where(low, pltpu.roll(here, HD, 1), pltpu.roll(after, HD, 1))
        return jnp.where(start % 2 == 1, split, here)

    place = 2 * lax.broadcasted_iota(jnp.int32, (size, LANES), 0) + jnp.where(low, 0, 1)
    first = cut(info_ref[1])
    out_ref[...] = first
    out_ref[...] = jnp.where(place < info_ref[3], out_ref[...], cut(info_ref[2]))


def unpack(got, first_unit, start_one, start_two, bound, size):
    amount = got.shape[1]
    out_rows = -(-size // (SUB * LANES)) * SUB
    info = jnp.stack([first_unit, start_one // HD, start_two // HD, bound // HD])
    return pl.pallas_call(
        unpack_kernel,
        out_shape=jax.ShapeDtypeStruct((out_rows, LANES), f32),
        in_specs=[
            pl.BlockSpec(memory_space=pltpu.SMEM),
            pl.BlockSpec(memory_space=pltpu.VMEM),
        ],
        out_specs=pl.BlockSpec(memory_space=pltpu.VMEM),
        scratch_shapes=[pltpu.VMEM((amount * UNIT + 2 * MARGIN, LANES), f32)],
        compiler_params=pltpu.CompilerParams(vmem_limit_bytes=VMEM_LIMIT),
        cost_estimate=pl.CostEstimate(
            flops=2 * amount * UNIT * LANES * D, bytes_accessed=6 * amount * UNIT * LANES, transcendentals=0
        ),
        name="unpack",
    )(info.astype(jnp.int32), got)


def nt(a, b):
    return lax.dot_general(a, b, (((1,), (1,)), ((), ())), preferred_element_type=f32)


def tn(a, b):
    return lax.dot_general(a, b, (((0,), (0,)), ((), ())), preferred_element_type=f32)


def nn(a, b):
    return lax.dot_general(a, b, (((1,), (0,)), ((), ())), preferred_element_type=f32)


QUARTERS = 4


def pick_tile(refs):
    quarter = pl.program_id(0) // (pl.num_programs(0) // QUARTERS)
    value = refs[0][...]
    for q in range(1, QUARTERS):
        value = jnp.where(quarter == q, refs[q][...], value)
    return value


def start_tile(refs):
    both = pick_tile(refs)
    x = both[:, :D].astype(f32)
    center = x - jnp.mean(x, axis=1, keepdims=True)
    inverse = lax.rsqrt(jnp.mean(center * center, axis=1, keepdims=True) + norm_eps)
    return center * inverse, both[:, D:]


def store_tile(refs, col, value):
    quarter = pl.program_id(0) // (pl.num_programs(0) // QUARTERS)
    for q in range(QUARTERS):

        @pl.when(quarter == q)
        def _():
            refs[q][:, col : col + D] = value


def layer_kernel(*refs):
    rows_refs, sums_refs = refs[:4], refs[12:16]
    seg_ref, table_ref, w_qkv_ref, w_up_ref, w_down_ref, w_out_ref, bias_ref, vec_ref = refs[4:12]
    gqkv_ref, gup_ref, gdown_ref, gout_ref, gbias_ref, gvec_ref = refs[16:22]
    aqkv, aup, adown, aout = refs[22:]
    step = pl.program_id(0)

    @pl.when(step == 0)
    def _():
        for ref in (aqkv, aup, adown, aout, gbias_ref, gvec_ref):
            ref[...] = jnp.zeros(ref.shape, ref.dtype)

    length = seg_ref.shape[1]
    wide = 2 * LANES
    hat, go = start_tile(rows_refs)
    gain_one, shift_one = vec_ref[1:2, :], vec_ref[2:3, :]
    gain_two, shift_two = vec_ref[3:4, :], vec_ref[4:5, :]
    in_one = (hat * gain_one + shift_one).astype(bf16)
    in_two = (hat * gain_two + shift_two).astype(bf16)
    hidden = nn(in_two, w_up_ref[...]) + bias_ref[1:2, :]
    cdf = 0.5 * (1.0 + lax.erf(hidden * root_half))
    active = (hidden * cdf).astype(bf16)
    slope = cdf + hidden * jnp.exp(-0.5 * hidden * hidden) * inv_root_twopi
    ghid = nt(go, w_down_ref[...]) * slope
    ghid_bf = ghid.astype(bf16)
    low_rot = lax.broadcasted_iota(jnp.int32, (TILE, wide), 1) % HD < ROT // 2
    low = lax.broadcasted_iota(jnp.int32, (length, LANES), 1) < HD
    row_id = lax.broadcasted_iota(jnp.int32, (length, length), 0)
    col_id = lax.broadcasted_iota(jnp.int32, (length, length), 1)
    spot = lax.broadcasted_iota(jnp.int32, (length, wide), 1).astype(f32)
    rows_f = lax.broadcasted_iota(jnp.int32, (length, 1), 0).astype(f32)

    masks, picks = [], []
    for b in range(TILE // length):
        seg_row = seg_ref[pl.ds(step * (TILE // length) + b, 1), :]
        seg_col = jnp.sum(jnp.where(row_id == col_id, seg_row, 0.0), axis=1, keepdims=True)
        masks.append(jnp.where((seg_col == seg_row) & (col_id <= row_id), 0.0, -1e30))
        picks.append(jnp.where(spot == rows_f - seg_col, 1.0, 0.0).astype(bf16))
    pick = jnp.concatenate(picks, axis=0)
    cosine = nn(pick, table_ref[0]) + nn(pick, table_ref[1])
    sine = nn(pick, table_ref[2]) + nn(pick, table_ref[3])

    def swap(v):
        ahead = pltpu.roll(v, wide - ROT // 2, 1)
        return jnp.where(low_rot, ahead, pltpu.roll(v, ROT // 2, 1))

    mixed = nn(in_one, w_qkv_ref[...]) + bias_ref[0:1, :]
    rot = mixed * cosine + swap(mixed) * sine
    gheads = nt(go, w_out_ref[...]).astype(bf16)
    scale = HD ** (-0.5)
    heads, gmix = [], []
    for b in range(TILE // length):
        part = slice(b * length, (b + 1) * length)
        qk = rot[part, :LANES]
        vv = rot[part, LANES:].astype(bf16)
        turned = pltpu.roll(qk, HD, 1)
        q_low = jnp.where(low, qk, 0.0).astype(bf16)
        k_low = jnp.where(low, turned, 0.0).astype(bf16)
        q_high = jnp.where(low, 0.0, turned).astype(bf16)
        gh = gheads[part]
        scores = nt(q_low, k_low) * scale + masks[b]
        expd = jnp.exp(scores - jnp.max(scores, axis=1, keepdims=True))
        probs = expd / jnp.sum(expd, axis=1, keepdims=True)
        probs_bf = probs.astype(bf16)
        head = nn(probs_bf, vv).astype(bf16)
        heads.append(head)
        delta = jnp.sum(gh.astype(f32) * head.astype(f32), axis=1, keepdims=True)
        gs = (probs * (nt(gh, vv) - delta) * scale).astype(bf16)
        gqk = nn(gs, k_low) + tn(gs, q_high)
        gv = tn(probs_bf, gh)
        gmix.append(jnp.concatenate([gqk, gv], axis=1))
    head = jnp.concatenate(heads, axis=0)
    gmix = jnp.concatenate(gmix, axis=0)
    gmix = gmix * cosine - swap(gmix) * sine
    gmix_bf = gmix.astype(bf16)

    out = nn(head, w_out_ref[...]) + nn(active, w_down_ref[...])
    store_tile(sums_refs, 0, out.astype(bf16))
    norm_one = nt(gmix_bf, w_qkv_ref[...])
    norm_two = nt(ghid_bf, w_up_ref[...])
    store_tile(sums_refs, D, (norm_one * gain_one + norm_two * gain_two).astype(bf16))
    gvec_ref[0:1, :] += jnp.sum(norm_one * hat, axis=0, keepdims=True)
    gvec_ref[1:2, :] += jnp.sum(norm_one, axis=0, keepdims=True)
    gvec_ref[2:3, :] += jnp.sum(norm_two * hat, axis=0, keepdims=True)
    gvec_ref[3:4, :] += jnp.sum(norm_two, axis=0, keepdims=True)
    gvec_ref[4:5, :] += jnp.sum(go.astype(f32), axis=0, keepdims=True)
    gbias_ref[0:1, :] += jnp.sum(gmix, axis=0, keepdims=True)
    gbias_ref[1:2, :] += jnp.sum(ghid, axis=0, keepdims=True)
    aqkv[...] += tn(in_one, gmix_bf)
    aup[...] += tn(in_two, ghid_bf)
    adown[...] += tn(active, go)
    aout[...] += tn(head, go)

    @pl.when(step == pl.num_programs(0) - 1)
    def _():
        gqkv_ref[...] = aqkv[...].astype(bf16)
        gup_ref[...] = aup[...].astype(bf16)
        gdown_ref[...] = adown[...].astype(bf16)
        gout_ref[...] = aout[...].astype(bf16)


def quarter_tiles(width, count):
    def spec(q):
        return pl.BlockSpec((TILE, width), lambda i: (jnp.clip(i - q * count, 0, count - 1), 0))

    return [spec(q) for q in range(QUARTERS)]


def whole(*shape):
    return pl.BlockSpec(shape, lambda i: (0,) * len(shape))


def layer(rows, seg, table, w_qkv, w_up, w_down, w_out, bias, vec):
    count = rows[0].shape[0] // TILE
    wide = 2 * LANES
    cols = FF // HEADS
    weights = [(D, wide), (D, cols), (cols, D), (LANES, D)]
    small = [(8, wide), (8, D)]
    return pl.pallas_call(
        layer_kernel,
        grid=(QUARTERS * count,),
        in_specs=[
            *quarter_tiles(2 * D, count),
            whole(*seg.shape),
            whole(*table.shape),
            *[whole(*shape) for shape in weights + small],
        ],
        out_specs=[
            *quarter_tiles(2 * D, count),
            *[whole(*shape) for shape in weights + small],
        ],
        out_shape=[
            *[jax.ShapeDtypeStruct(rows[0].shape, bf16)] * QUARTERS,
            *[jax.ShapeDtypeStruct(shape, bf16) for shape in weights],
            *[jax.ShapeDtypeStruct(shape, f32) for shape in small],
        ],
        scratch_shapes=[pltpu.VMEM(shape, f32) for shape in weights],
        compiler_params=pltpu.CompilerParams(vmem_limit_bytes=VMEM_LIMIT),
        cost_estimate=pl.CostEstimate(
            flops=24 * QUARTERS * rows[0].shape[0] * D * FF // HEADS,
            bytes_accessed=4 * QUARTERS * rows[0].size,
            transcendentals=0,
        ),
        name="layer",
    )(*rows, seg, table, w_qkv, w_up, w_down, w_out, bias, vec)


def turn_table():
    wide = 2 * LANES
    lane = jnp.arange(wide)
    inner = lane % HD
    turns = (inner < ROT) & (lane < 2 * HD)
    frequency = 10000.0 ** (-2.0 * (lane % (ROT // 2)).astype(f32) / ROT)
    phase = jnp.arange(wide, dtype=f32)[:, None] * frequency[None]
    cosine = jnp.where(turns, jnp.cos(phase), 1.0)
    sine = jnp.where(turns, jnp.where(inner < ROT // 2, -1.0, 1.0) * jnp.sin(phase), 0.0)
    out = []
    for values in (cosine, sine):
        top = lax.reduce_precision(values, 8, 7)
        out += [top.astype(bf16), (values - top).astype(bf16)]
    return jnp.stack(out)


def offer_params(lay, params, segment, shard_id, rep_id):
    table = jnp.asarray(lay.tables)[shard_id]
    rows = (lay.units + 1) * UNIT
    chunk = params.astype(bf16)
    padded = jnp.pad(chunk, (PAD, rows * D + 2 * PAD - chunk.shape[0]))
    first = lax.dynamic_slice(padded, (PAD - table[0],), (rows * D,)).reshape(rows * SUB, LANES)
    second = lax.dynamic_slice(padded, (PAD - table[1],), (rows * D,)).reshape(rows * SUB, LANES)
    body = pack(first, second, table[2] * SUB, shard_id * lay.units)
    size = chunk.shape[0]
    vec = []
    for flat_row, amount, _ in RUNS:
        start = flat_row * D - shard_id * size
        begin = jnp.clip(start, -PAD, size)
        piece = lax.dynamic_slice(padded, (PAD + begin,), (amount * D,))
        vec.append(jnp.where(start == begin, piece, 0).reshape(amount, D))
    qkv_cols = vec[0].reshape(3, HEADS, HD).transpose(1, 0, 2).reshape(HEADS, 3 * HD)
    up_cols = vec[2].reshape(FF // HEADS, HEADS).T
    used = qkv_cols.shape[1] + up_cols.shape[1]
    mixed_row = jnp.concatenate([qkv_cols, up_cols, jnp.zeros((HEADS, D - used), bf16)], axis=1)
    mixed_row = mixed_row[:, None]
    full = jnp.concatenate(
        [vec[1] + vec[3][:1], vec[3][1:], jnp.zeros((lay.slots - lay.units - 7, D), bf16)], axis=0
    )
    full = jnp.broadcast_to(full[None], (HEADS,) + full.shape)
    tail = jnp.concatenate([mixed_row, full], axis=1).reshape(HEADS, -1, LANES)
    parts = jnp.concatenate([body, tail], axis=1)
    wide = lay.share * SUB
    share = lax.dynamic_slice_in_dim(parts, rep_id * wide, wide, axis=1)
    seg_row = jnp.pad(segment.astype(bf16), (0, D - segment.shape[0]))
    seg_row = jnp.broadcast_to(seg_row.reshape(1, SUB, LANES), (HEADS, SUB, LANES))
    return jnp.concatenate([share, seg_row], axis=1)


def take_params(lay, got, shard_id, rep_id):
    got = all_shares(lay, got, rep_id).reshape(lay.ways, lay.slots, SUB, LANES)
    if lay.packs > 1:
        packs = [got] + [
            lax.ppermute(got, "shard", lay.xor(lay.ways * k)) for k in range(1, lay.packs)
        ]
        order = jnp.arange(lay.packs, dtype=jnp.int32) ^ (shard_id // lay.ways)
        got = jnp.take(jnp.stack(packs), order, axis=0)
        got = got.reshape(lay.n, lay.slots, SUB, LANES)
    carry = got[:-1, lay.units : lay.units + 1]
    carry = jnp.concatenate([jnp.zeros_like(carry[:1]), carry], axis=0)
    units = jnp.concatenate([got[:, :1] + carry, got[:, 1 : lay.units]], axis=1)
    units = units.reshape(MAT_ROWS // UNIT, SUB, LANES)
    w_qkv = units[: QKV_END // UNIT].reshape(D, 3 * HD)
    w_up = units[OUT_END // UNIT : UP_END // UNIT].reshape(D, FF // HEADS)
    w_down = units[UP_END // UNIT :].reshape(FF // HEADS, D)
    out_rows = units[QKV_END // UNIT : OUT_END // UNIT]
    w_out = exchange(lay, out_rows.reshape(HEADS, HD // HEADS, D))
    w_out = w_out.transpose(1, 0, 2).reshape(HD, D)
    extra = jnp.sum(got[:, lay.units + 1 : lay.units + 7].astype(f32), axis=0).reshape(6, D)
    b_qkv = extra[0, : 3 * HD]
    b_up = extra[0, 3 * HD : 3 * HD + FF // HEADS]
    return w_qkv, b_qkv, w_out, w_up, b_up, w_down, extra[1:]


def share_sum(lay, parts, rep_id):
    by_rep = parts.reshape(parts.shape[0], lay.reps, lay.share, D)
    total = lax.dynamic_index_in_dim(by_rep, rep_id, axis=1, keepdims=False).astype(f32)
    for k in range(1, lay.reps):
        theirs = lax.dynamic_index_in_dim(by_rep, rep_id ^ k, axis=1, keepdims=False)
        total = total + lax.ppermute(theirs, "rep", lay.rep_xor(k)).astype(f32)
    return total.astype(bf16)


def windows(lay, units, first, last):
    body = units[: (last - first) * lay.units].reshape(last - first, lay.units, D)
    after = units[lay.units :: lay.units][: last - first, None]
    short = last - first - after.shape[0]
    after = jnp.pad(after, ((0, short), (0, 0), (0, 0)))
    room = jnp.zeros((last - first, lay.slots - lay.units - 1, D), bf16)
    return jnp.concatenate([body, after, room], axis=1)


def own_share(lay, late, early, mixed_row, full, shard_id, rep_id):
    total = jnp.concatenate([late, early], axis=0)
    tail = jnp.concatenate([mixed_row[None], full], axis=0)
    for k in [2**i for i in range((lay.reps - 1).bit_length())]:
        tail = tail + lax.ppermute(tail.astype(bf16), "rep", lay.rep_xor(k)).astype(f32)
    tail = jnp.pad(tail, ((lay.units + 1, lay.slots - lay.units - 7), (0, 0))).astype(bf16)
    tail = lax.dynamic_slice_in_dim(tail, rep_id * lay.share, lay.share, axis=0)
    total = total + tail[None]
    if lay.packs > 1:
        pack_id = shard_id // lay.ways
        by_pack = total.reshape(lay.packs, lay.ways, lay.share, D)
        total = lax.dynamic_index_in_dim(by_pack, pack_id, keepdims=False).astype(f32)
        for k in range(1, lay.packs):
            theirs = lax.dynamic_index_in_dim(by_pack, pack_id ^ k, keepdims=False)
            total = total + lax.ppermute(theirs, "shard", lay.xor(lay.ways * k)).astype(f32)
        total = total.astype(bf16)
    return total


def all_shares(lay, got, rep_id):
    got = [got] + [lax.ppermute(got, "rep", lay.rep_xor(k)) for k in range(1, lay.reps)]
    if lay.reps == 2:
        got = [jnp.where(rep_id == r, got[0], got[1]) for r in range(2)]
        return jnp.concatenate(got, axis=1)
    got = jnp.take(jnp.stack(got), jnp.arange(lay.reps, dtype=jnp.int32) ^ rep_id, axis=0)
    return jnp.moveaxis(got, 0, 1).reshape(got.shape[1], -1, got.shape[-1])


def owner_part(lay, got, shard_id):
    body = got[:, : lay.units + 1].reshape(lay.ways, -1, LANES)
    extra = got[:, lay.units + 1 : lay.units + 7].astype(f32)
    qkv_vec = extra[:, 0, : 3 * HD].reshape(HEADS, 3, HD).transpose(1, 0, 2).reshape(3 * D)
    up_vec = extra[:, 0, 3 * HD : 3 * HD + FF // HEADS].T.reshape(FF)
    norm_vec = jnp.sum(extra[:, 1:5], axis=0).reshape(4 * D)
    out_vec = extra[0, 5]
    small = jnp.concatenate([qkv_vec, out_vec, up_vec, out_vec, norm_vec])
    table = jnp.asarray(lay.tables)[shard_id]
    size = (MAT_ROWS + VEC_ROWS) * D // lay.n
    flat = unpack(
        body, shard_id * lay.units, PAD + table[0], PAD + table[1], table[3], size
    )
    flat = flat.reshape(-1)[:size]
    run = 5 * D
    start = jnp.clip(table[3], 0, size - run)
    ids = start + lax.iota(jnp.int32, run)
    from_small = jnp.clip(start - table[5], -run, VEC_ROWS * D) + run
    vec = lax.dynamic_slice(jnp.pad(small, (run, run)), (from_small,), (run,))
    old = lax.dynamic_slice(flat, (start,), (run,))
    new = jnp.where((ids >= table[3]) & (ids < table[4]), vec, old)
    return lax.dynamic_update_slice(flat, new, (start,))


def per_device(lay, tokens, cotangent, segment, params, first_moment, second_moment):
    shard_id = lax.axis_index("shard")
    rep_id = lax.axis_index("rep")
    me = shard_id % lay.ways
    length = tokens.shape[0]
    blocks = lay.ways
    total_rows = blocks * length

    own_grad = jnp.where((segment >= 0)[:, None], cotangent, jnp.zeros_like(cotangent))
    block = jnp.concatenate([tokens, own_grad], axis=1)
    start = gather_start(lay, block)
    offer = offer_params(lay, params, segment, shard_id, rep_id)
    offer, start = lax.optimization_barrier((offer, start))
    got = exchange(lay, offer)
    chain, across = gather_line(lay, block, start)
    got, chain[-1] = lax.optimization_barrier((got, chain[-1]))
    seg_all = got[:, lay.share * SUB].astype(f32)
    w_qkv, b_qkv, w_out, w_up, b_up, w_down, full = take_params(
        lay, got[:, : lay.share * SUB], shard_id, rep_id
    )
    rows = gather_end(lay, chain, across)
    b_sum = full[0]
    spot = jnp.arange(blocks, dtype=jnp.int32)
    d_core, d_line, d_row = spot // (2 * lay.line), spot // 2 % lay.line, spot % 2
    source = (
        (me // 4 - d_line) % lay.line * 4 + ((me // 2 % 2) ^ d_row) * 2 + ((me % 2) ^ d_core)
    )
    seg = jnp.take(seg_all, source, axis=0)

    bias = jnp.pad(jnp.stack([jnp.pad(b_qkv, (0, HD)), b_up]), ((0, 6), (0, 0)))
    vec = jnp.pad(full, ((0, 8 - full.shape[0]), (0, 0)))
    *sums, grad_qkv, grad_w_up, grad_w_down, grad_w_out, bias_sums, vec_sums = layer(
        rows,
        seg,
        turn_table(),
        jnp.pad(w_qkv, ((0, 0), (0, HD))),
        w_up,
        w_down,
        jnp.pad(w_out, ((0, LANES - HD), (0, 0))),
        bias,
        vec,
    )
    own = tokens.astype(f32)
    own_center = own - jnp.mean(own, axis=-1, keepdims=True)
    own_inverse = lax.rsqrt(jnp.mean(own_center * own_center, axis=-1, keepdims=True) + norm_eps)
    own_hat = own_center * own_inverse
    grad_w_qkv = grad_qkv[:, : 3 * HD]
    first = QKV_END // UNIT // lay.units - 1
    cut = -(-OUT_END // UNIT // lay.units)
    units_qkv = grad_w_qkv.reshape(QKV_END // UNIT, D)
    units_feed = jnp.concatenate([grad_w_up.reshape(FF // UNIT, D), grad_w_down], axis=0)
    early = jnp.concatenate(
        [
            windows(lay, units_qkv[: first * lay.units + 1], 0, first),
            windows(lay, units_feed[cut * lay.units - OUT_END // UNIT :], cut, lay.n),
        ],
        axis=0,
    )
    early = share_sum(lay, early, rep_id)
    back = grad_w_out[:HD].reshape(HD // HEADS, HEADS, D).transpose(1, 0, 2)
    back = exchange(lay, back).reshape(HD, D)
    units = jnp.concatenate(
        [units_qkv[first * lay.units :], back, units_feed[: (cut + 1) * lay.units]], axis=0
    )
    late = windows(lay, units[: (cut - first) * lay.units + 1], first, cut)
    late = share_sum(lay, late, rep_id)
    late = jnp.concatenate([early[:first], late], axis=0)
    early = early[first:]
    used = 3 * HD + FF // HEADS
    mixed_row = jnp.concatenate(
        [bias_sums[0, : 3 * HD], bias_sums[1], jnp.zeros((D - used,), f32)]
    )
    vectors = vec_sums[:5]
    share = own_share(lay, late, early, mixed_row, vectors, shard_id, rep_id)

    kept, sent = scatter_planes(lay, sums, length)
    top = lay.line - 1
    share, sent[top] = lax.optimization_barrier((share, sent[top]))
    got = exchange(lay, share)
    total = scatter_step(lay, None, kept, sent, top)
    total = scatter_step(lay, total, kept, sent, top - 1)
    got, total = lax.optimization_barrier((got, total))
    got = all_shares(lay, got, rep_id)
    for d in range(top - 2, 0, -1):
        total = scatter_step(lay, total, kept, sent, d)
    got, total = lax.optimization_barrier((got, total))
    grad_total = owner_part(lay, got, shard_id)
    sums = scatter_step(lay, total, kept, sent, 0)
    out_sum, g_sum = sums[:, :D], sums[:, D:]
    out_rows = (tokens.astype(f32) + out_sum + b_sum).astype(bf16)
    grad_rows = (
        own_grad.astype(f32)
        + own_inverse
        * (
            g_sum
            - jnp.mean(g_sum, axis=-1, keepdims=True)
            - own_hat * jnp.mean(g_sum * own_hat, axis=-1, keepdims=True)
        )
    ).astype(bf16)

    new_weights, first_new, second_new = adam_update(
        params, first_moment, second_moment, grad_total
    )
    return (out_rows, grad_rows, grad_total, new_weights, first_new, second_new)


def solution(mesh):
    lay = Layout(mesh)
    in_specs = (
        P(("rep", "shard"), None),
        P(("rep", "shard"), None),
        P(("rep", "shard")),
        P("shard"),
        P("shard"),
        P("shard"),
    )
    out_specs = (
        P(("rep", "shard"), None),
        P(("rep", "shard"), None),
        P("shard"),
        P("shard"),
        P("shard"),
        P("shard"),
    )

    def body(*args):
        return per_device(lay, *args)

    return jax.shard_map(body, mesh=mesh, in_specs=in_specs, out_specs=out_specs, check_vma=False)
```

```python
import math

import jax
import jax.numpy as jnp
import numpy as np
from jax import lax
from jax.experimental import pallas as pl
from jax.experimental.pallas import tpu as pltpu
from jax.sharding import PartitionSpec as P

D = 1024
HEADS = 16
HD = 64
ROT = 16
FF = 4096
STEP = 4
UNIT = HEADS

norm_eps = 1e-05
adam_eps = 1e-08
beta_one = 0.9
beta_two = 0.999
learn_rate = 0.003
decay_rate = 0.1
root_half = 0.7071067811865476
inv_root_twopi = 0.3989422804014327


QKV_END = 3 * D
OUT_END = QKV_END + D
UP_END = OUT_END + FF
DOWN_END = UP_END + FF
MAT_ROWS = DOWN_END
SECTIONS = ((0, QKV_END, 0), (QKV_END, OUT_END, 3), (OUT_END, UP_END, 4), (UP_END, DOWN_END, 8))
RUNS = (
    (QKV_END, 3, 0),
    (OUT_END + 3, 1, 3),
    (UP_END + 4, 4, 4),
    (DOWN_END + 8, 5, 8),
)
VEC_ROWS = 13
PAD = 8 * D

f32 = jnp.float32
bf16 = jnp.bfloat16


def owner_tables(owners):
    total = (MAT_ROWS + VEC_ROWS) * D
    part = total // owners
    lead = VEC_ROWS * D // owners
    rows = []
    for s in range(owners):
        start, end = s * part, (s + 1) * part
        first = next((i for i, (a, b, v) in enumerate(SECTIONS) if (b + v) * D > start), 3)
        second = min(first + 1, 3)
        run_row, run_len, vec_row = RUNS[first]
        run_a = min(max(run_row * D - start, 0), part)
        run_b = min(max((run_row + run_len) * D - start, 0), part)
        rows.append(
            (
                lead * s - SECTIONS[first][2] * D,
                lead * s - SECTIONS[second][2] * D,
                (SECTIONS[first][1] - (MAT_ROWS // owners) * s) if first < 3 else 2 * MAT_ROWS,
                run_a,
                run_b,
                run_row * D - start - vec_row * D,
            )
        )
    return np.array(rows, np.int32)


def rotate(values, cosine, sine_part):
    half_rot = ROT // 2
    lower_half = values[..., :half_rot]
    upper_half = values[..., half_rot:ROT]
    return jnp.concatenate(
        [
            lower_half * cosine - upper_half * sine_part,
            upper_half * cosine + lower_half * sine_part,
            values[..., ROT:],
        ],
        axis=-1,
    )


def gelu_parts(values):
    cdf = 0.5 * (1.0 + lax.erf(values * root_half))
    return values * cdf, cdf + values * jnp.exp(-0.5 * values * values) * inv_root_twopi


def adam_update(weights, moment_one, moment_two, grad_total):
    first_new = beta_one * moment_one + (1.0 - beta_one) * grad_total
    second_new = beta_two * moment_two + (1.0 - beta_two) * grad_total * grad_total
    correct_one = 1.0 - beta_one**STEP
    correct_two = 1.0 - beta_two**STEP
    change = first_new / correct_one / (jnp.sqrt(second_new / correct_two) + adam_eps)
    return (weights - learn_rate * (change + decay_rate * weights), first_new, second_new)


def bmm(spec, a, b):
    return jnp.einsum(spec, a, b, preferred_element_type=f32)


class Layout:
    def __init__(self, mesh):
        self.n = mesh.shape["shard"]
        self.reps = mesh.shape["rep"]
        self.ways = HEADS
        assert self.n % self.ways == 0
        self.packs = self.n // self.ways
        self.core, self.row = 2, 2
        self.line = self.ways // 4
        self.units = MAT_ROWS // UNIT // self.n
        slots = self.units + 1 + 1 + 5
        self.slots = -(-slots // self.reps) * self.reps
        self.share = self.slots // self.reps
        self.tables = owner_tables(self.n)

    def xor(self, k):
        return [(i, i ^ k) for i in range(self.n)]

    def step(self, k):
        w = self.ways
        return [(i, i - i % w + (i % w + 4 * k) % w) for i in range(self.n)]

    def rep_xor(self, k):
        return [(i, i ^ k) for i in range(self.reps)]


def gather_start(lay, block):
    along = lax.ppermute(block, "shard", lay.step(1))
    return along, lax.ppermute(block, "shard", lay.xor(2))


def gather_line(lay, chain, across):
    along = lax.ppermute(chain[-1], "shard", lay.step(1))
    return chain + [along], across + [lax.ppermute(chain[-1], "shard", lay.xor(2))]


def gather_end(lay, chain, across):
    across = across + [lax.ppermute(chain[-1], "shard", lay.xor(2))]
    plane = [piece for pair in zip(chain, across) for piece in pair]
    near, far = (
        jnp.concatenate(plane[i : i + lay.line], axis=0) for i in range(0, 2 * lay.line, lay.line)
    )
    return near, far, *(lax.ppermute(half, "shard", lay.xor(1)) for half in (near, far))


def scatter_planes(lay, quarters, length):
    near, far, other_near, other_far = quarters
    kept, sent = {}, {}
    for base, own, other in ((lay.line // 2, far, other_far), (0, near, other_near)):
        came = lax.ppermute(other, "shard", lay.xor(1))
        for d in range(lay.line // 2 - 1, -1, -1):
            at = slice(2 * d * length, (2 * d + 1) * length)
            to = slice((2 * d + 1) * length, (2 * d + 2) * length)
            kept[base + d] = own[at].astype(f32) + came[at].astype(f32)
            sent[base + d] = lax.ppermute(
                (own[to].astype(f32) + came[to].astype(f32)).astype(bf16), "shard", lay.xor(2)
            )
    return kept, sent


def scatter_step(lay, total, kept, sent, d):
    mine = kept[d] + sent[d].astype(f32)
    if total is None:
        return mine
    return mine + lax.ppermute(total.astype(bf16), "shard", lay.step(-1)).astype(f32)


def exchange(lay, parts):
    groups = [list(range(p * lay.ways, (p + 1) * lay.ways)) for p in range(lay.packs)]
    return lax.all_to_all(
        parts, "shard", 0, 0, axis_index_groups=groups if lay.packs > 1 else None, tiled=True
    )


LANES = 128
SUB = D // LANES
TILE = 256
VMEM_LIMIT = 56 * 1024 * 1024


def spread_matrix():
    row = lax.broadcasted_iota(jnp.int32, (D, D), 0)
    col = lax.broadcasted_iota(jnp.int32, (D, D), 1)
    return jnp.where(row == (col % HD) * HEADS + col // HD, 1.0, 0.0).astype(bf16)


def unit_masks(first_unit, amount):
    unit = lax.broadcasted_iota(jnp.int32, (amount, LANES), 0) // SUB + first_unit
    is_up = (unit >= OUT_END // UNIT) & (unit < UP_END // UNIT)
    by_row = ((unit >= QKV_END // UNIT) & (unit < OUT_END // UNIT)) | (unit >= UP_END // UNIT)
    return is_up, by_row


def pack_kernel(info_ref, first_ref, second_ref, out_ref, x_ref):
    rows = first_ref.shape[0]
    amount = rows // UNIT
    ids = lax.broadcasted_iota(jnp.int32, (LANES, LANES), 0)

    def strip(i, carry):
        begin = pl.multiple_of(i * LANES, LANES)
        at = pl.ds(begin, LANES)
        x_ref[at, :] = jnp.where(
            ids < info_ref[0] - begin, first_ref[at, :].astype(f32), second_ref[at, :].astype(f32)
        )
        return carry

    lax.fori_loop(0, rows // LANES, strip, 0)
    is_up, by_row = unit_masks(info_ref[1], amount)
    low = lax.broadcasted_iota(jnp.int32, (amount, LANES), 1) < HD
    spread = spread_matrix()
    halves = []
    for p in range(2):
        cols = [x_ref[pl.ds(SUB * p + a, amount, stride=UNIT), :] for a in range(SUB)]
        moved = jnp.dot(
            jnp.concatenate(cols, axis=1).astype(bf16), spread, preferred_element_type=f32
        )
        halves.append(
            [
                jnp.where(is_up, moved[:, a * LANES : (a + 1) * LANES], cols[a])
                for a in range(SUB)
            ]
        )
    whole = x_ref[...].reshape(amount // SUB, UNIT, SUB, LANES)
    for t in range(HEADS):
        zero, one = halves[0][t // 2], halves[1][t // 2]
        if t % 2 == 0:
            piece = jnp.where(low, zero, pltpu.roll(one, HD, 1))
        else:
            piece = jnp.where(low, pltpu.roll(zero, HD, 1), one)
        direct = whole[:, t].reshape(amount, LANES)
        out_ref[t] = jnp.where(by_row, direct, piece).astype(bf16)


def pack(first, second, bound, first_unit):
    rows = first.shape[0]
    return pl.pallas_call(
        pack_kernel,
        out_shape=jax.ShapeDtypeStruct((HEADS, rows // UNIT, LANES), bf16),
        in_specs=[
            pl.BlockSpec(memory_space=pltpu.SMEM),
            pl.BlockSpec(memory_space=pltpu.VMEM),
            pl.BlockSpec(memory_space=pltpu.VMEM),
        ],
        out_specs=pl.BlockSpec(memory_space=pltpu.VMEM),
        scratch_shapes=[pltpu.VMEM((rows, LANES), f32)],
        compiler_params=pltpu.CompilerParams(vmem_limit_bytes=VMEM_LIMIT),
        cost_estimate=pl.CostEstimate(
            flops=2 * rows * LANES * D, bytes_accessed=6 * rows * LANES, transcendentals=0
        ),
        name="pack",
    )(jnp.stack([bound, first_unit]).astype(jnp.int32), first, second)


MARGIN = 64


def unpack_kernel(info_ref, got_ref, out_ref, x_ref):
    amount = got_ref.shape[1]
    rows = amount * UNIT
    is_up, by_row = unit_masks(info_ref[0], amount)
    low = lax.broadcasted_iota(jnp.int32, (amount, LANES), 1) < HD
    spread = spread_matrix()
    x_ref[pl.ds(0, MARGIN), :] = jnp.zeros((MARGIN, LANES), f32)
    x_ref[pl.ds(MARGIN + rows, 2 * MARGIN), :] = jnp.zeros((2 * MARGIN, LANES), f32)
    for p in range(2):
        cols = []
        for a in range(SUB):
            even, odd = got_ref[2 * a].astype(f32), got_ref[2 * a + 1].astype(f32)
            if p == 0:
                cols.append(jnp.where(low, even, pltpu.roll(odd, HD, 1)))
            else:
                cols.append(jnp.where(low, pltpu.roll(even, HD, 1), odd))
        moved = lax.dot_general(
            jnp.concatenate(cols, axis=1).astype(bf16),
            spread,
            (((1,), (1,)), ((), ())),
            preferred_element_type=f32,
        )
        for a in range(SUB):
            x_ref[pl.ds(MARGIN + SUB * p + a, amount, stride=UNIT), :] = jnp.where(
                is_up, moved[:, a * LANES : (a + 1) * LANES], cols[a]
            )
    whole = x_ref[pl.ds(MARGIN, rows), :].reshape(amount // SUB, UNIT, SUB, LANES)
    keep = by_row.reshape(amount // SUB, SUB, LANES)
    mixed = [
        jnp.where(keep, got_ref[t].astype(f32).reshape(amount // SUB, SUB, LANES), whole[:, t])
        for t in range(HEADS)
    ]
    x_ref[pl.ds(MARGIN, rows), :] = jnp.stack(mixed, axis=1).reshape(rows, LANES)
    low = lax.broadcasted_iota(jnp.int32, (LANES, LANES), 1) < HD
    place = 2 * lax.broadcasted_iota(jnp.int32, (LANES, LANES), 0) + jnp.where(low, 0, 1)

    def strip(i, carry):
        begin = pl.multiple_of(i * LANES, LANES)

        def cut(start):
            here = x_ref[pl.ds(start // 2 + begin, LANES), :]
            after = x_ref[pl.ds(start // 2 + begin + 1, LANES), :]
            split = jnp.where(low, pltpu.roll(here, HD, 1), pltpu.roll(after, HD, 1))
            return jnp.where(start % 2 == 1, split, here)

        out_ref[pl.ds(begin, LANES), :] = jnp.where(
            place < info_ref[3] - 2 * begin, cut(info_ref[1]), cut(info_ref[2])
        )
        return carry

    lax.fori_loop(0, out_ref.shape[0] // LANES, strip, 0)


def unpack(got, first_unit, start_one, start_two, bound):
    amount = got.shape[1]
    info = jnp.stack([first_unit, start_one // HD, start_two // HD, bound // HD])
    return pl.pallas_call(
        unpack_kernel,
        out_shape=jax.ShapeDtypeStruct((amount * UNIT, LANES), f32),
        in_specs=[
            pl.BlockSpec(memory_space=pltpu.SMEM),
            pl.BlockSpec(memory_space=pltpu.VMEM),
        ],
        out_specs=pl.BlockSpec(memory_space=pltpu.VMEM),
        scratch_shapes=[pltpu.VMEM((amount * UNIT + 3 * MARGIN, LANES), f32)],
        compiler_params=pltpu.CompilerParams(vmem_limit_bytes=VMEM_LIMIT),
        cost_estimate=pl.CostEstimate(
            flops=2 * amount * UNIT * LANES * D, bytes_accessed=6 * amount * UNIT * LANES, transcendentals=0
        ),
        name="unpack",
    )(info.astype(jnp.int32), got)


def nt(a, b):
    return lax.dot_general(a, b, (((1,), (1,)), ((), ())), preferred_element_type=f32)


def tn(a, b):
    return lax.dot_general(a, b, (((0,), (0,)), ((), ())), preferred_element_type=f32)


def nn(a, b):
    return lax.dot_general(a, b, (((1,), (0,)), ((), ())), preferred_element_type=f32)


QUARTERS = 4


STRIP = 64


def move_tile(refs, tile_ref, inward):
    quarter = pl.program_id(0) // (pl.num_programs(0) // QUARTERS)
    for q in range(QUARTERS):
        source, target = (refs[q], tile_ref) if inward else (tile_ref, refs[q])

        @pl.when(quarter == q)
        def _():
            def strip(i, carry):
                at = pl.ds(pl.multiple_of(i * STRIP, STRIP), STRIP)
                target[at, :] = source[at, :]
                return carry

            lax.fori_loop(0, TILE // STRIP, strip, 0)


def layer_kernel(*refs):
    rows_refs, sums_refs = refs[:4], refs[12:16]
    seg_ref, table_ref, w_qkv_ref, w_up_ref, w_down_ref, w_out_ref, bias_ref, vec_ref = refs[4:12]
    gqkv_ref, gfeed_ref, gout_ref, gbias_ref, gvec_ref = refs[16:21]
    aqkv, aup_low, aup_high, adown, aout, tile, sums = refs[21:]
    step = pl.program_id(0)

    @pl.when(step == 0)
    def _():
        for ref in (aqkv, aup_low, aup_high, adown, aout, gbias_ref, gvec_ref):
            ref[...] = jnp.zeros(ref.shape, ref.dtype)

    length = seg_ref.shape[1]
    wide = 2 * LANES
    move_tile(rows_refs, tile, True)
    x = tile[:, :D].astype(f32)
    center = x - jnp.mean(x, axis=1, keepdims=True)
    inverse = lax.rsqrt(jnp.mean(center * center, axis=1, keepdims=True) + norm_eps)
    hat = center * inverse
    go = tile[:, D:]
    gain_one, shift_one = vec_ref[1:2, :], vec_ref[2:3, :]
    gain_two, shift_two = vec_ref[3:4, :], vec_ref[4:5, :]
    in_one = (hat * gain_one + shift_one).astype(bf16)
    in_two = (hat * gain_two + shift_two).astype(bf16)
    hidden = nn(in_two, w_up_ref[...]) + bias_ref[1:2, :]
    cdf = 0.5 * (1.0 + lax.erf(hidden * root_half))
    active = (hidden * cdf).astype(bf16)
    slope = cdf + hidden * jnp.exp(-0.5 * hidden * hidden) * inv_root_twopi
    ghid = nt(go, w_down_ref[...]) * slope
    ghid_bf = ghid.astype(bf16)
    low_rot = lax.broadcasted_iota(jnp.int32, (TILE, wide), 1) % HD < ROT // 2
    low = lax.broadcasted_iota(jnp.int32, (length, LANES), 1) < HD
    row_id = lax.broadcasted_iota(jnp.int32, (length, length), 0)
    col_id = lax.broadcasted_iota(jnp.int32, (length, length), 1)
    spot = lax.broadcasted_iota(jnp.int32, (length, wide), 1).astype(f32)
    rows_f = lax.broadcasted_iota(jnp.int32, (length, 1), 0).astype(f32)

    masks, picks = [], []
    for b in range(TILE // length):
        seg_row = seg_ref[pl.ds(step * (TILE // length) + b, 1), :]
        seg_col = jnp.sum(jnp.where(row_id == col_id, seg_row, 0.0), axis=1, keepdims=True)
        masks.append(jnp.where((seg_col == seg_row) & (col_id <= row_id), 0.0, -1e30))
        picks.append(jnp.where(spot == rows_f - seg_col, 1.0, 0.0).astype(bf16))
    pick = jnp.concatenate(picks, axis=0)
    cosine = nn(pick, table_ref[0]) + nn(pick, table_ref[1])
    sine = nn(pick, table_ref[2]) + nn(pick, table_ref[3])

    def swap(v):
        ahead = pltpu.roll(v, wide - ROT // 2, 1)
        return jnp.where(low_rot, ahead, pltpu.roll(v, ROT // 2, 1))

    mixed = nn(in_one, w_qkv_ref[...]) + bias_ref[0:1, :]
    rot = mixed * cosine + swap(mixed) * sine
    gheads = nt(go, w_out_ref[...]).astype(bf16)
    scale = HD ** (-0.5)
    heads, gmix = [], []
    for b in range(TILE // length):
        part = slice(b * length, (b + 1) * length)
        qk = rot[part, :LANES]
        vv = rot[part, LANES:].astype(bf16)
        turned = pltpu.roll(qk, HD, 1)
        q_low = jnp.where(low, qk, 0.0).astype(bf16)
        k_low = jnp.where(low, turned, 0.0).astype(bf16)
        q_high = jnp.where(low, 0.0, turned).astype(bf16)
        gh = gheads[part]
        scores = nt(q_low, k_low) * scale + masks[b]
        expd = jnp.exp(scores - jnp.max(scores, axis=1, keepdims=True))
        probs = expd / jnp.sum(expd, axis=1, keepdims=True)
        probs_bf = probs.astype(bf16)
        head = nn(probs_bf, vv).astype(bf16)
        heads.append(head)
        delta = jnp.sum(gh.astype(f32) * head.astype(f32), axis=1, keepdims=True)
        gs = (probs * (nt(gh, vv) - delta) * scale).astype(bf16)
        gqk = nn(gs, k_low) + tn(gs, q_high)
        gv = tn(probs_bf, gh)
        gmix.append(jnp.concatenate([gqk, gv], axis=1))
    head = jnp.concatenate(heads, axis=0)
    gmix = jnp.concatenate(gmix, axis=0)
    gmix = gmix * cosine - swap(gmix) * sine
    gmix_bf = gmix.astype(bf16)

    sums[:, :D] = (nn(head, w_out_ref[...]) + nn(active, w_down_ref[...])).astype(bf16)
    norm_one = nt(gmix_bf, w_qkv_ref[...])
    norm_two = nt(ghid_bf, w_up_ref[...])
    sums[:, D:] = (norm_one * gain_one + norm_two * gain_two).astype(bf16)
    gvec_ref[0:1, :] += jnp.sum(norm_one * hat, axis=0, keepdims=True)
    gvec_ref[1:2, :] += jnp.sum(norm_one, axis=0, keepdims=True)
    gvec_ref[2:3, :] += jnp.sum(norm_two * hat, axis=0, keepdims=True)
    gvec_ref[3:4, :] += jnp.sum(norm_two, axis=0, keepdims=True)
    gvec_ref[4:5, :] += jnp.sum(go.astype(f32), axis=0, keepdims=True)
    gbias_ref[0:1, :] += jnp.sum(gmix, axis=0, keepdims=True)
    gbias_ref[1:2, :] += jnp.sum(ghid, axis=0, keepdims=True)
    aqkv[...] += tn(in_one, gmix_bf)
    for half, ref in enumerate((aup_low, aup_high)):
        ref[...] += tn(in_two, ghid_bf[:, half * LANES : (half + 1) * LANES])
    adown[...] += tn(active, go)
    aout[...] += tn(head, go)
    move_tile(sums_refs, sums, False)

    @pl.when(step == pl.num_programs(0) - 1)
    def _():
        gqkv_ref[...] = aqkv[...].astype(bf16)
        cols = FF // HEADS
        for k in range(D // cols):
            for half, ref in enumerate((aup_low, aup_high)):
                rows = ref[pl.ds(k, cols, stride=D // cols), :]
                lanes = pl.ds(k * cols + half * LANES, LANES)
                gfeed_ref[pl.ds(0, cols), lanes] = rows.astype(bf16)
        gfeed_ref[pl.ds(cols, cols), :] = adown[...].astype(bf16)
        gout_ref[...] = aout[...].astype(bf16)


def quarter_tiles(width, count):
    def spec(q):
        return pl.BlockSpec((TILE, width), lambda i: (jnp.clip(i - q * count, 0, count - 1), 0))

    return [spec(q) for q in range(QUARTERS)]


def whole(*shape):
    return pl.BlockSpec(shape, lambda i: (0,) * len(shape))


def layer(rows, seg, table, w_qkv, w_up, w_down, w_out, bias, vec):
    count = rows[0].shape[0] // TILE
    wide = 2 * LANES
    cols = FF // HEADS
    weights = [(D, wide), (D, cols), (cols, D), (LANES, D)]
    grads = [(D, wide), (2 * cols, D), (LANES, D)]
    small = [(8, wide), (8, D)]
    return pl.pallas_call(
        layer_kernel,
        grid=(QUARTERS * count,),
        in_specs=[
            *quarter_tiles(2 * D, count),
            whole(*seg.shape),
            whole(*table.shape),
            *[whole(*shape) for shape in weights + small],
        ],
        out_specs=[
            *quarter_tiles(2 * D, count),
            *[whole(*shape) for shape in grads + small],
        ],
        out_shape=[
            *[jax.ShapeDtypeStruct(rows[0].shape, bf16)] * QUARTERS,
            *[jax.ShapeDtypeStruct(shape, bf16) for shape in grads],
            *[jax.ShapeDtypeStruct(shape, f32) for shape in small],
        ],
        scratch_shapes=[
            pltpu.VMEM((D, wide), f32),
            *[pltpu.VMEM((D, LANES), f32)] * 2,
            pltpu.VMEM((cols, D), f32),
            pltpu.VMEM((LANES, D), f32),
            *[pltpu.VMEM((TILE, 2 * D), bf16)] * 2,
        ],
        compiler_params=pltpu.CompilerParams(vmem_limit_bytes=VMEM_LIMIT),
        cost_estimate=pl.CostEstimate(
            flops=24 * QUARTERS * rows[0].shape[0] * D * FF // HEADS,
            bytes_accessed=4 * QUARTERS * rows[0].size,
            transcendentals=0,
        ),
        name="layer",
    )(*rows, seg, table, w_qkv, w_up, w_down, w_out, bias, vec)


def turn_table():
    wide = 2 * LANES
    lane = jnp.arange(wide)
    inner = lane % HD
    turns = (inner < ROT) & (lane < 2 * HD)
    frequency = 10000.0 ** (-2.0 * (lane % (ROT // 2)).astype(f32) / ROT)
    phase = jnp.arange(wide, dtype=f32)[:, None] * frequency[None]
    cosine = jnp.where(turns, jnp.cos(phase), 1.0)
    sine = jnp.where(turns, jnp.where(inner < ROT // 2, -1.0, 1.0) * jnp.sin(phase), 0.0)
    out = []
    for values in (cosine, sine):
        top = lax.reduce_precision(values, 8, 7)
        out += [top.astype(bf16), (values - top).astype(bf16)]
    return jnp.stack(out)


def cut_windows(lay, params, shard_id):
    table = jnp.asarray(lay.tables)[shard_id]
    rows = (lay.units + 1) * UNIT
    chunk = params.astype(bf16)
    padded = jnp.pad(chunk, (PAD, rows * D + 2 * PAD - chunk.shape[0]))
    first = lax.dynamic_slice(padded, (PAD - table[0],), (rows * D,)).reshape(rows * SUB, LANES)
    second = lax.dynamic_slice(padded, (PAD - table[1],), (rows * D,)).reshape(rows * SUB, LANES)
    return padded, first, second


def offer_params(lay, cuts, size, segment, shard_id, rep_id):
    table = jnp.asarray(lay.tables)[shard_id]
    padded, first, second = cuts
    body = pack(first, second, table[2] * SUB, shard_id * lay.units)
    vec = []
    for flat_row, amount, _ in RUNS:
        start = flat_row * D - shard_id * size
        begin = jnp.clip(start, -PAD, size)
        piece = lax.dynamic_slice(padded, (PAD + begin,), (amount * D,))
        vec.append(jnp.where(start == begin, piece, 0).reshape(amount, D))
    qkv_cols = vec[0].reshape(3, HEADS, HD).transpose(1, 0, 2).reshape(HEADS, 3 * HD)
    up_cols = vec[2].reshape(FF // HEADS, HEADS).T
    used = qkv_cols.shape[1] + up_cols.shape[1]
    mixed_row = jnp.concatenate([qkv_cols, up_cols, jnp.zeros((HEADS, D - used), bf16)], axis=1)
    mixed_row = mixed_row[:, None]
    full = jnp.concatenate(
        [vec[1] + vec[3][:1], vec[3][1:], jnp.zeros((lay.slots - lay.units - 7, D), bf16)], axis=0
    )
    full = jnp.broadcast_to(full[None], (HEADS,) + full.shape)
    tail = jnp.concatenate([mixed_row, full], axis=1).reshape(HEADS, -1, LANES)
    parts = jnp.concatenate([body, tail], axis=1)
    wide = lay.share * SUB
    share = lax.dynamic_slice_in_dim(parts, rep_id * wide, wide, axis=1)
    seg_row = jnp.pad(segment.astype(bf16), (0, D - segment.shape[0]))
    seg_row = jnp.broadcast_to(seg_row.reshape(1, SUB, LANES), (HEADS, SUB, LANES))
    return jnp.concatenate([share, seg_row], axis=1)


def take_params(lay, got, shard_id, rep_id):
    got = all_shares(lay, got, rep_id).reshape(lay.ways, lay.slots, SUB, LANES)
    if lay.packs > 1:
        packs = [got] + [
            lax.ppermute(got, "shard", lay.xor(lay.ways * k)) for k in range(1, lay.packs)
        ]
        order = jnp.arange(lay.packs, dtype=jnp.int32) ^ (shard_id // lay.ways)
        got = jnp.take(jnp.stack(packs), order, axis=0)
        got = got.reshape(lay.n, lay.slots, SUB, LANES)
    carry = got[:-1, lay.units : lay.units + 1]
    carry = jnp.concatenate([jnp.zeros_like(carry[:1]), carry], axis=0)
    units = jnp.concatenate([got[:, :1] + carry, got[:, 1 : lay.units]], axis=1)
    units = units.reshape(MAT_ROWS // UNIT, SUB, LANES)
    w_qkv = units[: QKV_END // UNIT].reshape(D, 3 * HD)
    w_up = units[OUT_END // UNIT : UP_END // UNIT].reshape(D, FF // HEADS)
    w_down = units[UP_END // UNIT :].reshape(FF // HEADS, D)
    out_rows = units[QKV_END // UNIT : OUT_END // UNIT]
    w_out = exchange(lay, out_rows.reshape(HEADS, HD // HEADS, D))
    w_out = w_out.transpose(1, 0, 2).reshape(HD, D)
    extra = jnp.sum(got[:, lay.units + 1 : lay.units + 7].astype(f32), axis=0).reshape(6, D)
    b_qkv = extra[0, : 3 * HD]
    b_up = extra[0, 3 * HD : 3 * HD + FF // HEADS]
    return w_qkv, b_qkv, w_out, w_up, b_up, w_down, extra[1:]


def share_sum(lay, parts, rep_id):
    by_rep = parts.reshape(parts.shape[0], lay.reps, lay.share, D)
    total = lax.dynamic_index_in_dim(by_rep, rep_id, axis=1, keepdims=False).astype(f32)
    for k in range(1, lay.reps):
        theirs = lax.dynamic_index_in_dim(by_rep, rep_id ^ k, axis=1, keepdims=False)
        total = total + lax.ppermute(theirs, "rep", lay.rep_xor(k)).astype(f32)
    return total.astype(bf16)


def windows(lay, units, first, last):
    body = units[: (last - first) * lay.units].reshape(last - first, lay.units, D)
    after = units[lay.units :: lay.units][: last - first, None]
    short = last - first - after.shape[0]
    after = jnp.pad(after, ((0, short), (0, 0), (0, 0)))
    room = jnp.zeros((last - first, lay.slots - lay.units - 1, D), bf16)
    return jnp.concatenate([body, after, room], axis=1)


def own_share(lay, late, early, mixed_row, full, shard_id, rep_id):
    total = jnp.concatenate([late, early], axis=0)
    tail = jnp.concatenate([mixed_row[None], full], axis=0)
    for k in [2**i for i in range((lay.reps - 1).bit_length())]:
        tail = tail + lax.ppermute(tail.astype(bf16), "rep", lay.rep_xor(k)).astype(f32)
    tail = jnp.pad(tail, ((lay.units + 1, lay.slots - lay.units - 7), (0, 0))).astype(bf16)
    tail = lax.dynamic_slice_in_dim(tail, rep_id * lay.share, lay.share, axis=0)
    total = total + tail[None]
    if lay.packs > 1:
        pack_id = shard_id // lay.ways
        by_pack = total.reshape(lay.packs, lay.ways, lay.share, D)
        total = lax.dynamic_index_in_dim(by_pack, pack_id, keepdims=False).astype(f32)
        for k in range(1, lay.packs):
            theirs = lax.dynamic_index_in_dim(by_pack, pack_id ^ k, keepdims=False)
            total = total + lax.ppermute(theirs, "shard", lay.xor(lay.ways * k)).astype(f32)
        total = total.astype(bf16)
    return total


def all_shares(lay, got, rep_id):
    got = [got] + [lax.ppermute(got, "rep", lay.rep_xor(k)) for k in range(1, lay.reps)]
    if lay.reps == 2:
        got = [jnp.where(rep_id == r, got[0], got[1]) for r in range(2)]
        return jnp.concatenate(got, axis=1)
    got = jnp.take(jnp.stack(got), jnp.arange(lay.reps, dtype=jnp.int32) ^ rep_id, axis=0)
    return jnp.moveaxis(got, 0, 1).reshape(got.shape[1], -1, got.shape[-1])


def owner_part(lay, got, shard_id):
    body = got[:, : lay.units + 1].reshape(lay.ways, -1, LANES)
    extra = got[:, lay.units + 1 : lay.units + 7].astype(f32)
    qkv_vec = extra[:, 0, : 3 * HD].reshape(HEADS, 3, HD).transpose(1, 0, 2).reshape(3 * D)
    up_vec = extra[:, 0, 3 * HD : 3 * HD + FF // HEADS].T.reshape(FF)
    norm_vec = jnp.sum(extra[:, 1:5], axis=0).reshape(4 * D)
    out_vec = extra[0, 5]
    small = jnp.concatenate([qkv_vec, out_vec, up_vec, out_vec, norm_vec])
    table = jnp.asarray(lay.tables)[shard_id]
    size = (MAT_ROWS + VEC_ROWS) * D // lay.n
    flat = unpack(
        body, shard_id * lay.units, PAD + table[0], PAD + table[1], table[3]
    )
    flat = flat.reshape(-1)[:size]
    run = 5 * D
    start = jnp.clip(table[3], 0, size - run)
    ids = start + lax.iota(jnp.int32, run)
    from_small = jnp.clip(start - table[5], -run, VEC_ROWS * D) + run
    vec = lax.dynamic_slice(jnp.pad(small, (run, run)), (from_small,), (run,))
    old = lax.dynamic_slice(flat, (start,), (run,))
    new = jnp.where((ids >= table[3]) & (ids < table[4]), vec, old)
    return lax.dynamic_update_slice(flat, new, (start,))


def per_device(lay, tokens, cotangent, segment, params, first_moment, second_moment):
    shard_id = lax.axis_index("shard")
    rep_id = lax.axis_index("rep")
    me = shard_id % lay.ways
    length = tokens.shape[0]
    blocks = lay.ways
    total_rows = blocks * length

    own_grad = jnp.where((segment >= 0)[:, None], cotangent, jnp.zeros_like(cotangent))
    block = jnp.concatenate([tokens, own_grad], axis=1)
    start = gather_start(lay, block)
    cuts = cut_windows(lay, params, shard_id)
    cuts, start = lax.optimization_barrier((cuts, start))
    chain, across = gather_line(lay, [block, start[0]], [start[1]])
    offer = offer_params(lay, cuts, params.shape[0], segment, shard_id, rep_id)
    offer, chain, across = lax.optimization_barrier((offer, chain, across))
    got = exchange(lay, offer)
    while len(chain) < lay.line:
        chain, across = gather_line(lay, chain, across)
    got, chain[-1] = lax.optimization_barrier((got, chain[-1]))
    seg_all = got[:, lay.share * SUB].astype(f32)
    w_qkv, b_qkv, w_out, w_up, b_up, w_down, full = take_params(
        lay, got[:, : lay.share * SUB], shard_id, rep_id
    )
    rows = gather_end(lay, chain, across)
    b_sum = full[0]
    spot = jnp.arange(blocks, dtype=jnp.int32)
    d_core, d_line, d_row = spot // (2 * lay.line), spot // 2 % lay.line, spot % 2
    source = (
        (me // 4 - d_line) % lay.line * 4 + ((me // 2 % 2) ^ d_row) * 2 + ((me % 2) ^ d_core)
    )
    seg = jnp.take(seg_all, source, axis=0)

    bias = jnp.pad(jnp.stack([jnp.pad(b_qkv, (0, HD)), b_up]), ((0, 6), (0, 0)))
    vec = jnp.pad(full, ((0, 8 - full.shape[0]), (0, 0)))
    *sums, grad_qkv, units_feed, grad_w_out, bias_sums, vec_sums = layer(
        rows,
        seg,
        turn_table(),
        jnp.pad(w_qkv, ((0, 0), (0, HD))),
        w_up,
        w_down,
        jnp.pad(w_out, ((0, LANES - HD), (0, 0))),
        bias,
        vec,
    )
    own = tokens.astype(f32)
    own_center = own - jnp.mean(own, axis=-1, keepdims=True)
    own_inverse = lax.rsqrt(jnp.mean(own_center * own_center, axis=-1, keepdims=True) + norm_eps)
    own_hat = own_center * own_inverse
    grad_w_qkv = grad_qkv[:, : 3 * HD]
    first = QKV_END // UNIT // lay.units - 1
    cut = -(-OUT_END // UNIT // lay.units)
    units_qkv = grad_w_qkv.reshape(QKV_END // UNIT, D)
    early = jnp.concatenate(
        [
            windows(lay, units_qkv[: first * lay.units + 1], 0, first),
            windows(lay, units_feed[cut * lay.units - OUT_END // UNIT :], cut, lay.n),
        ],
        axis=0,
    )
    early = share_sum(lay, early, rep_id)
    back = grad_w_out[:HD].reshape(HD // HEADS, HEADS, D).transpose(1, 0, 2)
    back = exchange(lay, back).reshape(HD, D)
    units = jnp.concatenate(
        [units_qkv[first * lay.units :], back, units_feed[: (cut + 1) * lay.units]], axis=0
    )
    late = windows(lay, units[: (cut - first) * lay.units + 1], first, cut)
    late = share_sum(lay, late, rep_id)
    late = jnp.concatenate([early[:first], late], axis=0)
    early = early[first:]
    used = 3 * HD + FF // HEADS
    mixed_row = jnp.concatenate(
        [bias_sums[0, : 3 * HD], bias_sums[1], jnp.zeros((D - used,), f32)]
    )
    vectors = vec_sums[:5]
    share = own_share(lay, late, early, mixed_row, vectors, shard_id, rep_id)

    kept, sent = scatter_planes(lay, sums, length)
    top = lay.line - 1
    share, sent[top] = lax.optimization_barrier((share, sent[top]))
    got = exchange(lay, share)
    total = scatter_step(lay, None, kept, sent, top)
    total = scatter_step(lay, total, kept, sent, top - 1)
    got, total = lax.optimization_barrier((got, total))
    got = all_shares(lay, got, rep_id)
    for d in range(top - 2, 0, -1):
        total = scatter_step(lay, total, kept, sent, d)
    got, total = lax.optimization_barrier((got, total))
    grad_total = owner_part(lay, got, shard_id)
    sums = scatter_step(lay, total, kept, sent, 0)
    out_sum, g_sum = sums[:, :D], sums[:, D:]
    out_rows = (tokens.astype(f32) + out_sum + b_sum).astype(bf16)
    grad_rows = (
        own_grad.astype(f32)
        + own_inverse
        * (
            g_sum
            - jnp.mean(g_sum, axis=-1, keepdims=True)
            - own_hat * jnp.mean(g_sum * own_hat, axis=-1, keepdims=True)
        )
    ).astype(bf16)

    new_weights, first_new, second_new = adam_update(
        params, first_moment, second_moment, grad_total
    )
    return (out_rows, grad_rows, grad_total, new_weights, first_new, second_new)


def solution(mesh):
    lay = Layout(mesh)
    in_specs = (
        P(("rep", "shard"), None),
        P(("rep", "shard"), None),
        P(("rep", "shard")),
        P("shard"),
        P("shard"),
        P("shard"),
    )
    out_specs = (
        P(("rep", "shard"), None),
        P(("rep", "shard"), None),
        P("shard"),
        P("shard"),
        P("shard"),
        P("shard"),
    )

    def body(*args):
        return per_device(lay, *args)

    return jax.shard_map(body, mesh=mesh, in_specs=in_specs, out_specs=out_specs, check_vma=False)
```

```python
import jax
import jax.numpy as jnp
import numpy as np
from jax import lax
from jax.experimental import pallas as pl
from jax.experimental.pallas import tpu as pltpu
from jax.sharding import PartitionSpec as P


D = 1024
HEADS = 16
HD = 64
ROT = 16
FF = 4096
STEP = 4
UNIT = HEADS

norm_eps = 1e-05
adam_eps = 1e-08
beta_one = 0.9
beta_two = 0.999
learn_rate = 0.003
decay_rate = 0.1
root_half = 0.7071067811865476
inv_root_twopi = 0.3989422804014327


QKV_END = 3 * D
OUT_END = QKV_END + D
UP_END = OUT_END + FF
DOWN_END = UP_END + FF
MAT_ROWS = DOWN_END
SECTIONS = ((0, QKV_END, 0), (QKV_END, OUT_END, 3), (OUT_END, UP_END, 4), (UP_END, DOWN_END, 8))
RUNS = (
    (QKV_END, 3, 0),
    (OUT_END + 3, 1, 3),
    (UP_END + 4, 4, 4),
    (DOWN_END + 8, 5, 8),
)
VEC_ROWS = 13
PAD = 8 * D

f32 = jnp.float32
bf16 = jnp.bfloat16


def owner_tables(owners):
    total = (MAT_ROWS + VEC_ROWS) * D
    part = total // owners
    lead = VEC_ROWS * D // owners
    rows = []
    for s in range(owners):
        start = s * part
        first = next((i for i, (a, b, v) in enumerate(SECTIONS) if (b + v) * D > start), 3)
        second = min(first + 1, 3)
        run_row, run_len, vec_row = RUNS[first]
        run_a = min(max(run_row * D - start, 0), part)
        run_b = min(max((run_row + run_len) * D - start, 0), part)
        rows.append(
            (
                lead * s - SECTIONS[first][2] * D,
                lead * s - SECTIONS[second][2] * D,
                (SECTIONS[first][1] - (MAT_ROWS // owners) * s) if first < 3 else 2 * MAT_ROWS,
                run_a,
                run_b,
                run_row * D - start - vec_row * D,
            )
        )
    return np.array(rows, np.int32)


def adam_update(weights, moment_one, moment_two, grad_total):
    first_new = beta_one * moment_one + (1.0 - beta_one) * grad_total
    second_new = beta_two * moment_two + (1.0 - beta_two) * grad_total * grad_total
    correct_one = 1.0 - beta_one**STEP
    correct_two = 1.0 - beta_two**STEP
    change = first_new / correct_one / (jnp.sqrt(second_new / correct_two) + adam_eps)
    return (weights - learn_rate * (change + decay_rate * weights), first_new, second_new)


class Layout:
    def __init__(self, mesh):
        self.n = mesh.shape["shard"]
        self.reps = mesh.shape["rep"]
        self.ways = HEADS
        assert self.n % self.ways == 0
        self.packs = self.n // self.ways
        self.core, self.row = 2, 2
        self.line = self.ways // 4
        self.units = MAT_ROWS // UNIT // self.n
        slots = self.units + 1 + 1 + 5
        self.slots = -(-slots // self.reps) * self.reps
        self.share = self.slots // self.reps
        self.tables = owner_tables(self.n)

    def xor(self, k):
        return [(i, i ^ k) for i in range(self.n)]

    def step(self, k):
        w = self.ways
        return [(i, i - i % w + (i % w + 4 * k) % w) for i in range(self.n)]

    def rep_xor(self, k):
        return [(i, i ^ k) for i in range(self.reps)]


def gather_start(lay, block):
    along = lax.ppermute(block, "shard", lay.step(1))
    return along, lax.ppermute(block, "shard", lay.xor(2))


def gather_line(lay, chain, across):
    along = lax.ppermute(chain[-1], "shard", lay.step(1))
    return chain + [along], across + [lax.ppermute(chain[-1], "shard", lay.xor(2))]


def gather_end(lay, chain, across):
    across = across + [lax.ppermute(chain[-1], "shard", lay.xor(2))]
    plane = [piece for pair in zip(chain, across) for piece in pair]
    near, far = (
        jnp.concatenate(plane[i : i + lay.line], axis=0) for i in range(0, 2 * lay.line, lay.line)
    )
    return near, far, *(lax.ppermute(half, "shard", lay.xor(1)) for half in (near, far))


def scatter_planes(lay, quarters, length):
    near, far, other_near, other_far = quarters
    kept, sent = {}, {}
    for base, own, other in ((lay.line // 2, far, other_far), (0, near, other_near)):
        came = lax.ppermute(other, "shard", lay.xor(1))
        for d in range(lay.line // 2 - 1, -1, -1):
            at = slice(2 * d * length, (2 * d + 1) * length)
            to = slice((2 * d + 1) * length, (2 * d + 2) * length)
            kept[base + d] = own[at].astype(f32) + came[at].astype(f32)
            leaving = (own[to].astype(f32) + came[to].astype(f32)).astype(bf16)
            sent[base + d] = lax.ppermute(leaving, "shard", lay.xor(2))
    return kept, sent


def scatter_step(lay, total, kept, sent, d):
    mine = kept[d] + sent[d].astype(f32)
    if total is None:
        return mine
    return mine + lax.ppermute(total.astype(bf16), "shard", lay.step(-1)).astype(f32)


def exchange(lay, parts):
    groups = [list(range(p * lay.ways, (p + 1) * lay.ways)) for p in range(lay.packs)]
    return lax.all_to_all(
        parts, "shard", 0, 0, axis_index_groups=groups if lay.packs > 1 else None, tiled=True
    )


LANES = 128
SUB = D // LANES
TILE = 256
VMEM_LIMIT = 56 * 1024 * 1024


def spread_matrix():
    row = lax.broadcasted_iota(jnp.int32, (D, D), 0)
    col = lax.broadcasted_iota(jnp.int32, (D, D), 1)
    return jnp.where(row == (col % HD) * HEADS + col // HD, 1.0, 0.0).astype(bf16)


def unit_masks(first_unit, amount):
    unit = lax.broadcasted_iota(jnp.int32, (amount, LANES), 0) // SUB + first_unit
    is_up = (unit >= OUT_END // UNIT) & (unit < UP_END // UNIT)
    by_row = ((unit >= QKV_END // UNIT) & (unit < OUT_END // UNIT)) | (unit >= UP_END // UNIT)
    return is_up, by_row


def pack_kernel(info_ref, first_ref, second_ref, out_ref, x_ref):
    rows = first_ref.shape[0]
    amount = rows // UNIT
    ids = lax.broadcasted_iota(jnp.int32, (LANES, LANES), 0)

    def strip(i, carry):
        begin = pl.multiple_of(i * LANES, LANES)
        at = pl.ds(begin, LANES)
        x_ref[at, :] = jnp.where(
            ids < info_ref[0] - begin, first_ref[at, :].astype(f32), second_ref[at, :].astype(f32)
        )
        return carry

    lax.fori_loop(0, rows // LANES, strip, 0)
    is_up, by_row = unit_masks(info_ref[1], amount)
    low = lax.broadcasted_iota(jnp.int32, (amount, LANES), 1) < HD
    spread = spread_matrix()
    halves = []
    for p in range(2):
        cols = [x_ref[pl.ds(SUB * p + a, amount, stride=UNIT), :] for a in range(SUB)]
        moved = jnp.dot(
            jnp.concatenate(cols, axis=1).astype(bf16), spread, preferred_element_type=f32
        )
        halves.append(
            [
                jnp.where(is_up, moved[:, a * LANES : (a + 1) * LANES], cols[a])
                for a in range(SUB)
            ]
        )
    whole = x_ref[...].reshape(amount // SUB, UNIT, SUB, LANES)
    for t in range(HEADS):
        zero, one = halves[0][t // 2], halves[1][t // 2]
        if t % 2 == 0:
            piece = jnp.where(low, zero, pltpu.roll(one, HD, 1))
        else:
            piece = jnp.where(low, pltpu.roll(zero, HD, 1), one)
        direct = whole[:, t].reshape(amount, LANES)
        out_ref[t] = jnp.where(by_row, direct, piece).astype(bf16)


def pack(first, second, bound, first_unit):
    rows = first.shape[0]
    return pl.pallas_call(
        pack_kernel,
        out_shape=jax.ShapeDtypeStruct((HEADS, rows // UNIT, LANES), bf16),
        in_specs=[
            pl.BlockSpec(memory_space=pltpu.SMEM),
            pl.BlockSpec(memory_space=pltpu.VMEM),
            pl.BlockSpec(memory_space=pltpu.VMEM),
        ],
        out_specs=pl.BlockSpec(memory_space=pltpu.VMEM),
        scratch_shapes=[pltpu.VMEM((rows, LANES), f32)],
        compiler_params=pltpu.CompilerParams(vmem_limit_bytes=VMEM_LIMIT),
        cost_estimate=pl.CostEstimate(
            flops=2 * rows * LANES * D, bytes_accessed=6 * rows * LANES, transcendentals=0
        ),
        name="pack",
    )(jnp.stack([bound, first_unit]).astype(jnp.int32), first, second)


MARGIN = 64


def unpack_kernel(info_ref, got_ref, out_ref, x_ref):
    amount = got_ref.shape[1]
    rows = amount * UNIT
    is_up, by_row = unit_masks(info_ref[0], amount)
    low = lax.broadcasted_iota(jnp.int32, (amount, LANES), 1) < HD
    spread = spread_matrix()
    x_ref[pl.ds(0, MARGIN), :] = jnp.zeros((MARGIN, LANES), f32)
    x_ref[pl.ds(MARGIN + rows, 2 * MARGIN), :] = jnp.zeros((2 * MARGIN, LANES), f32)
    for p in range(2):
        cols = []
        for a in range(SUB):
            even, odd = got_ref[2 * a].astype(f32), got_ref[2 * a + 1].astype(f32)
            if p == 0:
                cols.append(jnp.where(low, even, pltpu.roll(odd, HD, 1)))
            else:
                cols.append(jnp.where(low, pltpu.roll(even, HD, 1), odd))
        moved = lax.dot_general(
            jnp.concatenate(cols, axis=1).astype(bf16),
            spread,
            (((1,), (1,)), ((), ())),
            preferred_element_type=f32,
        )
        for a in range(SUB):
            x_ref[pl.ds(MARGIN + SUB * p + a, amount, stride=UNIT), :] = jnp.where(
                is_up, moved[:, a * LANES : (a + 1) * LANES], cols[a]
            )
    whole = x_ref[pl.ds(MARGIN, rows), :].reshape(amount // SUB, UNIT, SUB, LANES)
    keep = by_row.reshape(amount // SUB, SUB, LANES)
    mixed = [
        jnp.where(keep, got_ref[t].astype(f32).reshape(amount // SUB, SUB, LANES), whole[:, t])
        for t in range(HEADS)
    ]
    x_ref[pl.ds(MARGIN, rows), :] = jnp.stack(mixed, axis=1).reshape(rows, LANES)
    strips = out_ref.shape[0] // LANES
    length = LANES * next(k for k in (7, 5, 4, 3, 2, 1) if strips % k == 0)
    low = lax.broadcasted_iota(jnp.int32, (length, LANES), 1) < HD
    place = 2 * lax.broadcasted_iota(jnp.int32, (length, LANES), 0) + jnp.where(low, 0, 1)

    def strip(i, carry):
        begin = pl.multiple_of(i * length, LANES)

        def cut(start):
            here = x_ref[pl.ds(start // 2 + begin, length), :]
            after = x_ref[pl.ds(start // 2 + begin + 1, length), :]
            split = jnp.where(low, pltpu.roll(here, HD, 1), pltpu.roll(after, HD, 1))
            return jnp.where(start % 2 == 1, split, here)

        out_ref[pl.ds(begin, length), :] = jnp.where(
            place < info_ref[3] - 2 * begin, cut(info_ref[1]), cut(info_ref[2])
        )
        return carry

    lax.fori_loop(0, out_ref.shape[0] // length, strip, 0)


def unpack(got, first_unit, start_one, start_two, bound):
    amount = got.shape[1]
    info = jnp.stack([first_unit, start_one // HD, start_two // HD, bound // HD])
    return pl.pallas_call(
        unpack_kernel,
        out_shape=jax.ShapeDtypeStruct((amount * UNIT, LANES), f32),
        in_specs=[
            pl.BlockSpec(memory_space=pltpu.SMEM),
            pl.BlockSpec(memory_space=pltpu.VMEM),
        ],
        out_specs=pl.BlockSpec(memory_space=pltpu.VMEM),
        scratch_shapes=[pltpu.VMEM((amount * UNIT + 3 * MARGIN, LANES), f32)],
        compiler_params=pltpu.CompilerParams(vmem_limit_bytes=VMEM_LIMIT),
        cost_estimate=pl.CostEstimate(
            flops=2 * amount * UNIT * LANES * D, bytes_accessed=6 * amount * UNIT * LANES, transcendentals=0
        ),
        name="unpack",
    )(info.astype(jnp.int32), got)


def nt(a, b):
    return lax.dot_general(a, b, (((1,), (1,)), ((), ())), preferred_element_type=f32)


def tn(a, b):
    return lax.dot_general(a, b, (((0,), (0,)), ((), ())), preferred_element_type=f32)


def nn(a, b):
    return lax.dot_general(a, b, (((1,), (0,)), ((), ())), preferred_element_type=f32)


QUARTERS = 4


STRIP = 64


def move_tile(refs, tile_ref, inward):
    quarter = pl.program_id(0) // (pl.num_programs(0) // QUARTERS)
    for q in range(QUARTERS):
        source, target = (refs[q], tile_ref) if inward else (tile_ref, refs[q])

        @pl.when(quarter == q)
        def _():
            def strip(i, carry):
                at = pl.ds(pl.multiple_of(i * STRIP, STRIP), STRIP)
                target[at, :] = source[at, :]
                return carry

            lax.fori_loop(0, TILE // STRIP, strip, 0)


def layer_kernel(*refs):
    rows_refs, sums_refs = refs[:4], refs[12:16]
    seg_ref, table_ref, w_qkv_ref, w_up_ref, w_down_ref, w_out_ref, bias_ref, vec_ref = refs[4:12]
    gqkv_ref, gfeed_ref, gout_ref, gbias_ref, gvec_ref = refs[16:21]
    aqkv, aup_low, aup_high, adown, aout, tile, sums = refs[21:]
    step = pl.program_id(0)

    @pl.when(step == 0)
    def _():
        for ref in (aqkv, aup_low, aup_high, adown, aout, gbias_ref, gvec_ref):
            ref[...] = jnp.zeros(ref.shape, ref.dtype)

    length = seg_ref.shape[1]
    wide = 2 * LANES
    move_tile(rows_refs, tile, True)
    x = tile[:, :D].astype(f32)
    center = x - jnp.mean(x, axis=1, keepdims=True)
    inverse = lax.rsqrt(jnp.mean(center * center, axis=1, keepdims=True) + norm_eps)
    hat = center * inverse
    go = tile[:, D:]
    gain_one, shift_one = vec_ref[1:2, :], vec_ref[2:3, :]
    gain_two, shift_two = vec_ref[3:4, :], vec_ref[4:5, :]
    in_one = (hat * gain_one + shift_one).astype(bf16)
    in_two = (hat * gain_two + shift_two).astype(bf16)
    hidden = nn(in_two, w_up_ref[...]) + bias_ref[1:2, :]
    cdf = 0.5 * (1.0 + lax.erf(hidden * root_half))
    active = (hidden * cdf).astype(bf16)
    slope = cdf + hidden * jnp.exp(-0.5 * hidden * hidden) * inv_root_twopi
    ghid = nt(go, w_down_ref[...]) * slope
    ghid_bf = ghid.astype(bf16)
    low_rot = lax.broadcasted_iota(jnp.int32, (TILE, wide), 1) % HD < ROT // 2
    low = lax.broadcasted_iota(jnp.int32, (length, LANES), 1) < HD
    row_id = lax.broadcasted_iota(jnp.int32, (length, length), 0)
    col_id = lax.broadcasted_iota(jnp.int32, (length, length), 1)
    spot = lax.broadcasted_iota(jnp.int32, (length, wide), 1).astype(f32)
    rows_f = lax.broadcasted_iota(jnp.int32, (length, 1), 0).astype(f32)

    masks, picks = [], []
    for b in range(TILE // length):
        seg_row = seg_ref[pl.ds(step * (TILE // length) + b, 1), :]
        seg_col = jnp.sum(jnp.where(row_id == col_id, seg_row, 0.0), axis=1, keepdims=True)
        masks.append(jnp.where((seg_col == seg_row) & (col_id <= row_id), 0.0, -1e30))
        picks.append(jnp.where(spot == rows_f - seg_col, 1.0, 0.0).astype(bf16))
    pick = jnp.concatenate(picks, axis=0)
    cosine = nn(pick, table_ref[0]) + nn(pick, table_ref[1])
    sine = nn(pick, table_ref[2]) + nn(pick, table_ref[3])

    def swap(v):
        ahead = pltpu.roll(v, wide - ROT // 2, 1)
        return jnp.where(low_rot, ahead, pltpu.roll(v, ROT // 2, 1))

    mixed = nn(in_one, w_qkv_ref[...]) + bias_ref[0:1, :]
    rot = mixed * cosine + swap(mixed) * sine
    gheads = nt(go, w_out_ref[...]).astype(bf16)
    scale = HD ** (-0.5)
    heads, gmix = [], []
    for b in range(TILE // length):
        part = slice(b * length, (b + 1) * length)
        qk = rot[part, :LANES]
        vv = rot[part, LANES:].astype(bf16)
        turned = pltpu.roll(qk, HD, 1)
        q_low = jnp.where(low, qk, 0.0).astype(bf16)
        k_low = jnp.where(low, turned, 0.0).astype(bf16)
        q_high = jnp.where(low, 0.0, turned).astype(bf16)
        gh = gheads[part]
        scores = nt(q_low, k_low) * scale + masks[b]
        expd = jnp.exp(scores - jnp.max(scores, axis=1, keepdims=True))
        probs = expd / jnp.sum(expd, axis=1, keepdims=True)
        probs_bf = probs.astype(bf16)
        head = nn(probs_bf, vv).astype(bf16)
        heads.append(head)
        delta = jnp.sum(gh.astype(f32) * head.astype(f32), axis=1, keepdims=True)
        gs = (probs * (nt(gh, vv) - delta) * scale).astype(bf16)
        gqk = nn(gs, k_low) + tn(gs, q_high)
        gv = tn(probs_bf, gh)
        gmix.append(jnp.concatenate([gqk, gv], axis=1))
    head = jnp.concatenate(heads, axis=0)
    gmix = jnp.concatenate(gmix, axis=0)
    gmix = gmix * cosine - swap(gmix) * sine
    gmix_bf = gmix.astype(bf16)

    sums[:, :D] = (nn(head, w_out_ref[...]) + nn(active, w_down_ref[...])).astype(bf16)
    norm_one = nt(gmix_bf, w_qkv_ref[...])
    norm_two = nt(ghid_bf, w_up_ref[...])
    sums[:, D:] = (norm_one * gain_one + norm_two * gain_two).astype(bf16)
    gvec_ref[0:1, :] += jnp.sum(norm_one * hat, axis=0, keepdims=True)
    gvec_ref[1:2, :] += jnp.sum(norm_one, axis=0, keepdims=True)
    gvec_ref[2:3, :] += jnp.sum(norm_two * hat, axis=0, keepdims=True)
    gvec_ref[3:4, :] += jnp.sum(norm_two, axis=0, keepdims=True)
    gvec_ref[4:5, :] += jnp.sum(go.astype(f32), axis=0, keepdims=True)
    gbias_ref[0:1, :] += jnp.sum(gmix, axis=0, keepdims=True)
    gbias_ref[1:2, :] += jnp.sum(ghid, axis=0, keepdims=True)
    aqkv[...] += tn(in_one, gmix_bf)
    for half, ref in enumerate((aup_low, aup_high)):
        ref[...] += tn(in_two, ghid_bf[:, half * LANES : (half + 1) * LANES])
    adown[...] += tn(active, go)
    aout[...] += tn(head, go)
    move_tile(sums_refs, sums, False)

    @pl.when(step == pl.num_programs(0) - 1)
    def _():
        gqkv_ref[...] = aqkv[...].astype(bf16)
        cols = FF // HEADS
        for k in range(D // cols):
            for half, ref in enumerate((aup_low, aup_high)):
                rows = ref[pl.ds(k, cols, stride=D // cols), :]
                lanes = pl.ds(k * cols + half * LANES, LANES)
                gfeed_ref[pl.ds(0, cols), lanes] = rows.astype(bf16)
        gfeed_ref[pl.ds(cols, cols), :] = adown[...].astype(bf16)
        gout_ref[...] = aout[...].astype(bf16)


def quarter_tiles(width, count):
    def spec(q):
        return pl.BlockSpec((TILE, width), lambda i: (jnp.clip(i - q * count, 0, count - 1), 0))

    return [spec(q) for q in range(QUARTERS)]


def whole(*shape):
    return pl.BlockSpec(shape, lambda i: (0,) * len(shape))


def layer(rows, seg, table, w_qkv, w_up, w_down, w_out, bias, vec):
    count = rows[0].shape[0] // TILE
    wide = 2 * LANES
    cols = FF // HEADS
    weights = [(D, wide), (D, cols), (cols, D), (LANES, D)]
    grads = [(D, wide), (2 * cols, D), (LANES, D)]
    small = [(8, wide), (8, D)]
    return pl.pallas_call(
        layer_kernel,
        grid=(QUARTERS * count,),
        in_specs=[
            *quarter_tiles(2 * D, count),
            whole(*seg.shape),
            whole(*table.shape),
            *[whole(*shape) for shape in weights + small],
        ],
        out_specs=[
            *quarter_tiles(2 * D, count),
            *[whole(*shape) for shape in grads + small],
        ],
        out_shape=[
            *[jax.ShapeDtypeStruct(rows[0].shape, bf16)] * QUARTERS,
            *[jax.ShapeDtypeStruct(shape, bf16) for shape in grads],
            *[jax.ShapeDtypeStruct(shape, f32) for shape in small],
        ],
        scratch_shapes=[
            pltpu.VMEM((D, wide), f32),
            *[pltpu.VMEM((D, LANES), f32)] * 2,
            pltpu.VMEM((cols, D), f32),
            pltpu.VMEM((LANES, D), f32),
            *[pltpu.VMEM((TILE, 2 * D), bf16)] * 2,
        ],
        compiler_params=pltpu.CompilerParams(vmem_limit_bytes=VMEM_LIMIT),
        cost_estimate=pl.CostEstimate(
            flops=24 * QUARTERS * rows[0].shape[0] * D * FF // HEADS,
            bytes_accessed=4 * QUARTERS * rows[0].size,
            transcendentals=0,
        ),
        name="layer",
    )(*rows, seg, table, w_qkv, w_up, w_down, w_out, bias, vec)


def turn_table():
    wide = 2 * LANES
    lane = jnp.arange(wide)
    inner = lane % HD
    turns = (inner < ROT) & (lane < 2 * HD)
    frequency = 10000.0 ** (-2.0 * (lane % (ROT // 2)).astype(f32) / ROT)
    phase = jnp.arange(wide, dtype=f32)[:, None] * frequency[None]
    cosine = jnp.where(turns, jnp.cos(phase), 1.0)
    sine = jnp.where(turns, jnp.where(inner < ROT // 2, -1.0, 1.0) * jnp.sin(phase), 0.0)
    out = []
    for values in (cosine, sine):
        top = lax.reduce_precision(values, 8, 7)
        out += [top.astype(bf16), (values - top).astype(bf16)]
    return jnp.stack(out)


def cut_windows(lay, params, shard_id):
    table = jnp.asarray(lay.tables)[shard_id]
    rows = (lay.units + 1) * UNIT
    chunk = params.astype(bf16)
    padded = jnp.pad(chunk, (PAD, rows * D + 2 * PAD - chunk.shape[0]))
    first = lax.dynamic_slice(padded, (PAD - table[0],), (rows * D,)).reshape(rows * SUB, LANES)
    second = lax.dynamic_slice(padded, (PAD - table[1],), (rows * D,)).reshape(rows * SUB, LANES)
    return padded, first, second


def offer_params(lay, cuts, size, segment, shard_id, rep_id):
    table = jnp.asarray(lay.tables)[shard_id]
    padded, first, second = cuts
    body = pack(first, second, table[2] * SUB, shard_id * lay.units)
    vec = []
    for flat_row, amount, _ in RUNS:
        start = flat_row * D - shard_id * size
        begin = jnp.clip(start, -PAD, size)
        piece = lax.dynamic_slice(padded, (PAD + begin,), (amount * D,))
        vec.append(jnp.where(start == begin, piece, 0).reshape(amount, D))
    qkv_cols = vec[0].reshape(3, HEADS, HD).transpose(1, 0, 2).reshape(HEADS, 3 * HD)
    up_cols = vec[2].reshape(FF // HEADS, HEADS).T
    used = qkv_cols.shape[1] + up_cols.shape[1]
    mixed_row = jnp.concatenate([qkv_cols, up_cols, jnp.zeros((HEADS, D - used), bf16)], axis=1)
    mixed_row = mixed_row[:, None]
    full = jnp.concatenate(
        [vec[1] + vec[3][:1], vec[3][1:], jnp.zeros((lay.slots - lay.units - 7, D), bf16)], axis=0
    )
    full = jnp.broadcast_to(full[None], (HEADS,) + full.shape)
    tail = jnp.concatenate([mixed_row, full], axis=1).reshape(HEADS, -1, LANES)
    parts = jnp.concatenate([body, tail], axis=1)
    wide = lay.share * SUB
    share = lax.dynamic_slice_in_dim(parts, rep_id * wide, wide, axis=1)
    seg_row = jnp.pad(segment.astype(bf16), (0, D - segment.shape[0]))
    seg_row = jnp.broadcast_to(seg_row.reshape(1, SUB, LANES), (HEADS, SUB, LANES))
    return jnp.concatenate([share, seg_row], axis=1)


def take_params(lay, got, shard_id, rep_id):
    got = all_shares(lay, got, rep_id).reshape(lay.ways, lay.slots, SUB, LANES)
    if lay.packs > 1:
        packs = [got] + [
            lax.ppermute(got, "shard", lay.xor(lay.ways * k)) for k in range(1, lay.packs)
        ]
        order = jnp.arange(lay.packs, dtype=jnp.int32) ^ (shard_id // lay.ways)
        got = jnp.take(jnp.stack(packs), order, axis=0)
        got = got.reshape(lay.n, lay.slots, SUB, LANES)
    carry = got[:-1, lay.units : lay.units + 1]
    carry = jnp.concatenate([jnp.zeros_like(carry[:1]), carry], axis=0)
    units = jnp.concatenate([got[:, :1] + carry, got[:, 1 : lay.units]], axis=1)
    units = units.reshape(MAT_ROWS // UNIT, SUB, LANES)
    w_qkv = units[: QKV_END // UNIT].reshape(D, 3 * HD)
    w_up = units[OUT_END // UNIT : UP_END // UNIT].reshape(D, FF // HEADS)
    w_down = units[UP_END // UNIT :].reshape(FF // HEADS, D)
    out_rows = units[QKV_END // UNIT : OUT_END // UNIT]
    w_out = exchange(lay, out_rows.reshape(HEADS, HD // HEADS, D))
    w_out = w_out.transpose(1, 0, 2).reshape(HD, D)
    extra = jnp.sum(got[:, lay.units + 1 : lay.units + 7].astype(f32), axis=0).reshape(6, D)
    b_qkv = extra[0, : 3 * HD]
    b_up = extra[0, 3 * HD : 3 * HD + FF // HEADS]
    return w_qkv, b_qkv, w_out, w_up, b_up, w_down, extra[1:]


def share_sum(lay, parts, rep_id):
    if lay.reps == 2:
        low, high = parts[:, : lay.share], parts[:, lay.share :]
        theirs = lax.ppermute(jnp.where(rep_id == 0, high, low), "rep", lay.rep_xor(1))
        mine = jnp.where(rep_id == 0, low, high)
        return (mine.astype(f32) + theirs.astype(f32)).astype(bf16)
    by_rep = parts.reshape(parts.shape[0], lay.reps, lay.share, D)
    total = lax.dynamic_index_in_dim(by_rep, rep_id, axis=1, keepdims=False).astype(f32)
    for k in range(1, lay.reps):
        theirs = lax.dynamic_index_in_dim(by_rep, rep_id ^ k, axis=1, keepdims=False)
        total = total + lax.ppermute(theirs, "rep", lay.rep_xor(k)).astype(f32)
    return total.astype(bf16)


def windows(lay, units, first, last):
    body = units[: (last - first) * lay.units].reshape(last - first, lay.units, D)
    after = units[lay.units :: lay.units][: last - first, None]
    short = last - first - after.shape[0]
    after = jnp.pad(after, ((0, short), (0, 0), (0, 0)))
    room = jnp.zeros((last - first, lay.slots - lay.units - 1, D), bf16)
    return jnp.concatenate([body, after, room], axis=1)


def own_share(lay, late, early, mixed_row, full, shard_id, rep_id):
    total = jnp.concatenate([late, early], axis=0)
    tail = jnp.concatenate([mixed_row[None], full], axis=0)
    for k in [2**i for i in range((lay.reps - 1).bit_length())]:
        came = lax.ppermute(tail.astype(bf16), "rep", lay.rep_xor(k))
        tail = tail + came.astype(f32)
    tail = jnp.pad(tail, ((lay.units + 1, lay.slots - lay.units - 7), (0, 0))).astype(bf16)
    tail = lax.dynamic_slice_in_dim(tail, rep_id * lay.share, lay.share, axis=0)
    total = total + tail[None]
    if lay.packs > 1:
        pack_id = shard_id // lay.ways
        by_pack = total.reshape(lay.packs, lay.ways, lay.share, D)
        total = lax.dynamic_index_in_dim(by_pack, pack_id, keepdims=False).astype(f32)
        for k in range(1, lay.packs):
            theirs = lax.dynamic_index_in_dim(by_pack, pack_id ^ k, keepdims=False)
            total = total + lax.ppermute(theirs, "shard", lay.xor(lay.ways * k)).astype(f32)
        total = total.astype(bf16)
    return total


def all_shares(lay, got, rep_id):
    got = [got] + [lax.ppermute(got, "rep", lay.rep_xor(k)) for k in range(1, lay.reps)]
    if lay.reps == 2:
        got = [jnp.where(rep_id == r, got[0], got[1]) for r in range(2)]
        return jnp.concatenate(got, axis=1)
    got = jnp.take(jnp.stack(got), jnp.arange(lay.reps, dtype=jnp.int32) ^ rep_id, axis=0)
    return jnp.moveaxis(got, 0, 1).reshape(got.shape[1], -1, got.shape[-1])


def owner_part(lay, got, shard_id):
    body = got[:, : lay.units + 1].reshape(lay.ways, -1, LANES)
    extra = got[:, lay.units + 1 : lay.units + 7].astype(f32)
    qkv_vec = extra[:, 0, : 3 * HD].reshape(HEADS, 3, HD).transpose(1, 0, 2).reshape(3 * D)
    up_vec = extra[:, 0, 3 * HD : 3 * HD + FF // HEADS].T.reshape(FF)
    norm_vec = jnp.sum(extra[:, 1:5], axis=0).reshape(4 * D)
    out_vec = extra[0, 5]
    small = jnp.concatenate([qkv_vec, out_vec, up_vec, out_vec, norm_vec])
    table = jnp.asarray(lay.tables)[shard_id]
    size = (MAT_ROWS + VEC_ROWS) * D // lay.n
    flat = unpack(body, shard_id * lay.units, PAD + table[0], PAD + table[1], table[3])
    flat = flat.reshape(-1)[:size]
    run = 5 * D
    start = jnp.clip(table[3], 0, size - run)
    ids = start + lax.iota(jnp.int32, run)
    from_small = jnp.clip(start - table[5], -run, VEC_ROWS * D) + run
    vec = lax.dynamic_slice(jnp.pad(small, (run, run)), (from_small,), (run,))
    old = lax.dynamic_slice(flat, (start,), (run,))
    new = jnp.where((ids >= table[3]) & (ids < table[4]), vec, old)
    return lax.dynamic_update_slice(flat, new, (start,))


def per_device(lay, tokens, cotangent, segment, params, first_moment, second_moment):
    shard_id = lax.axis_index("shard")
    rep_id = lax.axis_index("rep")
    me = shard_id % lay.ways
    length = tokens.shape[0]
    blocks = lay.ways

    own_grad = jnp.where((segment >= 0)[:, None], cotangent, jnp.zeros_like(cotangent))
    block = jnp.concatenate([tokens, own_grad], axis=1)
    start = gather_start(lay, block)
    cuts = cut_windows(lay, params, shard_id)
    cuts, start = lax.optimization_barrier((cuts, start))
    chain, across = gather_line(lay, [block, start[0]], [start[1]])
    offer = offer_params(lay, cuts, params.shape[0], segment, shard_id, rep_id)
    offer, chain, across = lax.optimization_barrier((offer, chain, across))
    got = exchange(lay, offer)
    while len(chain) < lay.line:
        chain, across = gather_line(lay, chain, across)
    got, chain[-1] = lax.optimization_barrier((got, chain[-1]))
    seg_all = got[:, lay.share * SUB].astype(f32)
    w_qkv, b_qkv, w_out, w_up, b_up, w_down, full = take_params(
        lay, got[:, : lay.share * SUB], shard_id, rep_id
    )
    rows = gather_end(lay, chain, across)
    b_sum = full[0]
    spot = jnp.arange(blocks, dtype=jnp.int32)
    d_core, d_line, d_row = spot // (2 * lay.line), spot // 2 % lay.line, spot % 2
    source = (
        (me // 4 - d_line) % lay.line * 4 + ((me // 2 % 2) ^ d_row) * 2 + ((me % 2) ^ d_core)
    )
    seg = jnp.take(seg_all, source, axis=0)

    bias = jnp.pad(jnp.stack([jnp.pad(b_qkv, (0, HD)), b_up]), ((0, 6), (0, 0)))
    vec = jnp.pad(full, ((0, 8 - full.shape[0]), (0, 0)))
    *sums, grad_qkv, units_feed, grad_w_out, bias_sums, vec_sums = layer(
        rows,
        seg,
        turn_table(),
        jnp.pad(w_qkv, ((0, 0), (0, HD))),
        w_up,
        w_down,
        jnp.pad(w_out, ((0, LANES - HD), (0, 0))),
        bias,
        vec,
    )
    own = tokens.astype(f32)
    own_center = own - jnp.mean(own, axis=-1, keepdims=True)
    own_inverse = lax.rsqrt(jnp.mean(own_center * own_center, axis=-1, keepdims=True) + norm_eps)
    own_hat = own_center * own_inverse
    grad_w_qkv = grad_qkv[:, : 3 * HD]
    first = QKV_END // UNIT // lay.units - 1
    cut = -(-OUT_END // UNIT // lay.units)
    units_qkv = grad_w_qkv.reshape(QKV_END // UNIT, D)
    early = jnp.concatenate(
        [
            windows(lay, units_qkv[: first * lay.units + 1], 0, first),
            windows(lay, units_feed[cut * lay.units - OUT_END // UNIT :], cut, lay.n),
        ],
        axis=0,
    )
    early = share_sum(lay, early, rep_id)
    back = grad_w_out[:HD].reshape(HD // HEADS, HEADS, D).transpose(1, 0, 2)
    back = exchange(lay, back).reshape(HD, D)
    units = jnp.concatenate(
        [units_qkv[first * lay.units :], back, units_feed[: (cut + 1) * lay.units]], axis=0
    )
    late = windows(lay, units[: (cut - first) * lay.units + 1], first, cut)
    late = share_sum(lay, late, rep_id)
    late = jnp.concatenate([early[:first], late], axis=0)
    early = early[first:]
    used = 3 * HD + FF // HEADS
    mixed_row = jnp.concatenate(
        [bias_sums[0, : 3 * HD], bias_sums[1], jnp.zeros((D - used,), f32)]
    )
    vectors = vec_sums[:5]
    share = own_share(lay, late, early, mixed_row, vectors, shard_id, rep_id)

    kept, sent = scatter_planes(lay, sums, length)
    top = lay.line - 1
    share, sent[top] = lax.optimization_barrier((share, sent[top]))
    got = exchange(lay, share)
    total = scatter_step(lay, None, kept, sent, top)
    total = scatter_step(lay, total, kept, sent, top - 1)
    got, total = lax.optimization_barrier((got, total))
    got = all_shares(lay, got, rep_id)
    for d in range(top - 2, 0, -1):
        total = scatter_step(lay, total, kept, sent, d)
    got, total = lax.optimization_barrier((got, total))
    grad_total = owner_part(lay, got, shard_id)
    sums = scatter_step(lay, total, kept, sent, 0)
    out_sum, g_sum = sums[:, :D], sums[:, D:]
    out_rows = (tokens.astype(f32) + out_sum + b_sum).astype(bf16)
    grad_rows = (
        own_grad.astype(f32)
        + own_inverse
        * (
            g_sum
            - jnp.mean(g_sum, axis=-1, keepdims=True)
            - own_hat * jnp.mean(g_sum * own_hat, axis=-1, keepdims=True)
        )
    ).astype(bf16)

    new_weights, first_new, second_new = adam_update(
        params, first_moment, second_moment, grad_total
    )
    return (out_rows, grad_rows, grad_total, new_weights, first_new, second_new)


def solution(mesh):
    lay = Layout(mesh)
    in_specs = (
        P(("rep", "shard"), None),
        P(("rep", "shard"), None),
        P(("rep", "shard")),
        P("shard"),
        P("shard"),
        P("shard"),
    )
    out_specs = (
        P(("rep", "shard"), None),
        P(("rep", "shard"), None),
        P("shard"),
        P("shard"),
        P("shard"),
        P("shard"),
    )

    def body(*args):
        return per_device(lay, *args)

    return jax.shard_map(body, mesh=mesh, in_specs=in_specs, out_specs=out_specs, check_vma=False)
```
